32 devices in a mesh: tm: 4 (over y, x), rows: 2 (over core), cols: 4 (over z).
Axes of the slice: x: 2, y: 2, z: 4, core: 2. Of those that a mesh axis runs over, the one named last changes fastest.
Arguments:
- inputs: bfloat16 [4, 34, 32, 128], P('tm', 'rows', 'cols'), may hold values from -6 to 6
- cotangent: bfloat16 [4, 34, 32, 128], P('tm', 'rows', 'cols'), may hold values from -6 to 6
- weight_one: bfloat16 [27, 128, 128], replicated, may hold values from -0.109375 to 0.109375
- weight_two: bfloat16 [27, 128, 128], replicated, may hold values from -0.109375 to 0.109375
Outputs:
- grad_inputs: float32 [4, 34, 32, 128], P('tm', 'rows', 'cols')
- grad_one: float32 [27, 128, 128], P(None, ('tm', 'rows'), 'cols')
- grad_two: float32 [27, 128, 128], P(None, ('tm', 'rows'), 'cols')
The draws below stay inside these ranges and needn't reach their ends.
All inputs are finite; a program needn't handle non-finite values.
Results may differ from the reference program's by a relative error of at most 0.0029.
Values may be sent and summed in bfloat16 or wider, within the bound.
A program may use at most 64 MiB of HBM per device.

```python
import jax
import jax.numpy as jnp

C = 128
FRAMES = 4
HEIGHT = 34
WIDTH = 32


def strengthened(values, key, source, target, shards_of, factor):
    def block_of(dim):
        return (jnp.arange(values.shape[dim]) // (values.shape[dim] // shards_of)).reshape((-1,) + (1,) * (values.ndim - 1 - dim))

    one_side = jax.random.permutation(key, shards_of)[block_of(target)]
    other_side = (block_of(target) + shards_of // 2) % shards_of
    return jnp.where((block_of(source) == one_side) | (block_of(source) == other_side), factor * values, values)


def shard_levels(stream_key, extent, cuts, least, top_value):
    factor_of, own = 1.0, jax.random.fold_in(stream_key, 6)
    for position, parts in cuts:
        draws = jnp.exp(jax.random.uniform(jax.random.fold_in(own, position), (parts,), jnp.float32, least / len(cuts), top_value / len(cuts)))
        factor_of = factor_of * jnp.repeat(draws, extent[position] // parts).reshape([-1 if axis == position else 1 for axis in range(len(extent))])
    return factor_of


def scatter_about(key, extent, deviation, limit, split=(), held_as=jnp.bfloat16):
    level = shard_levels(key, extent, split, -0.22, 0.18) if split else 1.0
    array = jax.random.normal(key, extent, jnp.float32) * deviation * level
    return jnp.minimum(jnp.maximum(array, -limit), limit).astype(held_as)


def bell_draw_with(stream_key, extent, deviation, reach, shards, heavy, kind=jnp.bfloat16):
    drawn = deviation * jax.random.normal(stream_key, extent, jnp.float32)
    if shards:
        drawn = drawn * shard_levels(stream_key, extent, shards, -0.22, 0.18)
    return jnp.clip(strengthened(drawn, jax.random.fold_in(stream_key, 3), *heavy), -reach, reach).astype(kind)


def setup_inputs(seed: int = 0) -> dict:
    keys = jax.random.split(jax.random.key(seed), 5)
    inputs = bell_draw_with(keys[0], (FRAMES, HEIGHT, WIDTH, C), 1.0, 6.0, ((0, 4), (1, 2), (2, 4)), (1, 3, 2, 2.0))
    cotangent = bell_draw_with(keys[1], (FRAMES, HEIGHT, WIDTH, C), 1.0, 6.0, ((0, 4), (1, 2), (2, 4)), (2, 3, 4, 2.0))
    weight_one = scatter_about(keys[2], (27, C, C), (27 * C) ** -0.5, 0.109375)
    weight_two = scatter_about(keys[3], (27, C, C), (27 * C) ** -0.5, 0.109375)
    return dict(inputs=inputs, cotangent=cotangent, weight_one=weight_one, weight_two=weight_two)


def past_pad(volume):
    return jnp.pad(volume, ((2, 0), (1, 1), (1, 1), (0, 0)))

def future_pad(volume):
    return jnp.pad(volume, ((0, 2), (1, 1), (1, 1), (0, 0)))

def convolve(padded, weight, adjoint):
    total = jnp.zeros((FRAMES * HEIGHT * WIDTH, C), jnp.float32)
    for t_off in range(3):
        for h_off in range(3):
            for w_off in range(3):
                tap_index = t_off * 9 + h_off * 3 + w_off
                if adjoint:
                    window = padded[2 - t_off:2 - t_off + FRAMES, 2 - h_off:2 - h_off + HEIGHT, 2 - w_off:2 - w_off + WIDTH]
                    matrix = weight[tap_index].T
                else:
                    window = padded[t_off:t_off + FRAMES, h_off:h_off + HEIGHT, w_off:w_off + WIDTH]
                    matrix = weight[tap_index]
                total = total + jnp.dot(window.reshape(-1, C), matrix, preferred_element_type=jnp.float32)
    return total

def kernel_grad(padded, right_side):
    pieces = []
    for t_off in range(3):
        for h_off in range(3):
            for w_off in range(3):
                window = padded[t_off:t_off + FRAMES, h_off:h_off + HEIGHT, w_off:w_off + WIDTH].reshape(-1, C)
                pieces.append(jnp.dot(window.T, right_side, preferred_element_type=jnp.float32))
    return jnp.stack(pieces)

def reference(inputs, cotangent, weight_one, weight_two):
    hidden = convolve(past_pad(inputs), weight_one, False)
    squash = jax.nn.sigmoid(hidden)
    activation = (hidden * squash).astype(jnp.bfloat16)
    flat_grad = cotangent.reshape(-1, C)
    grad_act = convolve(future_pad(cotangent), weight_two, True)
    grad_hidden = (grad_act * squash * (1.0 + hidden * (1.0 - squash))).astype(jnp.bfloat16)
    grad_two = kernel_grad(past_pad(activation.reshape(FRAMES, HEIGHT, WIDTH, C)), flat_grad)
    grad_one = kernel_grad(past_pad(inputs), grad_hidden)
    back = convolve(future_pad(grad_hidden.reshape(FRAMES, HEIGHT, WIDTH, C)), weight_one, True)
    grad_inputs = cotangent.astype(jnp.float32) + back.reshape(FRAMES, HEIGHT, WIDTH, C)
    return (grad_inputs, grad_one, grad_two)
```

```python
import functools

import jax
import jax.numpy as jnp
from jax import lax
from jax.experimental import pallas as pl
from jax.experimental.pallas import tpu as pltpu
from jax.sharding import PartitionSpec as P

MESH = pl.DeviceIdType.MESH
NT = (((1,), (1,)), ((), ()))
C = 128


def kernel(
    dims,
    x_ref,
    c_ref,
    w1_ref,
    w2_ref,
    back_ref,
    acc,
    gat,
    flat,
    hf,
    hal,
    sx,
    sc,
    x9,
    c9,
    r1,
    r2,
    conv,
    gate,
    at,
    xt,
    ghb,
    ghf,
    own3,
    gf,
    sh,
    imc,
    part,
    pstage,
    pland,
    pp,
    stage,
    landed,
    rim,
    edge,
    rim_in,
    edge_in,
    corner_in,
    grim,
    gedge,
    grim_in,
    gedge_in,
    gcorner_in,
    own_sem,
    w1_sem,
    w2_sem,
    blk_send,
    blk_recv,
    hal_send,
    hal_recv,
    near_sem,
    gnear_sem,
    pair_send,
    pair_recv,
    rs_send,
    rs_recv,
):
    tmn, rn, zn, rows, cols, chunk, chunk_pad, slots = dims
    cells = rows * cols
    lift = (rows + 2) * cols
    left = 2 * cols
    right = left + -(-(rows + 2) // 8) * 8
    mp, kp = x9.shape[1], c9.shape[1]
    taps = 27 * chunk_pad
    cwp = rn * chunk_pad
    ochunk = C // zn
    bf, f32 = jnp.bfloat16, jnp.float32
    tm, row, col = lax.axis_index("tm"), lax.axis_index("rows"), lax.axis_index("cols")
    vert = (row > 0, row < rn - 1)
    side = (col > 0, col < zn - 1)
    step = (-1, 1)

    barrier = pltpu.get_barrier_semaphore()

    def greet(place):
        pl.semaphore_signal(barrier, inc=1, device_id=place, device_id_type=MESH)

    for d in range(1, tmn):
        greet((lax.rem(tm + d, tmn), row, col))
    for d in range(1, rn):
        greet((tm, lax.rem(row + d, rn), col))
    for d in range(1, zn):
        greet((tm, row, lax.rem(col + d, zn)))
    for v in range(2):
        for h in range(2):

            @pl.when(jnp.logical_and(vert[v], side[h]))
            def _():
                greet((tm, row + step[v], col + step[h]))

    blocks = (x_ref, c_ref)

    def keep(which):
        return pltpu.make_async_copy(blocks[which], gat.at[which, tm], own_sem.at[which])

    def load_one(k):
        a, q = k // 9, k % 9
        return pltpu.make_async_copy(
            w1_ref.at[pl.ds(C * k, C), :], r1.at[pl.ds(C * q, C), pl.ds(C * a, C)], w1_sem.at[k]
        )

    def load_two(k):
        a, q = k // 9, k % 9
        return pltpu.make_async_copy(
            w2_ref.at[pl.ds(C * k, C), :], r2.at[pl.ds(C * a, C), pl.ds(C * q, C)], w2_sem.at[k]
        )

    keep(0).start()
    keep(1).start()
    for k in range(27):
        load_one(k).start()
    for k in range(27):
        load_two(k).start()

    hf[...] = jnp.zeros(hf.shape, f32)

    for which in range(2):
        keep(which).wait()
        flat[which] = gat[which, tm].astype(f32)
        for h in range(2):
            edge[h, which * rows : (which + 1) * rows, :] = flat[
                which, pl.ds(h * (cols - 1), rows, stride=cols), :
            ].astype(bf)
        for v in range(2):
            rim[v, which * cols : (which + 1) * cols, :] = flat[
                which, v * (cells - cols) : v * (cells - cols) + cols, :
            ].astype(bf)

    def remote(src, dst, send, recv, place):
        return pltpu.make_async_remote_copy(
            src_ref=src, dst_ref=dst, send_sem=send, recv_sem=recv, device_id=place, device_id_type=MESH
        )

    def near(out_rim, out_edge, in_rim, in_edge, in_corner, sems):
        found = []
        for v in range(2):
            found.append((
                vert[v],
                lambda v=v: remote(
                    out_rim.at[v], in_rim.at[1 - v], sems.at[0, v], sems.at[1, 1 - v], (tm, row + step[v], col)
                ),
                in_rim.at[v],
                sems.at[1, v],
            ))
        for h in range(2):
            found.append((
                side[h],
                lambda h=h: remote(
                    out_edge.at[h], in_edge.at[1 - h], sems.at[0, 2 + h], sems.at[1, 3 - h], (tm, row, col + step[h])
                ),
                in_edge.at[h],
                sems.at[1, 2 + h],
            ))
        for v in range(2):
            for h in range(2):
                found.append((
                    jnp.logical_and(vert[v], side[h]),
                    lambda v=v, h=h: remote(
                        out_edge.at[h],
                        in_corner.at[1 - v, 1 - h],
                        sems.at[0, 4 + 2 * v + h],
                        sems.at[1, 4 + 2 * (1 - v) + 1 - h],
                        (tm, row + step[v], col + step[h]),
                    ),
                    in_corner.at[v, h],
                    sems.at[1, 4 + 2 * v + h],
                ))
        return found

    def start_all(found):
        for cond, copy, _, _ in found:

            @pl.when(cond)
            def _():
                copy().start()

    def drain_all(found):
        for cond, copy, _, _ in found:

            @pl.when(cond)
            def _():
                copy().wait_send()

    def arrived(dst, sem):
        remote(dst, dst, sem, sem, (tm, row, col)).wait_recv()

    def await_all(found):
        for cond, _, dst, sem in found:

            @pl.when(cond)
            def _():
                arrived(dst, sem)

    def assemble(dst, count, in_rim, in_edge, in_corner):
        for v in range(2):

            @pl.when(vert[v])
            def _():
                got = in_rim[v].astype(f32)
                for q in range(count):
                    dst[q, v * cols : (v + 1) * cols, :] = got[q * cols : (q + 1) * cols]

        for h, base in enumerate((left, right)):

            @pl.when(side[h])
            def _():
                got = in_edge[h].astype(f32)
                for q in range(count):
                    dst[q, base + 1 : base + 1 + rows, :] = got[q * rows : (q + 1) * rows]

            for v in range(2):

                @pl.when(jnp.logical_and(vert[v], side[h]))
                def _():
                    got = in_corner[v, h].astype(f32)
                    put = base + v * (rows + 1)
                    for q in range(count):
                        take = q * rows + (1 - v) * (rows - 1)
                        dst[q, put : put + 1, :] = got[take : take + 1]

    def spread(dst, v, h):
        top, bottom = h[:cols], h[cols : 2 * cols]
        dst[1, :cols, :] = top
        dst[1, cols : cols + cells, :] = v
        dst[1, cols + cells : lift, :] = bottom
        dst[0, 1 : cols + 1, :] = top
        dst[0, cols + 1 : cols + cells + 1, :] = v
        dst[0, cols + cells + 1 : lift, :] = bottom[: cols - 1]
        dst[0, pl.ds(0, rows + 2, stride=cols), :] = h[left : left + rows + 2]
        dst[2, : cols - 1, :] = top[1:]
        dst[2, cols - 1 : cols + cells - 1, :] = v
        dst[2, cols + cells - 1 : lift - 1, :] = bottom
        dst[2, pl.ds(cols - 1, rows + 2, stride=cols), :] = h[right : right + rows + 2]

    corners = (vert[0].astype(jnp.int32) + vert[1].astype(jnp.int32)) * (
        side[0].astype(jnp.int32) + side[1].astype(jnp.int32)
    )
    pl.semaphore_wait(barrier, tmn + rn + zn - 3 + corners)

    rims = near(rim, edge, rim_in, edge_in, corner_in, near_sem)
    start_all(rims)

    def send_block(which, d):
        return remote(
            gat.at[which, tm],
            gat.at[which, tm],
            blk_send.at[which, d],
            blk_recv.at[which, tm],
            (lax.rem(tm + d, tmn), row, col),
        )

    def send_halo(d):
        return remote(
            hal.at[tm], hal.at[tm], hal_send.at[d], hal_recv.at[tm], (lax.rem(tm + d, tmn), row, col)
        )

    for d in range(1, tmn):
        send_block(0, d).start()

    for tail in (sx, sc):
        for s in range(tmn):
            for e in range(3):
                tail[s, e, lift:, :] = jnp.zeros((tail.shape[2] - lift, C), f32)
    for s in range(tmn):
        c9[s, mp:, :] = jnp.zeros((kp - mp, 9 * C), bf)
        xt[s] = jnp.zeros(xt.shape[1:], bf)
    at[...] = jnp.zeros(at.shape, bf)
    for s in range(tmn + 2):
        ghb[s] = jnp.zeros((kp, C), bf)
    ghf[tmn * cells :, :] = jnp.zeros((2 * cells, C), f32)
    gf[...] = jnp.zeros(gf.shape, f32)
    for j in range(3):
        for e in range(3):
            sh[j, e, lift:, :] = jnp.zeros((sh.shape[2] - lift, C), f32)
    pp[taps:, :] = jnp.zeros((pp.shape[0] - taps, C), f32)
    picked = jnp.concatenate(
        [
            jnp.where(
                (lax.broadcasted_iota(jnp.int32, (chunk_pad, C), 1)
                 == (tm * rn + r) * chunk + lax.broadcasted_iota(jnp.int32, (chunk_pad, C), 0))
                & (lax.broadcasted_iota(jnp.int32, (chunk_pad, C), 0) < chunk),
                1.0, 0.0,
            )
            for r in range(rn)
        ],
        axis=0,
    ).astype(bf)

    def tall(src):
        return lax.dot_general(picked, src, NT, preferred_element_type=f32).astype(bf)

    await_all(rims)
    assemble(hf, 2, rim_in, edge_in, corner_in)
    for which in range(2):
        hal[tm, which] = hf[which].astype(bf)
    for d in range(1, tmn):
        send_halo(d).start()
    for d in range(1, tmn):
        send_block(1, d).start()

    for m in range(tmn):

        @pl.when(tm != m)
        def _():
            arrived(gat.at[0, m], blk_recv.at[0, m])
            arrived(hal.at[m], hal_recv.at[m])

        spread(sx.at[m], gat[0, m].astype(f32), hal[m, 0].astype(f32))
        for q in range(9):
            b, e = q // 3, q % 3
            x9[m, :, C * q : C * (q + 1)] = sx[m, e, cols * b : cols * b + mp, :].astype(bf)

    for k in range(27):
        load_one(k).wait()

    conv[...] = jnp.dot(
        x9[...].reshape(tmn * mp, 9 * C), r1[...], preferred_element_type=f32
    )
    for t in range(tmn):
        hidden = conv[t * mp : t * mp + cells, 2 * C :]
        for a in range(2):
            s = t - 2 + a
            if s >= 0:
                hidden = hidden + conv[s * mp : s * mp + cells, C * a : C * (a + 1)]
        squash = jax.nn.sigmoid(hidden)
        gate[t] = squash * (1.0 + hidden * (1.0 - squash))
        at[(t + 2) * cwp : (t + 3) * cwp, :cells] = tall((hidden * squash).astype(bf))
    for s in range(tmn):
        for q in range(9):
            xt[s, cwp * q : cwp * (q + 1), :mp] = tall(x9[s, :, C * q : C * (q + 1)])

    for m in range(tmn):

        @pl.when(tm != m)
        def _():
            arrived(gat.at[1, m], blk_recv.at[1, m])

        spread(sc.at[m], gat[1, m].astype(f32), hal[m, 1].astype(f32))
        for q in range(9):
            b, e = q // 3, q % 3
            c9[m, :mp, C * q : C * (q + 1)] = sc[m, 2 - e, cols * (2 - b) : cols * (2 - b) + mp, :].astype(bf)

    def send_pair(tensor, r):
        return remote(
            pstage.at[tensor, r],
            pland.at[tensor, row],
            pair_send.at[tensor, r],
            pair_recv.at[tensor, row],
            (tm, r, col),
        )

    def send_pairs(tensor):
        for r in range(rn):

            @pl.when(row != r)
            def _():
                send_pair(tensor, r).start()

    def send_piece(tensor, z):
        return remote(
            stage.at[tensor, z], landed.at[tensor, col], rs_send.at[tensor, z], rs_recv.at[tensor, col], (tm, row, z)
        )

    group = slots * chunk_pad // zn

    def scatter(tensor):
        pp[:taps, :] = part[tensor, row]
        for r in range(rn):

            @pl.when(row != r)
            def _():
                arrived(pland.at[tensor, r], pair_recv.at[tensor, r])
                pp[:taps, :] += pland[tensor, r].astype(f32)

        for z in range(zn):
            stage[tensor, z] = jnp.concatenate(
                [pp[group * q : group * (q + 1), ochunk * z : ochunk * (z + 1)] for q in range(zn)],
                axis=1,
            ).astype(bf)
        for z in range(zn):

            @pl.when(col != z)
            def _():
                send_piece(tensor, z).start()

    total = None
    for s in range(tmn):
        got = jnp.dot(at[s * cwp : (s + 3) * cwp, :], c9[s], preferred_element_type=f32)
        total = got if total is None else total + got
    for a in range(3):
        for r in range(rn):
            for q in range(9):
                k = 9 * a + q
                piece = total[a * cwp + r * chunk_pad : a * cwp + (r + 1) * chunk_pad, C * q : C * (q + 1)]
                part[1, r, k * chunk_pad : (k + 1) * chunk_pad, :] = piece
                pstage[1, r, k * chunk_pad : (k + 1) * chunk_pad, :] = piece.astype(bf)
    send_pairs(1)

    for k in range(27):
        load_two(k).wait()
    conv[...] = lax.dot_general(
        c9[:, :mp, :].reshape(tmn * mp, 9 * C), r2[...], NT, preferred_element_type=f32
    )
    for t in range(tmn):
        grad = conv[t * mp : t * mp + cells, 2 * C :]
        for a in range(2):
            s = t + 2 - a
            if s < tmn:
                grad = grad + conv[s * mp : s * mp + cells, C * a : C * (a + 1)]
        grad = (grad * gate[t]).astype(bf)
        ghb[t, :cells, :] = grad
        ghf[t * cells : (t + 1) * cells, :] = grad.astype(f32)

    own3[...] = ghf[pl.ds(pl.multiple_of(tm * cells, 8), 3 * cells), :]
    for h in range(2):
        gedge[h] = own3[pl.ds(h * (cols - 1), 3 * rows, stride=cols), :].astype(bf)
    for v in range(2):
        grim[v] = jnp.concatenate(
            [
                own3[j * cells + v * (cells - cols) : j * cells + v * (cells - cols) + cols, :]
                for j in range(3)
            ],
            axis=0,
        ).astype(bf)
    grims = near(grim, gedge, grim_in, gedge_in, gcorner_in, gnear_sem)
    start_all(grims)

    scatter(1)

    total = None
    for s in range(tmn):
        right_side = jnp.concatenate([ghb[s + 2], ghb[s + 1], ghb[s]], axis=1)
        got = jnp.dot(xt[s], right_side, preferred_element_type=f32)
        total = got if total is None else total + got
    for q in range(9):
        for r in range(rn):
            for a in range(3):
                k = 9 * a + q
                piece = total[q * cwp + r * chunk_pad : q * cwp + (r + 1) * chunk_pad, C * a : C * (a + 1)]
                part[0, r, k * chunk_pad : (k + 1) * chunk_pad, :] = piece
                pstage[0, r, k * chunk_pad : (k + 1) * chunk_pad, :] = piece.astype(bf)
    send_pairs(0)

    await_all(grims)
    assemble(gf, 3, grim_in, gedge_in, gcorner_in)
    for j in range(3):
        spread(sh.at[j], own3[j * cells : (j + 1) * cells, :], gf[j])
        for q in range(9):
            b, e = q // 3, q % 3
            lane = C * (3 * q + 2 - j)
            imc[:, lane : lane + C] = sh[j, 2 - e, cols * (2 - b) : cols * (2 - b) + mp, :].astype(bf)

    scatter(0)

    total = None
    for q in range(9):
        got = lax.dot_general(
            imc[:, 3 * C * q : 3 * C * (q + 1)], r1[C * q : C * (q + 1), :], NT, preferred_element_type=f32
        )
        total = got if total is None else total + got
    back_ref[...] = flat[1] + total[:cells]

    for tensor in (1, 0):
        acc[tensor] = stage[tensor, col].astype(f32)
        for z in range(zn):

            @pl.when(col != z)
            def _():
                arrived(landed.at[tensor, z], rs_recv.at[tensor, z])
                acc[tensor] += landed[tensor, z].astype(f32)

    for which in range(2):
        for d in range(1, tmn):
            send_block(which, d).wait_send()
        for r in range(rn):

            @pl.when(row != r)
            def _():
                send_pair(which, r).wait_send()

        for z in range(zn):

            @pl.when(col != z)
            def _():
                send_piece(which, z).wait_send()

    for d in range(1, tmn):
        send_halo(d).wait_send()
    drain_all(rims)
    drain_all(grims)


def finish(zn, chunk, chunk_pad, slots, back_ref, acc_ref, out_ref, one_ref, two_ref):
    ochunk = C // zn
    out_ref[...] = back_ref[...]
    for tensor, out in enumerate((one_ref, two_ref)):
        got = acc_ref[tensor]
        whole = jnp.concatenate(
            [got[:, ochunk * q : ochunk * (q + 1)] for q in range(zn)], axis=0
        ).reshape(slots, chunk_pad, ochunk)
        out[...] = whole[:27, :chunk, :]


def body(sizes, inputs, cotangent, weight_one, weight_two):
    tmn, rn, zn = sizes
    _, rows, cols, channels = inputs.shape
    cells = rows * cols
    chunk = channels // (tmn * rn)
    chunk_pad = max(16, chunk)
    slots = 28
    lift = (rows + 2) * cols
    mp = -(-cells // 16) * 16
    kp = -(-cells // 128) * 128
    hs = -(-(2 * cols + 2 * (-(-(rows + 2) // 8) * 8)) // 16) * 16
    cwp = rn * chunk_pad
    taps = 27 * chunk_pad
    dims = (tmn, rn, zn, rows, cols, chunk, chunk_pad, slots)
    vmem = pl.BlockSpec(memory_space=pltpu.VMEM)
    bf, f32 = jnp.bfloat16, jnp.float32
    group = slots * chunk_pad // zn
    dma = pltpu.SemaphoreType.DMA
    lifted = lift + mp - cells
    back, acc = pl.pallas_call(
        functools.partial(kernel, dims),
        out_shape=(
            jax.ShapeDtypeStruct((cells, channels), f32),
            jax.ShapeDtypeStruct((2, group, channels), f32),
        ),
        in_specs=[pl.BlockSpec(memory_space=pl.ANY)] * 4,
        out_specs=(vmem,) * 2,
        scratch_shapes=[
            pltpu.VMEM((2, tmn, cells, channels), bf),
            pltpu.VMEM((2, cells, channels), f32),
            pltpu.VMEM((2, hs, channels), f32),
            pltpu.VMEM((tmn, 2, hs, channels), bf),
            pltpu.VMEM((tmn, 3, lifted, channels), f32),
            pltpu.VMEM((tmn, 3, lifted, channels), f32),
            pltpu.VMEM((tmn, mp, 9 * channels), bf),
            pltpu.VMEM((tmn, kp, 9 * channels), bf),
            pltpu.VMEM((9 * channels, 3 * channels), bf),
            pltpu.VMEM((3 * channels, 9 * channels), bf),
            pltpu.VMEM((tmn * mp, 3 * channels), f32),
            pltpu.VMEM((tmn, cells, channels), f32),
            pltpu.VMEM(((tmn + 2) * cwp, kp), bf),
            pltpu.VMEM((tmn, 9 * cwp, kp), bf),
            pltpu.VMEM((tmn + 2, kp, channels), bf),
            pltpu.VMEM(((tmn + 2) * cells, channels), f32),
            pltpu.VMEM((3 * cells, channels), f32),
            pltpu.VMEM((3, hs, channels), f32),
            pltpu.VMEM((3, 3, lifted, channels), f32),
            pltpu.VMEM((mp, 27 * channels), bf),
            pltpu.VMEM((2, rn, taps, channels), f32),
            pltpu.VMEM((2, rn, taps, channels), bf),
            pltpu.VMEM((2, rn, taps, channels), bf),
            pltpu.VMEM((slots * chunk_pad, channels), f32),
            pltpu.VMEM((2, zn, group, channels), bf),
            pltpu.VMEM((2, zn, group, channels), bf),
            pltpu.VMEM((2, 2 * cols, channels), bf),
            pltpu.VMEM((2, 2 * rows, channels), bf),
            pltpu.VMEM((2, 2 * cols, channels), bf),
            pltpu.VMEM((2, 2 * rows, channels), bf),
            pltpu.VMEM((2, 2, 2 * rows, channels), bf),
            pltpu.VMEM((2, 3 * cols, channels), bf),
            pltpu.VMEM((2, 3 * rows, channels), bf),
            pltpu.VMEM((2, 3 * cols, channels), bf),
            pltpu.VMEM((2, 3 * rows, channels), bf),
            pltpu.VMEM((2, 2, 3 * rows, channels), bf),
            dma((2,)),
            dma((27,)),
            dma((27,)),
            dma((2, tmn)),
            dma((2, tmn)),
            dma((tmn,)),
            dma((tmn,)),
            dma((2, 8)),
            dma((2, 8)),
            dma((2, rn)),
            dma((2, rn)),
            dma((2, zn)),
            dma((2, zn)),
        ],
        compiler_params=pltpu.CompilerParams(
            collective_id=0, has_side_effects=True, vmem_limit_bytes=60 * 1024 * 1024
        ),
    )(
        inputs.reshape(cells, channels),
        cotangent.reshape(cells, channels),
        weight_one.reshape(27 * channels, channels),
        weight_two.reshape(27 * channels, channels),
    )
    back, one, two = pl.pallas_call(
        functools.partial(finish, zn, chunk, chunk_pad, slots),
        out_shape=(
            jax.ShapeDtypeStruct((cells, channels), f32),
            jax.ShapeDtypeStruct((27, chunk, channels // zn), f32),
            jax.ShapeDtypeStruct((27, chunk, channels // zn), f32),
        ),
        in_specs=[vmem] * 2,
        out_specs=(vmem,) * 3,
    )(back, acc)
    return back.reshape(1, rows, cols, channels), one, two


def solution(mesh):
    sizes = (mesh.shape["tm"], mesh.shape["rows"], mesh.shape["cols"])
    placed = (P("tm", "rows", "cols", None), P("tm", "rows", "cols", None), P(), P())
    return jax.shard_map(
        functools.partial(body, sizes),
        mesh=mesh,
        in_specs=placed,
        out_specs=(
            P("tm", "rows", "cols", None),
            P(None, ("tm", "rows"), "cols"),
            P(None, ("tm", "rows"), "cols"),
        ),
        check_vma=False,
    )
```

```python
import functools

import jax
import jax.numpy as jnp
from jax import lax
from jax.experimental import pallas as pl
from jax.experimental.pallas import tpu as pltpu
from jax.sharding import PartitionSpec as P

MESH = pl.DeviceIdType.MESH
NT = (((1,), (1,)), ((), ()))
C = 128


def kernel(
    dims,
    x_ref,
    c_ref,
    w1_ref,
    w2_ref,
    back_ref,
    acc,
    gat,
    flat,
    sx,
    sc,
    x9,
    c9,
    r1,
    r2,
    conv,
    gate,
    at,
    xt,
    ghb,
    ghf,
    own3,
    gf,
    sh,
    imc,
    part,
    pstage,
    pland,
    pp,
    stage,
    landed,
    rim,
    edge,
    tip,
    rim_in,
    edge_in,
    tip_in,
    grim,
    gedge,
    grim_in,
    gedge_in,
    gcorner_in,
    own_sem,
    w1_sem,
    w2_sem,
    blk_send,
    blk_recv,
    near_send,
    near_recv,
    gnear_sem,
    pair_send,
    pair_recv,
    rs_send,
    rs_recv,
):
    tmn, rn, zn, rows, cols, chunk, chunk_pad, slots = dims
    cells = rows * cols
    lift = (rows + 2) * cols
    left = 2 * cols
    right = left + -(-(rows + 2) // 8) * 8
    mp, kp = x9.shape[1], c9.shape[1]
    taps = 27 * chunk_pad
    cwp = rn * chunk_pad
    ochunk = C // zn
    bf, f32 = jnp.bfloat16, jnp.float32
    tm, row, col = lax.axis_index("tm"), lax.axis_index("rows"), lax.axis_index("cols")
    vert = (row > 0, row < rn - 1)
    side = (col > 0, col < zn - 1)
    step = (-1, 1)

    def partner(d):
        if tmn == 4:
            flips = (tm, tm + 1 - 2 * lax.rem(tm, 2), tm + 2 - 4 * (tm // 2), 3 - tm)
            return flips[d]
        return lax.rem(tm + d, tmn)

    blocks = (x_ref, c_ref)

    def keep(which):
        return pltpu.make_async_copy(blocks[which], gat.at[which, tm], own_sem.at[which])

    keep(0).start()
    keep(1).start()
    barrier = pltpu.get_barrier_semaphore()

    def greet(place):
        pl.semaphore_signal(barrier, inc=1, device_id=place, device_id_type=MESH)

    for z in range(zn):

        @pl.when(jnp.logical_or(col - z > 1, z - col > 1))
        def _():
            greet((tm, row, z))

    for d in range(tmn - 1, 0, -1):
        greet((partner(d), row, col))
    for v in range(2):
        for h in range(2):

            @pl.when(jnp.logical_and(vert[v], side[h]))
            def _():
                for d in range(tmn - 1, -1, -1):
                    greet((partner(d), row + step[v], col + step[h]))

    for h in range(2):

        @pl.when(side[h])
        def _():
            for d in range(tmn - 1, -1, -1):
                greet((partner(d), row, col + step[h]))

    for v in range(2):

        @pl.when(vert[v])
        def _():
            for d in range(tmn - 1, -1, -1):
                greet((partner(d), row + step[v], col))

    for r in range(rn if rn > 2 else 0):

        @pl.when(jnp.logical_or(row - r > 1, r - row > 1))
        def _():
            greet((tm, r, col))

    def load_one(k):
        a, q = k // 9, k % 9
        return pltpu.make_async_copy(
            w1_ref.at[pl.ds(C * k, C), :], r1.at[pl.ds(C * q, C), pl.ds(C * a, C)], w1_sem.at[k]
        )

    def load_two(k):
        a, q = k // 9, k % 9
        return pltpu.make_async_copy(
            w2_ref.at[pl.ds(C * k, C), :], r2.at[pl.ds(C * a, C), pl.ds(C * q, C)], w2_sem.at[k]
        )

    for k in range(27):
        load_one(k).start()
    for k in range(27):
        load_two(k).start()

    for v in range(2):

        @pl.when(jnp.logical_not(vert[v]))
        def _():
            rim_in[:, :, v] = jnp.zeros((2, tmn, cols, C), bf)
            tip_in[:, :, v] = jnp.zeros((2, tmn, 2, 8, C), bf)

    for h in range(2):

        @pl.when(jnp.logical_not(side[h]))
        def _():
            edge_in[:, :, h] = jnp.zeros((2, tmn, rows, C), bf)
            tip_in[:, :, :, h] = jnp.zeros((2, tmn, 2, 8, C), bf)

    for which in range(2):
        keep(which).wait()
        flat[which] = gat[which, tm].astype(f32)
        for h in range(2):
            edge[which, h] = flat[which, pl.ds(h * (cols - 1), rows, stride=cols), :].astype(bf)
        for v in range(2):
            line = flat[which, v * (cells - cols) : v * (cells - cols) + cols, :]
            rim[which, v] = line.astype(bf)
            for h in range(2):
                tip[which, v, h] = jnp.broadcast_to(line[h * (cols - 1) : h * (cols - 1) + 1], (8, C)).astype(bf)

    def remote(src, dst, send, recv, place):
        return pltpu.make_async_remote_copy(
            src_ref=src, dst_ref=dst, send_sem=send, recv_sem=recv, device_id=place, device_id_type=MESH
        )

    def near(out_rim, out_edge, in_rim, in_edge, in_corner, sems):
        found = []
        for v in range(2):
            found.append((
                vert[v],
                lambda v=v: remote(
                    out_rim.at[v], in_rim.at[1 - v], sems.at[0, v], sems.at[1, 1 - v], (tm, row + step[v], col)
                ),
                in_rim.at[v],
                sems.at[1, v],
            ))
        for h in range(2):
            found.append((
                side[h],
                lambda h=h: remote(
                    out_edge.at[h], in_edge.at[1 - h], sems.at[0, 2 + h], sems.at[1, 3 - h], (tm, row, col + step[h])
                ),
                in_edge.at[h],
                sems.at[1, 2 + h],
            ))
        for v in range(2):
            for h in range(2):
                found.append((
                    jnp.logical_and(vert[v], side[h]),
                    lambda v=v, h=h: remote(
                        out_edge.at[h],
                        in_corner.at[1 - v, 1 - h],
                        sems.at[0, 4 + 2 * v + h],
                        sems.at[1, 4 + 2 * (1 - v) + 1 - h],
                        (tm, row + step[v], col + step[h]),
                    ),
                    in_corner.at[v, h],
                    sems.at[1, 4 + 2 * v + h],
                ))
        return found

    def start_all(found):
        for cond, copy, _, _ in found:

            @pl.when(cond)
            def _():
                copy().start()

    def drain_all(found):
        for cond, copy, _, _ in found:

            @pl.when(cond)
            def _():
                copy().wait_send()

    def arrived(dst, sem):
        remote(dst, dst, sem, sem, (tm, row, col)).wait_recv()

    def await_all(found):
        for cond, _, dst, sem in found:

            @pl.when(cond)
            def _():
                arrived(dst, sem)

    def assemble(dst, count, in_rim, in_edge, in_corner):
        for v in range(2):

            @pl.when(vert[v])
            def _():
                got = in_rim[v].astype(f32)
                for q in range(count):
                    dst[q, v * cols : (v + 1) * cols, :] = got[q * cols : (q + 1) * cols]

        for h, base in enumerate((left, right)):

            @pl.when(side[h])
            def _():
                got = in_edge[h].astype(f32)
                for q in range(count):
                    dst[q, base + 1 : base + 1 + rows, :] = got[q * rows : (q + 1) * rows]

            for v in range(2):

                @pl.when(jnp.logical_and(vert[v], side[h]))
                def _():
                    got = in_corner[v, h].astype(f32)
                    put = base + v * (rows + 1)
                    for q in range(count):
                        take = q * rows + (1 - v) * (rows - 1)
                        dst[q, put : put + 1, :] = got[take : take + 1]

    def spread(dst, v, top, bottom, sides, tips):
        dst[1, :cols, :] = top
        dst[1, cols : cols + cells, :] = v
        dst[1, cols + cells : lift, :] = bottom
        dst[0, 1 : cols + 1, :] = top
        dst[0, cols + 1 : cols + cells + 1, :] = v
        dst[0, cols + cells + 1 : lift, :] = bottom[: cols - 1]
        dst[0, :1, :] = tips[0][0]
        dst[0, pl.ds(cols, rows, stride=cols), :] = sides[0]
        dst[0, cols + cells : cols + cells + 1, :] = tips[1][0]
        dst[2, : cols - 1, :] = top[1:]
        dst[2, cols - 1 : cols + cells - 1, :] = v
        dst[2, cols + cells - 1 : lift - 1, :] = bottom
        dst[2, cols - 1 : cols, :] = tips[0][1]
        dst[2, pl.ds(2 * cols - 1, rows, stride=cols), :] = sides[1]
        dst[2, lift - 1 : lift, :] = tips[1][1]

    nv = vert[0].astype(jnp.int32) + vert[1].astype(jnp.int32)
    nh = side[0].astype(jnp.int32) + side[1].astype(jnp.int32)
    pl.semaphore_wait(barrier, tmn * (1 + nv) * (1 + nh) - 1 + zn - 1 - nh + rn - 1 - nv)

    def send_block(which, d):
        return remote(
            gat.at[which, tm],
            gat.at[which, tm],
            blk_send.at[which, d],
            blk_recv.at[which, tm],
            (partner(d), row, col),
        )

    def send_rim(which, v, d):
        return remote(
            rim.at[which, v],
            rim_in.at[which, tm, 1 - v],
            near_send.at[which, v, d],
            near_recv.at[which, 1 - v, tm],
            (partner(d), row + step[v], col),
        )

    def send_edge(which, h, d):
        return remote(
            edge.at[which, h],
            edge_in.at[which, tm, 1 - h],
            near_send.at[which, 2 + h, d],
            near_recv.at[which, 3 - h, tm],
            (partner(d), row, col + step[h]),
        )

    def send_tip(which, v, h, d):
        return remote(
            tip.at[which, v, h],
            tip_in.at[which, tm, 1 - v, 1 - h],
            near_send.at[which, 4 + 2 * v + h, d],
            near_recv.at[which, 4 + 2 * (1 - v) + 1 - h, tm],
            (partner(d), row + step[v], col + step[h]),
        )

    def each_near(which, act):
        for h in range(2):

            @pl.when(side[h])
            def _():
                for d in range(tmn - 1, -1, -1):
                    act(send_edge(which, h, d))

        for v in range(2):

            @pl.when(vert[v])
            def _():
                for d in range(tmn - 1, -1, -1):
                    act(send_rim(which, v, d))

        for v in range(2):
            for h in range(2):

                @pl.when(jnp.logical_and(vert[v], side[h]))
                def _():
                    for d in range(tmn - 1, -1, -1):
                        act(send_tip(which, v, h, d))

    for which in range(2):
        each_near(which, lambda copy: copy.start())
        for d in range(tmn - 1, 0, -1):
            send_block(which, d).start()

    def receive(which, ds, dst):
        for d in ds[ds[0] == 0 :]:
            arrived(gat.at[which, partner(d)], blk_recv.at[which, partner(d)])
        for h in range(2):

            @pl.when(side[h])
            def _():
                for d in ds:
                    arrived(edge_in.at[which, partner(d), h], near_recv.at[which, 2 + h, partner(d)])

        for v in range(2):

            @pl.when(vert[v])
            def _():
                for d in ds:
                    arrived(rim_in.at[which, partner(d), v], near_recv.at[which, v, partner(d)])

        for v in range(2):
            for h in range(2):

                @pl.when(jnp.logical_and(vert[v], side[h]))
                def _():
                    for d in ds:
                        arrived(tip_in.at[which, partner(d), v, h], near_recv.at[which, 4 + 2 * v + h, partner(d)])

        for d in ds:
            s = partner(d)
            spread(
                dst.at[d],
                gat[which, s].astype(f32),
                rim_in[which, s, 0].astype(f32),
                rim_in[which, s, 1].astype(f32),
                [edge_in[which, s, h].astype(f32) for h in range(2)],
                [[tip_in[which, s, v, h].astype(f32)[:1] for h in range(2)] for v in range(2)],
            )

    groups = [list(range(d, min(d + 2, tmn))) for d in range(0, tmn, 2)]

    for tail in (sx, sc):
        for s in range(tmn):
            for e in range(3):
                tail[s, e, lift:, :] = jnp.zeros((tail.shape[2] - lift, C), f32)
    for s in range(tmn):
        c9[s, mp:, :] = jnp.zeros((kp - mp, 9 * C), bf)
        xt[s] = jnp.zeros(xt.shape[1:], bf)
    at[...] = jnp.zeros(at.shape, bf)
    for s in range(tmn + 2):
        ghb[s] = jnp.zeros((kp, C), bf)
    ghf[tmn * cells :, :] = jnp.zeros((2 * cells, C), f32)
    gf[...] = jnp.zeros(gf.shape, f32)
    for j in range(3):
        for e in range(3):
            sh[j, e, lift:, :] = jnp.zeros((sh.shape[2] - lift, C), f32)
    pp[taps:, :] = jnp.zeros((pp.shape[0] - taps, C), f32)
    picked = jnp.concatenate(
        [
            jnp.where(
                (lax.broadcasted_iota(jnp.int32, (chunk_pad, C), 1)
                 == (tm * rn + r) * chunk + lax.broadcasted_iota(jnp.int32, (chunk_pad, C), 0))
                & (lax.broadcasted_iota(jnp.int32, (chunk_pad, C), 0) < chunk),
                1.0, 0.0,
            )
            for r in range(rn)
        ],
        axis=0,
    ).astype(bf)

    def tall(src):
        return lax.dot_general(picked, src, NT, preferred_element_type=f32).astype(bf)

    def choose_x(ds):
        for d in ds:
            for q in range(9):
                xt[d, cwp * q : cwp * (q + 1), :mp] = tall(x9[d, :, C * q : C * (q + 1)])

    for ds in groups:
        receive(0, ds, sx)
        for d in ds:
            for q in range(9):
                b, e = q // 3, q % 3
                x9[d, :, C * q : C * (q + 1)] = sx[d, e, cols * b : cols * b + mp, :].astype(bf)
        if ds[0] == 0:
            for k in range(27):
                load_one(k).wait()
        got = jnp.dot(
            x9[ds[0] : ds[-1] + 1].reshape(len(ds) * mp, 9 * C), r1[...], preferred_element_type=f32
        )
        for d in ds:
            conv[partner(d)] = got[(d - ds[0]) * mp : (d - ds[0] + 1) * mp]
        if ds is not groups[-1]:
            choose_x(ds)
    for t in range(tmn):
        hidden = conv[t, :cells, 2 * C :]
        for a in range(2):
            s = t - 2 + a
            if s >= 0:
                hidden = hidden + conv[s, :cells, C * a : C * (a + 1)]
        squash = jax.nn.sigmoid(hidden)
        gate[t] = squash * (1.0 + hidden * (1.0 - squash))
        at[(t + 2) * cwp : (t + 3) * cwp, :cells] = tall((hidden * squash).astype(bf))
    choose_x(groups[-1])
    for k in range(27):
        load_two(k).wait()

    def send_pair(tensor, r):
        return remote(
            pstage.at[tensor, r],
            pland.at[tensor, row],
            pair_send.at[tensor, r],
            pair_recv.at[tensor, row],
            (tm, r, col),
        )

    def send_pairs(tensor):
        for r in range(rn):

            @pl.when(row != r)
            def _():
                send_pair(tensor, r).start()

    def send_piece(tensor, z):
        return remote(
            stage.at[tensor, z], landed.at[tensor, col], rs_send.at[tensor, z], rs_recv.at[tensor, col], (tm, row, z)
        )

    group = slots * chunk_pad // zn

    def scatter(tensor):
        pp[:taps, :] = part[tensor, row]
        for r in range(rn):

            @pl.when(row != r)
            def _():
                arrived(pland.at[tensor, r], pair_recv.at[tensor, r])
                pp[:taps, :] += pland[tensor, r].astype(f32)

        for z in range(zn):
            stage[tensor, z] = jnp.concatenate(
                [pp[group * q : group * (q + 1), ochunk * z : ochunk * (z + 1)] for q in range(zn)],
                axis=1,
            ).astype(bf)
        for z in range(zn):

            @pl.when(col != z)
            def _():
                send_piece(tensor, z).start()

    total = None
    for ds in groups:
        receive(1, ds, sc)
        for d in ds:
            for q in range(9):
                b, e = q // 3, q % 3
                c9[d, :mp, C * q : C * (q + 1)] = sc[d, 2 - e, cols * (2 - b) : cols * (2 - b) + mp, :].astype(bf)
        for d in ds:
            lines = pl.ds(pl.multiple_of(partner(d) * cwp, 16), 3 * cwp)
            got = jnp.dot(at[lines, :], c9[d], preferred_element_type=f32)
            total = got if total is None else total + got
        if ds is groups[-1]:
            for a in range(3):
                for r in range(rn):
                    for q in range(9):
                        k = 9 * a + q
                        piece = total[a * cwp + r * chunk_pad : a * cwp + (r + 1) * chunk_pad, C * q : C * (q + 1)]
                        part[1, r, k * chunk_pad : (k + 1) * chunk_pad, :] = piece
                        pstage[1, r, k * chunk_pad : (k + 1) * chunk_pad, :] = piece.astype(bf)
            send_pairs(1)
        got = lax.dot_general(
            c9[ds[0] : ds[-1] + 1, :mp, :].reshape(len(ds) * mp, 9 * C), r2[...], NT, preferred_element_type=f32
        )
        for d in ds:
            conv[partner(d)] = got[(d - ds[0]) * mp : (d - ds[0] + 1) * mp]
    for t in range(tmn):
        grad = conv[t, :cells, 2 * C :]
        for a in range(2):
            s = t + 2 - a
            if s < tmn:
                grad = grad + conv[s, :cells, C * a : C * (a + 1)]
        grad = (grad * gate[t]).astype(bf)
        ghb[t, :cells, :] = grad
        ghf[t * cells : (t + 1) * cells, :] = grad.astype(f32)

    own3[...] = ghf[pl.ds(pl.multiple_of(tm * cells, 8), 3 * cells), :]
    for h in range(2):
        gedge[h] = own3[pl.ds(h * (cols - 1), 3 * rows, stride=cols), :].astype(bf)
    for v in range(2):
        grim[v] = jnp.concatenate(
            [
                own3[j * cells + v * (cells - cols) : j * cells + v * (cells - cols) + cols, :]
                for j in range(3)
            ],
            axis=0,
        ).astype(bf)
    grims = near(grim, gedge, grim_in, gedge_in, gcorner_in, gnear_sem)
    start_all(grims)

    scatter(1)

    total = None
    for d in range(tmn):
        s = partner(d)
        right_side = jnp.concatenate([ghb[s + 2], ghb[s + 1], ghb[s]], axis=1)
        got = jnp.dot(xt[d], right_side, preferred_element_type=f32)
        total = got if total is None else total + got
    for q in range(9):
        for r in range(rn):
            for a in range(3):
                k = 9 * a + q
                piece = total[q * cwp + r * chunk_pad : q * cwp + (r + 1) * chunk_pad, C * a : C * (a + 1)]
                part[0, r, k * chunk_pad : (k + 1) * chunk_pad, :] = piece
                pstage[0, r, k * chunk_pad : (k + 1) * chunk_pad, :] = piece.astype(bf)
    send_pairs(0)

    scatter(0)

    await_all(grims)
    assemble(gf, 3, grim_in, gedge_in, gcorner_in)
    for j in range(3):
        spread(
            sh.at[j],
            own3[j * cells : (j + 1) * cells, :],
            gf[j, :cols, :],
            gf[j, cols : 2 * cols, :],
            [gf[j, base + 1 : base + 1 + rows, :] for base in (left, right)],
            [[gf[j, base + put : base + put + 1, :] for base in (left, right)] for put in (0, rows + 1)],
        )
        for q in range(9):
            b, e = q // 3, q % 3
            lane = C * (3 * q + 2 - j)
            imc[:, lane : lane + C] = sh[j, 2 - e, cols * (2 - b) : cols * (2 - b) + mp, :].astype(bf)

    total = None
    for q in range(9):
        got = lax.dot_general(
            imc[:, 3 * C * q : 3 * C * (q + 1)], r1[C * q : C * (q + 1), :], NT, preferred_element_type=f32
        )
        total = got if total is None else total + got
    back_ref[...] = flat[1] + total[:cells]

    for tensor in (1, 0):
        acc[tensor] = stage[tensor, col].astype(f32)
        for z in range(zn):

            @pl.when(col != z)
            def _():
                arrived(landed.at[tensor, z], rs_recv.at[tensor, z])
                acc[tensor] += landed[tensor, z].astype(f32)

    for which in range(2):
        for d in range(1, tmn):
            send_block(which, d).wait_send()
        for r in range(rn):

            @pl.when(row != r)
            def _():
                send_pair(which, r).wait_send()

        for z in range(zn):

            @pl.when(col != z)
            def _():
                send_piece(which, z).wait_send()

    for which in range(2):
        each_near(which, lambda copy: copy.wait_send())
    drain_all(grims)


def finish(zn, chunk, chunk_pad, slots, back_ref, acc_ref, out_ref, one_ref, two_ref):
    ochunk = C // zn
    out_ref[...] = back_ref[...]
    for tensor, out in enumerate((one_ref, two_ref)):
        got = acc_ref[tensor]
        whole = jnp.concatenate(
            [got[:, ochunk * q : ochunk * (q + 1)] for q in range(zn)], axis=0
        ).reshape(slots, chunk_pad, ochunk)
        out[...] = whole[:27, :chunk, :]


def body(sizes, inputs, cotangent, weight_one, weight_two):
    tmn, rn, zn = sizes
    _, rows, cols, channels = inputs.shape
    cells = rows * cols
    chunk = channels // (tmn * rn)
    chunk_pad = max(16, chunk)
    slots = 28
    lift = (rows + 2) * cols
    mp = -(-cells // 16) * 16
    kp = -(-cells // 128) * 128
    hs = -(-(2 * cols + 2 * (-(-(rows + 2) // 8) * 8)) // 16) * 16
    cwp = rn * chunk_pad
    taps = 27 * chunk_pad
    dims = (tmn, rn, zn, rows, cols, chunk, chunk_pad, slots)
    vmem = pl.BlockSpec(memory_space=pltpu.VMEM)
    bf, f32 = jnp.bfloat16, jnp.float32
    group = slots * chunk_pad // zn
    dma = pltpu.SemaphoreType.DMA
    lifted = lift + mp - cells
    back, acc = pl.pallas_call(
        functools.partial(kernel, dims),
        out_shape=(
            jax.ShapeDtypeStruct((cells, channels), f32),
            jax.ShapeDtypeStruct((2, group, channels), f32),
        ),
        in_specs=[pl.BlockSpec(memory_space=pl.ANY)] * 4,
        out_specs=(vmem,) * 2,
        scratch_shapes=[
            pltpu.VMEM((2, tmn, cells, channels), bf),
            pltpu.VMEM((2, cells, channels), f32),
            pltpu.VMEM((tmn, 3, lifted, channels), f32),
            pltpu.VMEM((tmn, 3, lifted, channels), f32),
            pltpu.VMEM((tmn, mp, 9 * channels), bf),
            pltpu.VMEM((tmn, kp, 9 * channels), bf),
            pltpu.VMEM((9 * channels, 3 * channels), bf),
            pltpu.VMEM((3 * channels, 9 * channels), bf),
            pltpu.VMEM((tmn, mp, 3 * channels), f32),
            pltpu.VMEM((tmn, cells, channels), f32),
            pltpu.VMEM(((tmn + 2) * cwp, kp), bf),
            pltpu.VMEM((tmn, 9 * cwp, kp), bf),
            pltpu.VMEM((tmn + 2, kp, channels), bf),
            pltpu.VMEM(((tmn + 2) * cells, channels), f32),
            pltpu.VMEM((3 * cells, channels), f32),
            pltpu.VMEM((3, hs, channels), f32),
            pltpu.VMEM((3, 3, lifted, channels), f32),
            pltpu.VMEM((mp, 27 * channels), bf),
            pltpu.VMEM((2, rn, taps, channels), f32),
            pltpu.VMEM((2, rn, taps, channels), bf),
            pltpu.VMEM((2, rn, taps, channels), bf),
            pltpu.VMEM((slots * chunk_pad, channels), f32),
            pltpu.VMEM((2, zn, group, channels), bf),
            pltpu.VMEM((2, zn, group, channels), bf),
            pltpu.VMEM((2, 2, cols, channels), bf),
            pltpu.VMEM((2, 2, rows, channels), bf),
            pltpu.VMEM((2, 2, 2, 8, channels), bf),
            pltpu.VMEM((2, tmn, 2, cols, channels), bf),
            pltpu.VMEM((2, tmn, 2, rows, channels), bf),
            pltpu.VMEM((2, tmn, 2, 2, 8, channels), bf),
            pltpu.VMEM((2, 3 * cols, channels), bf),
            pltpu.VMEM((2, 3 * rows, channels), bf),
            pltpu.VMEM((2, 3 * cols, channels), bf),
            pltpu.VMEM((2, 3 * rows, channels), bf),
            pltpu.VMEM((2, 2, 3 * rows, channels), bf),
            dma((2,)),
            dma((27,)),
            dma((27,)),
            dma((2, tmn)),
            dma((2, tmn)),
            dma((2, 8, tmn)),
            dma((2, 8, tmn)),
            dma((2, 8)),
            dma((2, rn)),
            dma((2, rn)),
            dma((2, zn)),
            dma((2, zn)),
        ],
        compiler_params=pltpu.CompilerParams(
            collective_id=0, has_side_effects=True, vmem_limit_bytes=60 * 1024 * 1024
        ),
    )(
        inputs.reshape(cells, channels),
        cotangent.reshape(cells, channels),
        weight_one.reshape(27 * channels, channels),
        weight_two.reshape(27 * channels, channels),
    )
    back, one, two = pl.pallas_call(
        functools.partial(finish, zn, chunk, chunk_pad, slots),
        out_shape=(
            jax.ShapeDtypeStruct((cells, channels), f32),
            jax.ShapeDtypeStruct((27, chunk, channels // zn), f32),
            jax.ShapeDtypeStruct((27, chunk, channels // zn), f32),
        ),
        in_specs=[vmem] * 2,
        out_specs=(vmem,) * 3,
    )(back, acc)
    return back.reshape(1, rows, cols, channels), one, two


def solution(mesh):
    sizes = (mesh.shape["tm"], mesh.shape["rows"], mesh.shape["cols"])
    placed = (P("tm", "rows", "cols", None), P("tm", "rows", "cols", None), P(), P())
    return jax.shard_map(
        functools.partial(body, sizes),
        mesh=mesh,
        in_specs=placed,
        out_specs=(
            P("tm", "rows", "cols", None),
            P(None, ("tm", "rows"), "cols"),
            P(None, ("tm", "rows"), "cols"),
        ),
        check_vma=False,
    )
```

```python
import functools

import jax
import jax.numpy as jnp
from jax import lax
from jax.experimental import pallas as pl
from jax.experimental.pallas import tpu as pltpu
from jax.sharding import PartitionSpec as P

MESH = pl.DeviceIdType.MESH
NT = (((1,), (1,)), ((), ()))
C = 128


def kernel(
    dims,
    x_ref,
    c_ref,
    w1_ref,
    w2_ref,
    back_ref,
    one_ref,
    two_ref,
    gat,
    flat,
    sx,
    sc,
    x9,
    c9,
    r1,
    r2,
    conv,
    gate,
    at,
    xt,
    ghb,
    ghf,
    own3,
    gf,
    sh,
    imc,
    part,
    pstage,
    pland,
    pp,
    stage,
    landed,
    rim,
    edge,
    tip,
    rim_in,
    edge_in,
    tip_in,
    grim,
    gedge,
    grim_in,
    gedge_in,
    gcorner_in,
    own_sem,
    w1_sem,
    w2_sem,
    blk_send,
    blk_recv,
    near_send,
    near_recv,
    gnear_sem,
    pair_send,
    pair_recv,
    rs_send,
    rs_recv,
):
    tmn, rn, zn, rows, cols, chunk, chunk_pad, slots = dims
    cells = rows * cols
    lift = (rows + 2) * cols
    left = 2 * cols
    right = left + -(-(rows + 2) // 8) * 8
    mp, kp = x9.shape[1], c9.shape[1]
    taps = 27 * chunk_pad
    cwp = rn * chunk_pad
    ochunk = C // zn
    bf, f32 = jnp.bfloat16, jnp.float32
    tm, row, col = lax.axis_index("tm"), lax.axis_index("rows"), lax.axis_index("cols")
    vert = (row > 0, row < rn - 1)
    side = (col > 0, col < zn - 1)
    step = (-1, 1)

    def partner(d):
        if tmn == 4:
            flips = (tm, tm + 1 - 2 * lax.rem(tm, 2), tm + 2 - 4 * (tm // 2), 3 - tm)
            return flips[d]
        return lax.rem(tm + d, tmn)

    blocks = (x_ref, c_ref)

    def keep(which):
        return pltpu.make_async_copy(blocks[which], gat.at[which, tm], own_sem.at[which])

    keep(0).start()
    keep(1).start()
    barrier = pltpu.get_barrier_semaphore()

    def greet(place):
        pl.semaphore_signal(barrier, inc=1, device_id=place, device_id_type=MESH)

    for z in range(zn):

        @pl.when(jnp.logical_or(col - z > 1, z - col > 1))
        def _():
            greet((tm, row, z))

    for d in range(tmn - 1, 0, -1):
        greet((partner(d), row, col))
    for v in range(2):
        for h in range(2):

            @pl.when(jnp.logical_and(vert[v], side[h]))
            def _():
                for d in range(tmn - 1, -1, -1):
                    greet((partner(d), row + step[v], col + step[h]))

    for h in range(2):

        @pl.when(side[h])
        def _():
            for d in range(tmn - 1, -1, -1):
                greet((partner(d), row, col + step[h]))

    for v in range(2):

        @pl.when(vert[v])
        def _():
            for d in range(tmn - 1, -1, -1):
                greet((partner(d), row + step[v], col))

    for r in range(rn if rn > 2 else 0):

        @pl.when(jnp.logical_or(row - r > 1, r - row > 1))
        def _():
            greet((tm, r, col))

    def load_one(k):
        a, q = k // 9, k % 9
        return pltpu.make_async_copy(
            w1_ref.at[pl.ds(C * k, C), :], r1.at[pl.ds(C * q, C), pl.ds(C * a, C)], w1_sem.at[k]
        )

    def load_two(k):
        a, q = k // 9, k % 9
        return pltpu.make_async_copy(
            w2_ref.at[pl.ds(C * k, C), :], r2.at[pl.ds(C * a, C), pl.ds(C * q, C)], w2_sem.at[k]
        )

    for k in range(27):
        load_one(k).start()
    for k in range(27):
        load_two(k).start()

    for v in range(2):

        @pl.when(jnp.logical_not(vert[v]))
        def _():
            rim_in[:, :, v] = jnp.zeros((2, tmn, cols, C), bf)
            tip_in[:, :, v] = jnp.zeros((2, tmn, 2, 8, C), bf)

    for h in range(2):

        @pl.when(jnp.logical_not(side[h]))
        def _():
            edge_in[:, :, h] = jnp.zeros((2, tmn, rows, C), bf)
            tip_in[:, :, :, h] = jnp.zeros((2, tmn, 2, 8, C), bf)

    for which in range(2):
        keep(which).wait()
        flat[which] = gat[which, tm].astype(f32)
        for h in range(2):
            edge[which, h] = flat[which, pl.ds(h * (cols - 1), rows, stride=cols), :].astype(bf)
        for v in range(2):
            line = flat[which, v * (cells - cols) : v * (cells - cols) + cols, :]
            rim[which, v] = line.astype(bf)
            for h in range(2):
                tip[which, v, h] = jnp.broadcast_to(line[h * (cols - 1) : h * (cols - 1) + 1], (8, C)).astype(bf)

    def remote(src, dst, send, recv, place):
        return pltpu.make_async_remote_copy(
            src_ref=src, dst_ref=dst, send_sem=send, recv_sem=recv, device_id=place, device_id_type=MESH
        )

    def near(out_rim, out_edge, in_rim, in_edge, in_corner, sems):
        found = []
        for v in range(2):
            found.append((
                vert[v],
                lambda v=v: remote(
                    out_rim.at[v], in_rim.at[1 - v], sems.at[0, v], sems.at[1, 1 - v], (tm, row + step[v], col)
                ),
                in_rim.at[v],
                sems.at[1, v],
            ))
        for h in range(2):
            found.append((
                side[h],
                lambda h=h: remote(
                    out_edge.at[h], in_edge.at[1 - h], sems.at[0, 2 + h], sems.at[1, 3 - h], (tm, row, col + step[h])
                ),
                in_edge.at[h],
                sems.at[1, 2 + h],
            ))
        for v in range(2):
            for h in range(2):
                found.append((
                    jnp.logical_and(vert[v], side[h]),
                    lambda v=v, h=h: remote(
                        out_edge.at[h],
                        in_corner.at[1 - v, 1 - h],
                        sems.at[0, 4 + 2 * v + h],
                        sems.at[1, 4 + 2 * (1 - v) + 1 - h],
                        (tm, row + step[v], col + step[h]),
                    ),
                    in_corner.at[v, h],
                    sems.at[1, 4 + 2 * v + h],
                ))
        return found

    def start_all(found):
        for cond, copy, _, _ in found:

            @pl.when(cond)
            def _():
                copy().start()

    def drain_all(found):
        for cond, copy, _, _ in found:

            @pl.when(cond)
            def _():
                copy().wait_send()

    def arrived(dst, sem):
        remote(dst, dst, sem, sem, (tm, row, col)).wait_recv()

    def await_all(found):
        for cond, _, dst, sem in found:

            @pl.when(cond)
            def _():
                arrived(dst, sem)

    def assemble(dst, count, in_rim, in_edge, in_corner):
        for v in range(2):

            @pl.when(vert[v])
            def _():
                got = in_rim[v].astype(f32)
                for q in range(count):
                    dst[q, v * cols : (v + 1) * cols, :] = got[q * cols : (q + 1) * cols]

        for h, base in enumerate((left, right)):

            @pl.when(side[h])
            def _():
                got = in_edge[h].astype(f32)
                for q in range(count):
                    dst[q, base + 1 : base + 1 + rows, :] = got[q * rows : (q + 1) * rows]

            for v in range(2):

                @pl.when(jnp.logical_and(vert[v], side[h]))
                def _():
                    got = in_corner[v, h].astype(f32)
                    put = base + v * (rows + 1)
                    for q in range(count):
                        take = q * rows + (1 - v) * (rows - 1)
                        dst[q, put : put + 1, :] = got[take : take + 1]

    def spread(dst, v, top, bottom, sides, tips):
        dst[1, :cols, :] = top
        dst[1, cols : cols + cells, :] = v
        dst[1, cols + cells : lift, :] = bottom
        dst[0, 1 : cols + 1, :] = top
        dst[0, cols + 1 : cols + cells + 1, :] = v
        dst[0, cols + cells + 1 : lift, :] = bottom[: cols - 1]
        dst[0, :1, :] = tips[0][0]
        dst[0, pl.ds(cols, rows, stride=cols), :] = sides[0]
        dst[0, cols + cells : cols + cells + 1, :] = tips[1][0]
        dst[2, : cols - 1, :] = top[1:]
        dst[2, cols - 1 : cols + cells - 1, :] = v
        dst[2, cols + cells - 1 : lift - 1, :] = bottom
        dst[2, cols - 1 : cols, :] = tips[0][1]
        dst[2, pl.ds(2 * cols - 1, rows, stride=cols), :] = sides[1]
        dst[2, lift - 1 : lift, :] = tips[1][1]

    nv = vert[0].astype(jnp.int32) + vert[1].astype(jnp.int32)
    nh = side[0].astype(jnp.int32) + side[1].astype(jnp.int32)
    pl.semaphore_wait(barrier, tmn * (1 + nv) * (1 + nh) - 1 + zn - 1 - nh + rn - 1 - nv)

    def send_block(which, d):
        return remote(
            gat.at[which, tm],
            gat.at[which, tm],
            blk_send.at[which, d],
            blk_recv.at[which, tm],
            (partner(d), row, col),
        )

    def send_rim(which, v, d):
        return remote(
            rim.at[which, v],
            rim_in.at[which, tm, 1 - v],
            near_send.at[which, v, d],
            near_recv.at[which, 1 - v, tm],
            (partner(d), row + step[v], col),
        )

    def send_edge(which, h, d):
        return remote(
            edge.at[which, h],
            edge_in.at[which, tm, 1 - h],
            near_send.at[which, 2 + h, d],
            near_recv.at[which, 3 - h, tm],
            (partner(d), row, col + step[h]),
        )

    def send_tip(which, v, h, d):
        return remote(
            tip.at[which, v, h],
            tip_in.at[which, tm, 1 - v, 1 - h],
            near_send.at[which, 4 + 2 * v + h, d],
            near_recv.at[which, 4 + 2 * (1 - v) + 1 - h, tm],
            (partner(d), row + step[v], col + step[h]),
        )

    def each_near(which, ds, act):
        for h in range(2):

            @pl.when(side[h])
            def _():
                for d in ds:
                    act(send_edge(which, h, d))

        for v in range(2):

            @pl.when(vert[v])
            def _():
                for d in ds:
                    act(send_rim(which, v, d))

        for v in range(2):
            for h in range(2):

                @pl.when(jnp.logical_and(vert[v], side[h]))
                def _():
                    for d in ds:
                        act(send_tip(which, v, h, d))

    groups = [list(range(d, min(d + 2, tmn))) for d in range(0, tmn, 2)]
    for which in range(2):
        for ds in groups:
            each_near(which, ds[::-1], lambda copy: copy.start())
            for d in ds[::-1]:
                if d:
                    send_block(which, d).start()

    def receive(which, ds, dst):
        for d in ds[ds[0] == 0 :]:
            arrived(gat.at[which, partner(d)], blk_recv.at[which, partner(d)])
        for h in range(2):

            @pl.when(side[h])
            def _():
                for d in ds:
                    arrived(edge_in.at[which, partner(d), h], near_recv.at[which, 2 + h, partner(d)])

        for v in range(2):

            @pl.when(vert[v])
            def _():
                for d in ds:
                    arrived(rim_in.at[which, partner(d), v], near_recv.at[which, v, partner(d)])

        for v in range(2):
            for h in range(2):

                @pl.when(jnp.logical_and(vert[v], side[h]))
                def _():
                    for d in ds:
                        arrived(tip_in.at[which, partner(d), v, h], near_recv.at[which, 4 + 2 * v + h, partner(d)])

        for d in ds:
            s = partner(d)
            spread(
                dst.at[d],
                gat[which, s].astype(f32),
                rim_in[which, s, 0].astype(f32),
                rim_in[which, s, 1].astype(f32),
                [edge_in[which, s, h].astype(f32) for h in range(2)],
                [[tip_in[which, s, v, h].astype(f32)[:1] for h in range(2)] for v in range(2)],
            )

    for tail in (sx, sc):
        for s in range(tmn):
            for e in range(3):
                tail[s, e, lift:, :] = jnp.zeros((tail.shape[2] - lift, C), f32)
    for s in range(tmn):
        c9[s, mp:, :] = jnp.zeros((kp - mp, 9 * C), bf)
        xt[s] = jnp.zeros(xt.shape[1:], bf)
    at[...] = jnp.zeros(at.shape, bf)
    for s in range(tmn + 2):
        ghb[s] = jnp.zeros((kp, C), bf)
    ghf[tmn * cells :, :] = jnp.zeros((2 * cells, C), f32)
    gf[...] = jnp.zeros(gf.shape, f32)
    for j in range(3):
        for e in range(3):
            sh[j, e, lift:, :] = jnp.zeros((sh.shape[2] - lift, C), f32)
    pp[taps:, :] = jnp.zeros((pp.shape[0] - taps, C), f32)
    picked = jnp.concatenate(
        [
            jnp.where(
                (lax.broadcasted_iota(jnp.int32, (chunk_pad, C), 1)
                 == (tm * rn + r) * chunk + lax.broadcasted_iota(jnp.int32, (chunk_pad, C), 0))
                & (lax.broadcasted_iota(jnp.int32, (chunk_pad, C), 0) < chunk),
                1.0, 0.0,
            )
            for r in range(rn)
        ],
        axis=0,
    ).astype(bf)

    def tall(src):
        return lax.dot_general(picked, src, NT, preferred_element_type=f32).astype(bf)

    def choose_x(ds):
        for d in ds:
            for q in range(9):
                xt[d, cwp * q : cwp * (q + 1), :mp] = tall(x9[d, :, C * q : C * (q + 1)])

    for ds in groups:
        receive(0, ds, sx)
        for d in ds:
            for q in range(9):
                b, e = q // 3, q % 3
                x9[d, :, C * q : C * (q + 1)] = sx[d, e, cols * b : cols * b + mp, :].astype(bf)
        if ds[0] == 0:
            for k in range(27):
                load_one(k).wait()
        got = jnp.dot(
            x9[ds[0] : ds[-1] + 1].reshape(len(ds) * mp, 9 * C), r1[...], preferred_element_type=f32
        )
        for d in ds:
            conv[partner(d)] = got[(d - ds[0]) * mp : (d - ds[0] + 1) * mp]
        if ds is not groups[-1]:
            choose_x(ds)
    for t in range(tmn):
        hidden = conv[t, :cells, 2 * C :]
        for a in range(2):
            s = t - 2 + a
            if s >= 0:
                hidden = hidden + conv[s, :cells, C * a : C * (a + 1)]
        squash = jax.nn.sigmoid(hidden)
        gate[t] = squash * (1.0 + hidden * (1.0 - squash))
        at[(t + 2) * cwp : (t + 3) * cwp, :cells] = tall((hidden * squash).astype(bf))
    for k in range(27):
        load_two(k).wait()

    def send_pair(tensor, r):
        return remote(
            pstage.at[tensor, r],
            pland.at[tensor, row],
            pair_send.at[tensor, r],
            pair_recv.at[tensor, row],
            (tm, r, col),
        )

    def send_pairs(tensor):
        for r in range(rn):

            @pl.when(row != r)
            def _():
                send_pair(tensor, r).start()

    def send_piece(tensor, z):
        return remote(
            stage.at[tensor, z], landed.at[tensor, col], rs_send.at[tensor, z], rs_recv.at[tensor, col], (tm, row, z)
        )

    group = slots * chunk_pad // zn

    def scatter(tensor):
        pp[:taps, :] = part[tensor, row]
        for r in range(rn):

            @pl.when(row != r)
            def _():
                arrived(pland.at[tensor, r], pair_recv.at[tensor, r])
                pp[:taps, :] += pland[tensor, r].astype(f32)

        for z in range(zn):
            stage[tensor, z] = jnp.concatenate(
                [pp[group * q : group * (q + 1), ochunk * z : ochunk * (z + 1)] for q in range(zn)],
                axis=1,
            ).astype(bf)
        for z in range(zn):

            @pl.when(col != z)
            def _():
                send_piece(tensor, z).start()

    total = None
    for ds in groups:
        receive(1, ds, sc)
        for d in ds:
            for q in range(9):
                b, e = q // 3, q % 3
                c9[d, :mp, C * q : C * (q + 1)] = sc[d, 2 - e, cols * (2 - b) : cols * (2 - b) + mp, :].astype(bf)
        for d in ds:
            lines = pl.ds(pl.multiple_of(partner(d) * cwp, 16), 3 * cwp)
            got = jnp.dot(at[lines, :], c9[d], preferred_element_type=f32)
            total = got if total is None else total + got
        if ds is groups[-1]:
            for a in range(3):
                for r in range(rn):
                    for q in range(9):
                        k = 9 * a + q
                        piece = total[a * cwp + r * chunk_pad : a * cwp + (r + 1) * chunk_pad, C * q : C * (q + 1)]
                        part[1, r, k * chunk_pad : (k + 1) * chunk_pad, :] = piece
                        pstage[1, r, k * chunk_pad : (k + 1) * chunk_pad, :] = piece.astype(bf)
            send_pairs(1)
        got = lax.dot_general(
            c9[ds[0] : ds[-1] + 1, :mp, :].reshape(len(ds) * mp, 9 * C), r2[...], NT, preferred_element_type=f32
        )
        for d in ds:
            conv[partner(d)] = got[(d - ds[0]) * mp : (d - ds[0] + 1) * mp]
    for t in range(tmn):
        grad = conv[t, :cells, 2 * C :]
        for a in range(2):
            s = t + 2 - a
            if s < tmn:
                grad = grad + conv[s, :cells, C * a : C * (a + 1)]
        grad = (grad * gate[t]).astype(bf)
        ghb[t, :cells, :] = grad
        ghf[t * cells : (t + 1) * cells, :] = grad.astype(f32)

    own3[...] = ghf[pl.ds(pl.multiple_of(tm * cells, 8), 3 * cells), :]
    for h in range(2):
        gedge[h] = own3[pl.ds(h * (cols - 1), 3 * rows, stride=cols), :].astype(bf)
    for v in range(2):
        grim[v] = jnp.concatenate(
            [
                own3[j * cells + v * (cells - cols) : j * cells + v * (cells - cols) + cols, :]
                for j in range(3)
            ],
            axis=0,
        ).astype(bf)
    grims = near(grim, gedge, grim_in, gedge_in, gcorner_in, gnear_sem)
    start_all(grims)

    choose_x(groups[-1])

    scatter(1)

    total = None
    for d in range(tmn):
        s = partner(d)
        right_side = jnp.concatenate([ghb[s + 2], ghb[s + 1], ghb[s]], axis=1)
        got = jnp.dot(xt[d], right_side, preferred_element_type=f32)
        total = got if total is None else total + got
    for q in range(9):
        for r in range(rn):
            for a in range(3):
                k = 9 * a + q
                piece = total[q * cwp + r * chunk_pad : q * cwp + (r + 1) * chunk_pad, C * a : C * (a + 1)]
                part[0, r, k * chunk_pad : (k + 1) * chunk_pad, :] = piece
                pstage[0, r, k * chunk_pad : (k + 1) * chunk_pad, :] = piece.astype(bf)
    send_pairs(0)

    scatter(0)

    await_all(grims)
    assemble(gf, 3, grim_in, gedge_in, gcorner_in)
    for j in range(3):
        spread(
            sh.at[j],
            own3[j * cells : (j + 1) * cells, :],
            gf[j, :cols, :],
            gf[j, cols : 2 * cols, :],
            [gf[j, base + 1 : base + 1 + rows, :] for base in (left, right)],
            [[gf[j, base + put : base + put + 1, :] for base in (left, right)] for put in (0, rows + 1)],
        )
        for q in range(9):
            b, e = q // 3, q % 3
            lane = C * (3 * q + 2 - j)
            imc[:, lane : lane + C] = sh[j, 2 - e, cols * (2 - b) : cols * (2 - b) + mp, :].astype(bf)

    total = None
    for q in range(9):
        got = lax.dot_general(
            imc[:, 3 * C * q : 3 * C * (q + 1)], r1[C * q : C * (q + 1), :], NT, preferred_element_type=f32
        )
        total = got if total is None else total + got
    back_ref[...] = flat[1] + total[:cells]

    for tensor, out in ((1, two_ref), (0, one_ref)):
        for z in range(zn):

            @pl.when(col != z)
            def _():
                arrived(landed.at[tensor, z], rs_recv.at[tensor, z])

            @pl.when(col == z)
            def _():
                landed[tensor, z] = stage[tensor, z]

        got = landed[tensor, 0].astype(f32)
        for z in range(1, zn):
            got = got + landed[tensor, z].astype(f32)
        whole = jnp.concatenate(
            [got[:, ochunk * q : ochunk * (q + 1)] for q in range(zn)], axis=0
        ).reshape(slots, chunk_pad, ochunk)
        out[...] = whole[:27, :chunk, :]

    for which in range(2):
        for d in range(1, tmn):
            send_block(which, d).wait_send()
        for r in range(rn):

            @pl.when(row != r)
            def _():
                send_pair(which, r).wait_send()

        for z in range(zn):

            @pl.when(col != z)
            def _():
                send_piece(which, z).wait_send()

    for which in range(2):
        each_near(which, range(tmn), lambda copy: copy.wait_send())
    drain_all(grims)


def finish(back_ref, one_ref, two_ref, back_out, one_out, two_out, sem):
    pairs = ((back_ref, back_out), (one_ref, one_out), (two_ref, two_out))
    copies = [pltpu.make_async_copy(src, dst, sem.at[i]) for i, (src, dst) in enumerate(pairs)]
    for copy in copies:
        copy.start()
    for copy in copies:
        copy.wait()


def body(sizes, inputs, cotangent, weight_one, weight_two):
    tmn, rn, zn = sizes
    _, rows, cols, channels = inputs.shape
    cells = rows * cols
    chunk = channels // (tmn * rn)
    chunk_pad = max(16, chunk)
    slots = 28
    lift = (rows + 2) * cols
    mp = -(-cells // 16) * 16
    kp = -(-cells // 128) * 128
    hs = -(-(2 * cols + 2 * (-(-(rows + 2) // 8) * 8)) // 16) * 16
    cwp = rn * chunk_pad
    taps = 27 * chunk_pad
    dims = (tmn, rn, zn, rows, cols, chunk, chunk_pad, slots)
    vmem = pl.BlockSpec(memory_space=pltpu.VMEM)
    bf, f32 = jnp.bfloat16, jnp.float32
    group = slots * chunk_pad // zn
    dma = pltpu.SemaphoreType.DMA
    lifted = lift + mp - cells
    sums = (27, chunk, channels // zn)
    outs = pl.pallas_call(
        functools.partial(kernel, dims),
        out_shape=(
            pltpu.VMEM((cells, channels), f32),
            pltpu.VMEM(sums, f32),
            pltpu.VMEM(sums, f32),
        ),
        in_specs=[pl.BlockSpec(memory_space=pl.ANY)] * 4,
        out_specs=(vmem,) * 3,
        scratch_shapes=[
            pltpu.VMEM((2, tmn, cells, channels), bf),
            pltpu.VMEM((2, cells, channels), f32),
            pltpu.VMEM((tmn, 3, lifted, channels), f32),
            pltpu.VMEM((tmn, 3, lifted, channels), f32),
            pltpu.VMEM((tmn, mp, 9 * channels), bf),
            pltpu.VMEM((tmn, kp, 9 * channels), bf),
            pltpu.VMEM((9 * channels, 3 * channels), bf),
            pltpu.VMEM((3 * channels, 9 * channels), bf),
            pltpu.VMEM((tmn, mp, 3 * channels), f32),
            pltpu.VMEM((tmn, cells, channels), f32),
            pltpu.VMEM(((tmn + 2) * cwp, kp), bf),
            pltpu.VMEM((tmn, 9 * cwp, kp), bf),
            pltpu.VMEM((tmn + 2, kp, channels), bf),
            pltpu.VMEM(((tmn + 2) * cells, channels), f32),
            pltpu.VMEM((3 * cells, channels), f32),
            pltpu.VMEM((3, hs, channels), f32),
            pltpu.VMEM((3, 3, lifted, channels), f32),
            pltpu.VMEM((mp, 27 * channels), bf),
            pltpu.VMEM((2, rn, taps, channels), f32),
            pltpu.VMEM((2, rn, taps, channels), bf),
            pltpu.VMEM((2, rn, taps, channels), bf),
            pltpu.VMEM((slots * chunk_pad, channels), f32),
            pltpu.VMEM((2, zn, group, channels), bf),
            pltpu.VMEM((2, zn, group, channels), bf),
            pltpu.VMEM((2, 2, cols, channels), bf),
            pltpu.VMEM((2, 2, rows, channels), bf),
            pltpu.VMEM((2, 2, 2, 8, channels), bf),
            pltpu.VMEM((2, tmn, 2, cols, channels), bf),
            pltpu.VMEM((2, tmn, 2, rows, channels), bf),
            pltpu.VMEM((2, tmn, 2, 2, 8, channels), bf),
            pltpu.VMEM((2, 3 * cols, channels), bf),
            pltpu.VMEM((2, 3 * rows, channels), bf),
            pltpu.VMEM((2, 3 * cols, channels), bf),
            pltpu.VMEM((2, 3 * rows, channels), bf),
            pltpu.VMEM((2, 2, 3 * rows, channels), bf),
            dma((2,)),
            dma((27,)),
            dma((27,)),
            dma((2, tmn)),
            dma((2, tmn)),
            dma((2, 8, tmn)),
            dma((2, 8, tmn)),
            dma((2, 8)),
            dma((2, rn)),
            dma((2, rn)),
            dma((2, zn)),
            dma((2, zn)),
        ],
        compiler_params=pltpu.CompilerParams(
            collective_id=0, has_side_effects=True, vmem_limit_bytes=60 * 1024 * 1024
        ),
    )(
        inputs.reshape(cells, channels),
        cotangent.reshape(cells, channels),
        weight_one.reshape(27 * channels, channels),
        weight_two.reshape(27 * channels, channels),
    )
    back, one, two = pl.pallas_call(
        finish,
        out_shape=(
            jax.ShapeDtypeStruct((cells, channels), f32),
            jax.ShapeDtypeStruct(sums, f32),
            jax.ShapeDtypeStruct(sums, f32),
        ),
        in_specs=[vmem] * 3,
        out_specs=(pl.BlockSpec(memory_space=pl.ANY),) * 3,
        scratch_shapes=[dma((3,))],
    )(*[pltpu.with_memory_space_constraint(out, pltpu.VMEM) for out in outs])
    return back.reshape(1, rows, cols, channels), one, two


def solution(mesh):
    sizes = (mesh.shape["tm"], mesh.shape["rows"], mesh.shape["cols"])
    placed = (P("tm", "rows", "cols", None), P("tm", "rows", "cols", None), P(), P())
    return jax.shard_map(
        functools.partial(body, sizes),
        mesh=mesh,
        in_specs=placed,
        out_specs=(
            P("tm", "rows", "cols", None),
            P(None, ("tm", "rows"), "cols"),
            P(None, ("tm", "rows"), "cols"),
        ),
        check_vma=False,
    )
```

```python
import functools

import jax
import jax.numpy as jnp
from jax import lax
from jax.experimental import pallas as pl
from jax.experimental.pallas import tpu as pltpu
from jax.sharding import PartitionSpec as P

MESH = pl.DeviceIdType.MESH
NT = (((1,), (1,)), ((), ()))
C = 128


def kernel(
    dims,
    x_ref,
    c_ref,
    w1_ref,
    w2_ref,
    back_ref,
    one_ref,
    two_ref,
    gat,
    flat,
    sx,
    sc,
    x9,
    c9,
    r1,
    r2,
    conv,
    gate,
    at,
    xt,
    ghb,
    ghf,
    own3,
    gf,
    sh,
    imc,
    part,
    pstage,
    pland,
    pp,
    stage,
    landed,
    rim,
    edge,
    tip,
    rim_in,
    edge_in,
    tip_in,
    grim,
    gedge,
    grim_in,
    gedge_in,
    gcorner_in,
    own_sem,
    w_sem,
    blk_send,
    blk_recv,
    near_send,
    near_recv,
    gnear_sem,
    pair_send,
    pair_recv,
    rs_send,
    rs_recv,
):
    tmn, rn, zn, rows, cols, chunk, chunk_pad, slots = dims
    cells = rows * cols
    lift = (rows + 2) * cols
    left = 2 * cols
    right = left + -(-(rows + 2) // 8) * 8
    mp, kp = x9.shape[1], c9.shape[1]
    taps = 27 * chunk_pad
    cwp = rn * chunk_pad
    ochunk = C // zn
    bf, f32 = jnp.bfloat16, jnp.float32
    tm, row, col = lax.axis_index("tm"), lax.axis_index("rows"), lax.axis_index("cols")
    vert = (row > 0, row < rn - 1)
    side = (col > 0, col < zn - 1)
    step = (-1, 1)

    def partner(d):
        got, bit = tm, 1
        while bit <= d:
            if d & bit:
                got = got + bit - 2 * bit * lax.rem(got // bit, 2)
            bit *= 2
        return got

    blocks = (x_ref, c_ref)

    def keep(which):
        return pltpu.make_async_copy(blocks[which], gat.at[which, 0], own_sem.at[which])

    keep(0).start()
    keep(1).start()
    barrier = pltpu.get_barrier_semaphore()

    def greet(place):
        pl.semaphore_signal(barrier, inc=1, device_id=place, device_id_type=MESH)

    for z in range(zn):

        @pl.when(jnp.logical_or(col - z > 1, z - col > 1))
        def _():
            greet((tm, row, z))

    for d in range(tmn - 1, 0, -1):
        greet((partner(d), row, col))
    for v in range(2):
        for h in range(2):

            @pl.when(jnp.logical_and(vert[v], side[h]))
            def _():
                for d in range(tmn - 1, -1, -1):
                    greet((partner(d), row + step[v], col + step[h]))

    for h in range(2):

        @pl.when(side[h])
        def _():
            for d in range(tmn - 1, -1, -1):
                greet((partner(d), row, col + step[h]))

    for v in range(2):

        @pl.when(vert[v])
        def _():
            for d in range(tmn - 1, -1, -1):
                greet((partner(d), row + step[v], col))

    for r in range(rn if rn > 2 else 0):

        @pl.when(jnp.logical_or(row - r > 1, r - row > 1))
        def _():
            greet((tm, r, col))

    def load_one(k):
        a, q = k // 9, k % 9
        return pltpu.make_async_copy(
            w1_ref.at[pl.ds(C * k, C), :], r1.at[pl.ds(C * q, C), pl.ds(C * a, C)], w_sem.at[0]
        )

    def load_two(k):
        a, q = k // 9, k % 9
        return pltpu.make_async_copy(
            w2_ref.at[pl.ds(C * k, C), :], r2.at[pl.ds(C * a, C), pl.ds(C * q, C)], w_sem.at[1]
        )

    for k in range(27):
        load_one(k).start()
    for k in range(27):
        load_two(k).start()

    for v in range(2):

        @pl.when(jnp.logical_not(vert[v]))
        def _():
            rim_in[:, v] = jnp.zeros((2, tmn, cols, C), bf)
            tip_in[:, v] = jnp.zeros((2, 2, tmn, 8, C), bf)

    for h in range(2):

        @pl.when(jnp.logical_not(side[h]))
        def _():
            edge_in[:, h] = jnp.zeros((2, tmn, rows, C), bf)
            tip_in[:, :, h] = jnp.zeros((2, 2, tmn, 8, C), bf)

    for which in range(2):
        keep(which).wait()
        flat[which] = gat[which, 0].astype(f32)
        for h in range(2):
            edge[which, h] = flat[which, pl.ds(h * (cols - 1), rows, stride=cols), :].astype(bf)
        for v in range(2):
            line = flat[which, v * (cells - cols) : v * (cells - cols) + cols, :]
            rim[which, v] = line.astype(bf)
            for h in range(2):
                tip[which, v, h] = jnp.broadcast_to(line[h * (cols - 1) : h * (cols - 1) + 1], (8, C)).astype(bf)

    def remote(src, dst, send, recv, place):
        return pltpu.make_async_remote_copy(
            src_ref=src, dst_ref=dst, send_sem=send, recv_sem=recv, device_id=place, device_id_type=MESH
        )

    def near(out_rim, out_edge, in_rim, in_edge, in_corner, sems):
        found = []
        for v in range(2):
            found.append((
                vert[v],
                lambda v=v: remote(
                    out_rim.at[v], in_rim.at[1 - v], sems.at[0, v], sems.at[1, 1 - v], (tm, row + step[v], col)
                ),
                in_rim.at[v],
                sems.at[1, v],
            ))
        for h in range(2):
            found.append((
                side[h],
                lambda h=h: remote(
                    out_edge.at[h], in_edge.at[1 - h], sems.at[0, 2 + h], sems.at[1, 3 - h], (tm, row, col + step[h])
                ),
                in_edge.at[h],
                sems.at[1, 2 + h],
            ))
        for v in range(2):
            for h in range(2):
                found.append((
                    jnp.logical_and(vert[v], side[h]),
                    lambda v=v, h=h: remote(
                        out_edge.at[h],
                        in_corner.at[1 - v, 1 - h],
                        sems.at[0, 4 + 2 * v + h],
                        sems.at[1, 4 + 2 * (1 - v) + 1 - h],
                        (tm, row + step[v], col + step[h]),
                    ),
                    in_corner.at[v, h],
                    sems.at[1, 4 + 2 * v + h],
                ))
        return found

    def start_all(found):
        for cond, copy, _, _ in found:

            @pl.when(cond)
            def _():
                copy().start()

    def drain_all(found):
        for cond, copy, _, _ in found:

            @pl.when(cond)
            def _():
                copy().wait_send()

    def arrived(dst, sem):
        remote(dst, dst, sem, sem, (tm, row, col)).wait_recv()

    def await_all(found):
        for cond, _, dst, sem in found:

            @pl.when(cond)
            def _():
                arrived(dst, sem)

    def assemble(dst, count, in_rim, in_edge, in_corner):
        for v in range(2):

            @pl.when(vert[v])
            def _():
                got = in_rim[v].astype(f32)
                for q in range(count):
                    dst[q, v * cols : (v + 1) * cols, :] = got[q * cols : (q + 1) * cols]

        for h, base in enumerate((left, right)):

            @pl.when(side[h])
            def _():
                got = in_edge[h].astype(f32)
                for q in range(count):
                    dst[q, base + 1 : base + 1 + rows, :] = got[q * rows : (q + 1) * rows]

            for v in range(2):

                @pl.when(jnp.logical_and(vert[v], side[h]))
                def _():
                    got = in_corner[v, h].astype(f32)
                    put = base + v * (rows + 1)
                    for q in range(count):
                        take = q * rows + (1 - v) * (rows - 1)
                        dst[q, put : put + 1, :] = got[take : take + 1]

    def spread(dst, v, top, bottom, sides, tips):
        dst[1, :cols, :] = top
        dst[1, cols : cols + cells, :] = v
        dst[1, cols + cells : lift, :] = bottom
        dst[0, 1 : cols + 1, :] = top
        dst[0, cols + 1 : cols + cells + 1, :] = v
        dst[0, cols + cells + 1 : lift, :] = bottom[: cols - 1]
        dst[0, :1, :] = tips[0][0]
        dst[0, pl.ds(cols, rows, stride=cols), :] = sides[0]
        dst[0, cols + cells : cols + cells + 1, :] = tips[1][0]
        dst[2, : cols - 1, :] = top[1:]
        dst[2, cols - 1 : cols + cells - 1, :] = v
        dst[2, cols + cells - 1 : lift - 1, :] = bottom
        dst[2, cols - 1 : cols, :] = tips[0][1]
        dst[2, pl.ds(2 * cols - 1, rows, stride=cols), :] = sides[1]
        dst[2, lift - 1 : lift, :] = tips[1][1]

    nv = vert[0].astype(jnp.int32) + vert[1].astype(jnp.int32)
    nh = side[0].astype(jnp.int32) + side[1].astype(jnp.int32)
    pl.semaphore_wait(barrier, tmn * (1 + nv) * (1 + nh) - 1 + zn - 1 - nh + rn - 1 - nv)

    groups = [list(range(d, min(d + 2, tmn))) for d in range(0, tmn, 2)]

    def send_block(which, d):
        return remote(
            gat.at[which, 0],
            gat.at[which, d],
            blk_send.at[which],
            blk_recv.at[which, d // 2],
            (partner(d), row, col),
        )

    def send_rim(which, v, d):
        return remote(
            rim.at[which, v],
            rim_in.at[which, 1 - v, d],
            near_send.at[v],
            near_recv.at[which, d // 2, 1 - v],
            (partner(d), row + step[v], col),
        )

    def send_edge(which, h, d):
        return remote(
            edge.at[which, h],
            edge_in.at[which, 1 - h, d],
            near_send.at[2 + h],
            near_recv.at[which, d // 2, 3 - h],
            (partner(d), row, col + step[h]),
        )

    def send_tip(which, v, h, d):
        return remote(
            tip.at[which, v, h],
            tip_in.at[which, 1 - v, 1 - h, d],
            near_send.at[4 + 2 * v + h],
            near_recv.at[which, d // 2, 4 + 2 * (1 - v) + 1 - h],
            (partner(d), row + step[v], col + step[h]),
        )

    def send_near(which, ds):
        for h in range(2):

            @pl.when(side[h])
            def _():
                for d in ds:
                    send_edge(which, h, d).start()

        for v in range(2):

            @pl.when(vert[v])
            def _():
                for d in ds:
                    send_rim(which, v, d).start()

        for v in range(2):
            for h in range(2):

                @pl.when(jnp.logical_and(vert[v], side[h]))
                def _():
                    for d in ds:
                        send_tip(which, v, h, d).start()

    for which in range(2):
        for ds in groups:
            send_near(which, ds[::-1])
            for d in ds[::-1]:
                if d:
                    send_block(which, d).start()

    def sent(like, sem):
        remote(like, like, sem, sem, (tm, row, col)).wait_send()

    def receive(which, ds, dst):
        g, span = ds[0] // 2, pl.ds(ds[0], len(ds))
        if ds[-1]:
            arrived(gat.at[which, max(ds[0], 1) : ds[-1] + 1], blk_recv.at[which, g])
        for h in range(2):

            @pl.when(side[h])
            def _():
                arrived(edge_in.at[which, h, span], near_recv.at[which, g, 2 + h])

        for v in range(2):

            @pl.when(vert[v])
            def _():
                arrived(rim_in.at[which, v, span], near_recv.at[which, g, v])

        for v in range(2):
            for h in range(2):

                @pl.when(jnp.logical_and(vert[v], side[h]))
                def _():
                    arrived(tip_in.at[which, v, h, span], near_recv.at[which, g, 4 + 2 * v + h])

        for d in ds:
            spread(
                dst.at[d],
                gat[which, d].astype(f32),
                rim_in[which, 0, d].astype(f32),
                rim_in[which, 1, d].astype(f32),
                [edge_in[which, h, d].astype(f32) for h in range(2)],
                [[tip_in[which, v, h, d].astype(f32)[:1] for h in range(2)] for v in range(2)],
            )

    for tail in (sx, sc):
        for s in range(tmn):
            for e in range(3):
                tail[s, e, lift:, :] = jnp.zeros((tail.shape[2] - lift, C), f32)
    for s in range(tmn):
        c9[s, mp:, :] = jnp.zeros((kp - mp, 9 * C), bf)
        xt[s] = jnp.zeros(xt.shape[1:], bf)
    at[...] = jnp.zeros(at.shape, bf)
    for s in range(tmn + 2):
        ghb[s] = jnp.zeros((kp, C), bf)
    ghf[tmn * cells :, :] = jnp.zeros((2 * cells, C), f32)
    gf[...] = jnp.zeros(gf.shape, f32)
    for j in range(3):
        for e in range(3):
            sh[j, e, lift:, :] = jnp.zeros((sh.shape[2] - lift, C), f32)
    pp[taps:, :] = jnp.zeros((pp.shape[0] - taps, C), f32)
    picked = jnp.concatenate(
        [
            jnp.where(
                (lax.broadcasted_iota(jnp.int32, (chunk_pad, C), 1)
                 == (tm * rn + r) * chunk + lax.broadcasted_iota(jnp.int32, (chunk_pad, C), 0))
                & (lax.broadcasted_iota(jnp.int32, (chunk_pad, C), 0) < chunk),
                1.0, 0.0,
            )
            for r in range(rn)
        ],
        axis=0,
    ).astype(bf)

    def tall(src):
        return lax.dot_general(picked, src, NT, preferred_element_type=f32).astype(bf)

    def choose_x(ds):
        for d in ds:
            for e in range(3):
                got = lax.dot_general(picked, sx[d, e].astype(bf), NT, preferred_element_type=f32)
                for b in range(3):
                    q = 3 * b + e
                    xt[d, cwp * q : cwp * (q + 1), :mp] = got[:, cols * b : cols * b + mp].astype(bf)

    for ds in groups:
        receive(0, ds, sx)
        for d in ds:
            for q in range(9):
                b, e = q // 3, q % 3
                x9[d, :, C * q : C * (q + 1)] = sx[d, e, cols * b : cols * b + mp, :].astype(bf)
        if ds[0] == 0:
            pltpu.make_async_copy(r1, r1, w_sem.at[0]).wait()
        got = jnp.dot(
            x9[ds[0] : ds[-1] + 1].reshape(len(ds) * mp, 9 * C), r1[...], preferred_element_type=f32
        )
        for d in ds:
            conv[partner(d)] = got[(d - ds[0]) * mp : (d - ds[0] + 1) * mp]
    for t in range(tmn):
        hidden = conv[t, :cells, 2 * C :]
        for a in range(2):
            s = t - 2 + a
            if s >= 0:
                hidden = hidden + conv[s, :cells, C * a : C * (a + 1)]
        squash = jax.nn.sigmoid(hidden)
        gate[t] = squash * (1.0 + hidden * (1.0 - squash))
        at[(t + 2) * cwp : (t + 3) * cwp, :cells] = tall((hidden * squash).astype(bf))

    def send_pairs(tensor):
        for r in range(rn):

            @pl.when(row != r)
            def _():
                remote(
                    pstage.at[tensor, r],
                    pland.at[tensor, row],
                    pair_send.at[tensor],
                    pair_recv.at[tensor],
                    (tm, r, col),
                ).start()

    group = slots * chunk_pad // zn

    def scatter(tensor):
        pp[:taps, :] = part[tensor, row]
        if rn > 1:
            arrived(pland.at[tensor, : rn - 1], pair_recv.at[tensor])
        for r in range(rn):

            @pl.when(row != r)
            def _():
                pp[:taps, :] += pland[tensor, r].astype(f32)

        for z in range(zn):
            stage[tensor, z] = jnp.concatenate(
                [pp[group * q : group * (q + 1), ochunk * z : ochunk * (z + 1)] for q in range(zn)],
                axis=1,
            ).astype(bf)
        for z in range(zn):

            @pl.when(col != z)
            def _():
                remote(
                    stage.at[tensor, z],
                    landed.at[tensor, col],
                    rs_send.at[tensor],
                    rs_recv.at[tensor],
                    (tm, row, z),
                ).start()

    total = None
    for ds in groups:
        receive(1, ds, sc)
        for d in ds:
            for q in range(9):
                b, e = q // 3, q % 3
                c9[d, :mp, C * q : C * (q + 1)] = sc[d, 2 - e, cols * (2 - b) : cols * (2 - b) + mp, :].astype(bf)
        for d in ds:
            lines = pl.ds(pl.multiple_of(partner(d) * cwp, 16), 3 * cwp)
            got = jnp.dot(at[lines, :], c9[d], preferred_element_type=f32)
            total = got if total is None else total + got
    for a in range(3):
        for r in range(rn):
            for q in range(9):
                k = 9 * a + q
                piece = total[a * cwp + r * chunk_pad : a * cwp + (r + 1) * chunk_pad, C * q : C * (q + 1)]
                part[1, r, k * chunk_pad : (k + 1) * chunk_pad, :] = piece
                pstage[1, r, k * chunk_pad : (k + 1) * chunk_pad, :] = piece.astype(bf)
    send_pairs(1)

    pltpu.make_async_copy(r2, r2, w_sem.at[1]).wait()
    got = lax.dot_general(
        c9[:, :mp, :].reshape(tmn * mp, 9 * C), r2[...], NT, preferred_element_type=f32
    )
    for d in range(tmn):
        conv[partner(d)] = got[d * mp : (d + 1) * mp]
    for t in range(tmn):
        grad = conv[t, :cells, 2 * C :]
        for a in range(2):
            s = t + 2 - a
            if s < tmn:
                grad = grad + conv[s, :cells, C * a : C * (a + 1)]
        grad = (grad * gate[t]).astype(bf)
        ghb[t, :cells, :] = grad
        ghf[t * cells : (t + 1) * cells, :] = grad.astype(f32)

    own3[...] = ghf[pl.ds(pl.multiple_of(tm * cells, 8), 3 * cells), :]
    for h in range(2):
        gedge[h] = own3[pl.ds(h * (cols - 1), 3 * rows, stride=cols), :].astype(bf)
    for v in range(2):
        grim[v] = jnp.concatenate(
            [
                own3[j * cells + v * (cells - cols) : j * cells + v * (cells - cols) + cols, :]
                for j in range(3)
            ],
            axis=0,
        ).astype(bf)
    grims = near(grim, gedge, grim_in, gedge_in, gcorner_in, gnear_sem)
    start_all(grims)

    choose_x(range(tmn))

    scatter(1)

    total = None
    for d in range(tmn):
        s = partner(d)
        right_side = jnp.concatenate([ghb[s + 2], ghb[s + 1], ghb[s]], axis=1)
        got = jnp.dot(xt[d], right_side, preferred_element_type=f32)
        total = got if total is None else total + got
    for q in range(9):
        for r in range(rn):
            for a in range(3):
                k = 9 * a + q
                piece = total[q * cwp + r * chunk_pad : q * cwp + (r + 1) * chunk_pad, C * a : C * (a + 1)]
                part[0, r, k * chunk_pad : (k + 1) * chunk_pad, :] = piece
                pstage[0, r, k * chunk_pad : (k + 1) * chunk_pad, :] = piece.astype(bf)
    send_pairs(0)

    scatter(0)

    await_all(grims)
    assemble(gf, 3, grim_in, gedge_in, gcorner_in)
    for j in range(3):
        spread(
            sh.at[j],
            own3[j * cells : (j + 1) * cells, :],
            gf[j, :cols, :],
            gf[j, cols : 2 * cols, :],
            [gf[j, base + 1 : base + 1 + rows, :] for base in (left, right)],
            [[gf[j, base + put : base + put + 1, :] for base in (left, right)] for put in (0, rows + 1)],
        )
        for q in range(9):
            b, e = q // 3, q % 3
            lane = C * (3 * q + 2 - j)
            imc[:, lane : lane + C] = sh[j, 2 - e, cols * (2 - b) : cols * (2 - b) + mp, :].astype(bf)

    total = None
    for q in range(9):
        got = lax.dot_general(
            imc[:, 3 * C * q : 3 * C * (q + 1)], r1[C * q : C * (q + 1), :], NT, preferred_element_type=f32
        )
        total = got if total is None else total + got
    back_ref[...] = flat[1] + total[:cells]

    for tensor, out in ((1, two_ref), (0, one_ref)):
        landed[tensor, col] = stage[tensor, col]
        if zn > 1:
            arrived(landed.at[tensor, : zn - 1], rs_recv.at[tensor])
        got = landed[tensor, 0].astype(f32)
        for z in range(1, zn):
            got = got + landed[tensor, z].astype(f32)
        whole = jnp.concatenate(
            [got[:, ochunk * q : ochunk * (q + 1)] for q in range(zn)], axis=0
        ).reshape(slots, chunk_pad, ochunk)
        out[...] = whole[:27, :chunk, :]

    for which in range(2):
        if tmn > 1:
            sent(gat.at[which, 1:], blk_send.at[which])
        if rn > 1:
            sent(pstage.at[which, : rn - 1], pair_send.at[which])
        if zn > 1:
            sent(stage.at[which, : zn - 1], rs_send.at[which])
    for h in range(2):

        @pl.when(side[h])
        def _():
            sent(edge_in.at[:, h], near_send.at[2 + h])

    for v in range(2):

        @pl.when(vert[v])
        def _():
            sent(rim_in.at[:, v], near_send.at[v])

    for v in range(2):
        for h in range(2):

            @pl.when(jnp.logical_and(vert[v], side[h]))
            def _():
                sent(tip_in.at[:, v, h], near_send.at[4 + 2 * v + h])

    drain_all(grims)


def finish(back_ref, one_ref, two_ref, back_out, one_out, two_out, sem):
    pairs = ((back_ref, back_out), (one_ref, one_out), (two_ref, two_out))
    copies = [pltpu.make_async_copy(src, dst, sem.at[i]) for i, (src, dst) in enumerate(pairs)]
    for copy in copies:
        copy.start()
    for copy in copies:
        copy.wait()


def body(sizes, inputs, cotangent, weight_one, weight_two):
    tmn, rn, zn = sizes
    _, rows, cols, channels = inputs.shape
    cells = rows * cols
    chunk = channels // (tmn * rn)
    chunk_pad = max(16, chunk)
    slots = 28
    lift = (rows + 2) * cols
    mp = -(-cells // 16) * 16
    kp = -(-cells // 128) * 128
    hs = -(-(2 * cols + 2 * (-(-(rows + 2) // 8) * 8)) // 16) * 16
    cwp = rn * chunk_pad
    taps = 27 * chunk_pad
    dims = (tmn, rn, zn, rows, cols, chunk, chunk_pad, slots)
    vmem = pl.BlockSpec(memory_space=pltpu.VMEM)
    bf, f32 = jnp.bfloat16, jnp.float32
    group = slots * chunk_pad // zn
    dma = pltpu.SemaphoreType.DMA
    lifted = lift + mp - cells
    sums = (27, chunk, channels // zn)
    outs = pl.pallas_call(
        functools.partial(kernel, dims),
        out_shape=(
            pltpu.VMEM((cells, channels), f32),
            pltpu.VMEM(sums, f32),
            pltpu.VMEM(sums, f32),
        ),
        in_specs=[pl.BlockSpec(memory_space=pl.ANY)] * 4,
        out_specs=(vmem,) * 3,
        scratch_shapes=[
            pltpu.VMEM((2, tmn, cells, channels), bf),
            pltpu.VMEM((2, cells, channels), f32),
            pltpu.VMEM((tmn, 3, lifted, channels), f32),
            pltpu.VMEM((tmn, 3, lifted, channels), f32),
            pltpu.VMEM((tmn, mp, 9 * channels), bf),
            pltpu.VMEM((tmn, kp, 9 * channels), bf),
            pltpu.VMEM((9 * channels, 3 * channels), bf),
            pltpu.VMEM((3 * channels, 9 * channels), bf),
            pltpu.VMEM((tmn, mp, 3 * channels), f32),
            pltpu.VMEM((tmn, cells, channels), f32),
            pltpu.VMEM(((tmn + 2) * cwp, kp), bf),
            pltpu.VMEM((tmn, 9 * cwp, kp), bf),
            pltpu.VMEM((tmn + 2, kp, channels), bf),
            pltpu.VMEM(((tmn + 2) * cells, channels), f32),
            pltpu.VMEM((3 * cells, channels), f32),
            pltpu.VMEM((3, hs, channels), f32),
            pltpu.VMEM((3, 3, lifted, channels), f32),
            pltpu.VMEM((mp, 27 * channels), bf),
            pltpu.VMEM((2, rn, taps, channels), f32),
            pltpu.VMEM((2, rn, taps, channels), bf),
            pltpu.VMEM((2, rn, taps, channels), bf),
            pltpu.VMEM((slots * chunk_pad, channels), f32),
            pltpu.VMEM((2, zn, group, channels), bf),
            pltpu.VMEM((2, zn, group, channels), bf),
            pltpu.VMEM((2, 2, cols, channels), bf),
            pltpu.VMEM((2, 2, rows, channels), bf),
            pltpu.VMEM((2, 2, 2, 8, channels), bf),
            pltpu.VMEM((2, 2, tmn, cols, channels), bf),
            pltpu.VMEM((2, 2, tmn, rows, channels), bf),
            pltpu.VMEM((2, 2, 2, tmn, 8, channels), bf),
            pltpu.VMEM((2, 3 * cols, channels), bf),
            pltpu.VMEM((2, 3 * rows, channels), bf),
            pltpu.VMEM((2, 3 * cols, channels), bf),
            pltpu.VMEM((2, 3 * rows, channels), bf),
            pltpu.VMEM((2, 2, 3 * rows, channels), bf),
            dma((2,)),
            dma((2,)),
            dma((2,)),
            dma((2, -(-tmn // 2))),
            dma((8,)),
            dma((2, -(-tmn // 2), 8)),
            dma((2, 8)),
            dma((2,)),
            dma((2,)),
            dma((2,)),
            dma((2,)),
        ],
        compiler_params=pltpu.CompilerParams(
            collective_id=0, has_side_effects=True, vmem_limit_bytes=60 * 1024 * 1024
        ),
    )(
        inputs.reshape(cells, channels),
        cotangent.reshape(cells, channels),
        weight_one.reshape(27 * channels, channels),
        weight_two.reshape(27 * channels, channels),
    )
    back, one, two = pl.pallas_call(
        finish,
        out_shape=(
            jax.ShapeDtypeStruct((cells, channels), f32),
            jax.ShapeDtypeStruct(sums, f32),
            jax.ShapeDtypeStruct(sums, f32),
        ),
        in_specs=[vmem] * 3,
        out_specs=(pl.BlockSpec(memory_space=pl.ANY),) * 3,
        scratch_shapes=[dma((3,))],
    )(*[pltpu.with_memory_space_constraint(out, pltpu.VMEM) for out in outs])
    return back.reshape(1, rows, cols, channels), one, two


def solution(mesh):
    sizes = (mesh.shape["tm"], mesh.shape["rows"], mesh.shape["cols"])
    placed = (P("tm", "rows", "cols", None), P("tm", "rows", "cols", None), P(), P())
    return jax.shard_map(
        functools.partial(body, sizes),
        mesh=mesh,
        in_specs=placed,
        out_specs=(
            P("tm", "rows", "cols", None),
            P(None, ("tm", "rows"), "cols"),
            P(None, ("tm", "rows"), "cols"),
        ),
        check_vma=False,
    )
```

```python
import functools

import jax
import jax.numpy as jnp
from jax import lax
from jax.experimental import pallas as pl
from jax.experimental.pallas import tpu as pltpu
from jax.sharding import PartitionSpec as P

MESH = pl.DeviceIdType.MESH
NT = (((1,), (1,)), ((), ()))
C = 128


def kernel(
    dims,
    x_ref,
    c_ref,
    w1_ref,
    w2_ref,
    back_ref,
    one_ref,
    two_ref,
    gat,
    flat,
    sx,
    sc,
    x9,
    c9,
    r1,
    r2,
    conv,
    gate,
    at,
    xt,
    ghb,
    ghf,
    own3,
    gf,
    sh,
    imc,
    part,
    pstage,
    pland,
    pp,
    stage,
    landed,
    rim,
    edge,
    tip,
    rim_in,
    edge_in,
    tip_in,
    grim,
    gedge,
    grim_in,
    gedge_in,
    gcorner_in,
    own_sem,
    w_sem,
    blk_send,
    blk_recv,
    near_send,
    near_recv,
    told,
    gnear_sem,
    pair_send,
    pair_recv,
    rs_send,
    rs_recv,
):
    tmn, rn, zn, rows, cols, chunk, chunk_pad, slots = dims
    cells = rows * cols
    lift = (rows + 2) * cols
    left = 2 * cols
    right = left + -(-(rows + 2) // 8) * 8
    mp, kp = x9.shape[1], c9.shape[1]
    taps = 27 * chunk_pad
    cwp = rn * chunk_pad
    ochunk = C // zn
    bf, f32 = jnp.bfloat16, jnp.float32
    tm, row, col = lax.axis_index("tm"), lax.axis_index("rows"), lax.axis_index("cols")
    vert = (row > 0, row < rn - 1)
    side = (col > 0, col < zn - 1)
    step = (-1, 1)

    def partner(d):
        got, bit = tm, 1
        while bit <= d:
            if d & bit:
                got = got + bit - 2 * bit * lax.rem(got // bit, 2)
            bit *= 2
        return got

    blocks = (x_ref, c_ref)

    def keep(which):
        return pltpu.make_async_copy(blocks[which], gat.at[which, 0], own_sem.at[which])

    keep(0).start()
    keep(1).start()
    barrier = pltpu.get_barrier_semaphore()

    def greet(place):
        pl.semaphore_signal(barrier, inc=1, device_id=place, device_id_type=MESH)

    for d in range(tmn - 1, 0, -1):
        greet((partner(d), row, col))
    for v in range(2):

        @pl.when(vert[v])
        def _():
            for d in range(tmn - 1, -1, -1):
                greet((partner(d), row + step[v], col))

    for h in range(2):

        @pl.when(side[h])
        def _():
            greet((tm, row, col + step[h]))

    for r in range(rn if rn > 2 else 0):

        @pl.when(jnp.logical_or(row - r > 1, r - row > 1))
        def _():
            greet((tm, r, col))

    def load_one(k):
        a, q = k // 9, k % 9
        return pltpu.make_async_copy(
            w1_ref.at[pl.ds(C * k, C), :], r1.at[pl.ds(C * q, C), pl.ds(C * a, C)], w_sem.at[0]
        )

    def load_two(k):
        a, q = k // 9, k % 9
        return pltpu.make_async_copy(
            w2_ref.at[pl.ds(C * k, C), :], r2.at[pl.ds(C * a, C), pl.ds(C * q, C)], w_sem.at[1]
        )

    for k in range(27):
        load_one(k).start()
    for k in range(27):
        load_two(k).start()

    for v in range(2):

        @pl.when(jnp.logical_not(vert[v]))
        def _():
            rim_in[:, v] = jnp.zeros((2, tmn, cols, C), bf)
            tip_in[:, v] = jnp.zeros((2, 2, tmn, 8, C), bf)

    for h in range(2):

        @pl.when(jnp.logical_not(side[h]))
        def _():
            edge_in[:, h] = jnp.zeros((2, tmn, rows, C), bf)
            tip_in[:, :, h] = jnp.zeros((2, 2, tmn, 8, C), bf)

    for which in range(2):
        keep(which).wait()
        flat[which] = gat[which, 0].astype(f32)
        for h in range(2):
            edge[which, h] = flat[which, pl.ds(h * (cols - 1), rows, stride=cols), :].astype(bf)
        for v in range(2):
            line = flat[which, v * (cells - cols) : v * (cells - cols) + cols, :]
            rim[which, v] = line.astype(bf)
            for h in range(2):
                tip[which, v, h] = jnp.broadcast_to(line[h * (cols - 1) : h * (cols - 1) + 1], (8, C)).astype(bf)

    def remote(src, dst, send, recv, place):
        return pltpu.make_async_remote_copy(
            src_ref=src, dst_ref=dst, send_sem=send, recv_sem=recv, device_id=place, device_id_type=MESH
        )

    def near(out_rim, out_edge, in_rim, in_edge, in_corner, sems):
        found = []
        for v in range(2):
            found.append((
                vert[v],
                lambda v=v: remote(
                    out_rim.at[v], in_rim.at[1 - v], sems.at[0, v], sems.at[1, 1 - v], (tm, row + step[v], col)
                ),
                in_rim.at[v],
                sems.at[1, v],
            ))
        for h in range(2):
            found.append((
                side[h],
                lambda h=h: remote(
                    out_edge.at[h], in_edge.at[1 - h], sems.at[0, 2 + h], sems.at[1, 3 - h], (tm, row, col + step[h])
                ),
                in_edge.at[h],
                sems.at[1, 2 + h],
            ))
        for v in range(2):
            for h in range(2):
                found.append((
                    jnp.logical_and(vert[v], side[h]),
                    lambda v=v, h=h: remote(
                        out_edge.at[h],
                        in_corner.at[1 - v, 1 - h],
                        sems.at[0, 4 + 2 * v + h],
                        sems.at[1, 4 + 2 * (1 - v) + 1 - h],
                        (tm, row + step[v], col + step[h]),
                    ),
                    in_corner.at[v, h],
                    sems.at[1, 4 + 2 * v + h],
                ))
        return found

    def start_all(found):
        for cond, copy, _, _ in found:

            @pl.when(cond)
            def _():
                copy().start()

    def drain_all(found):
        for cond, copy, _, _ in found:

            @pl.when(cond)
            def _():
                copy().wait_send()

    def arrived(dst, sem):
        remote(dst, dst, sem, sem, (tm, row, col)).wait_recv()

    def await_all(found):
        for cond, _, dst, sem in found:

            @pl.when(cond)
            def _():
                arrived(dst, sem)

    def assemble(dst, count, in_rim, in_edge, in_corner):
        for v in range(2):

            @pl.when(vert[v])
            def _():
                got = in_rim[v].astype(f32)
                for q in range(count):
                    dst[q, v * cols : (v + 1) * cols, :] = got[q * cols : (q + 1) * cols]

        for h, base in enumerate((left, right)):

            @pl.when(side[h])
            def _():
                got = in_edge[h].astype(f32)
                for q in range(count):
                    dst[q, base + 1 : base + 1 + rows, :] = got[q * rows : (q + 1) * rows]

            for v in range(2):

                @pl.when(jnp.logical_and(vert[v], side[h]))
                def _():
                    got = in_corner[v, h].astype(f32)
                    put = base + v * (rows + 1)
                    for q in range(count):
                        take = q * rows + (1 - v) * (rows - 1)
                        dst[q, put : put + 1, :] = got[take : take + 1]

    def spread(dst, v, top, bottom, sides, tips):
        dst[1, :cols, :] = top
        dst[1, cols : cols + cells, :] = v
        dst[1, cols + cells : lift, :] = bottom
        dst[0, 1 : cols + 1, :] = top
        dst[0, cols + 1 : cols + cells + 1, :] = v
        dst[0, cols + cells + 1 : lift, :] = bottom[: cols - 1]
        dst[0, :1, :] = tips[0][0]
        dst[0, pl.ds(cols, rows, stride=cols), :] = sides[0]
        dst[0, cols + cells : cols + cells + 1, :] = tips[1][0]
        dst[2, : cols - 1, :] = top[1:]
        dst[2, cols - 1 : cols + cells - 1, :] = v
        dst[2, cols + cells - 1 : lift - 1, :] = bottom
        dst[2, cols - 1 : cols, :] = tips[0][1]
        dst[2, pl.ds(2 * cols - 1, rows, stride=cols), :] = sides[1]
        dst[2, lift - 1 : lift, :] = tips[1][1]

    nv = vert[0].astype(jnp.int32) + vert[1].astype(jnp.int32)
    nh = side[0].astype(jnp.int32) + side[1].astype(jnp.int32)
    pl.semaphore_wait(barrier, tmn * (1 + nv) - 1 + nh + rn - 1 - nv)

    def tell():
        for h in range(2):

            @pl.when(side[h])
            def _():
                pl.semaphore_signal(
                    told.at[1 - h], inc=1, device_id=(tm, row, col + step[h]), device_id_type=MESH
                )

    def hear():
        for h in range(2):

            @pl.when(side[h])
            def _():
                pl.semaphore_wait(told.at[h], 1)

    tell()

    groups = [list(range(d, min(d + 2, tmn))) for d in range(0, tmn, 2)]

    def send_block(which, d):
        return remote(
            gat.at[which, 0],
            gat.at[which, d],
            blk_send.at[which],
            blk_recv.at[which, d // 2],
            (partner(d), row, col),
        )

    def send_rim(which, v, d):
        return remote(
            rim.at[which, v],
            rim_in.at[which, 1 - v, d],
            near_send.at[v],
            near_recv.at[which, d // 2, 1 - v],
            (partner(d), row + step[v], col),
        )

    def send_edge(which, h, d):
        return remote(
            edge.at[which, h],
            edge_in.at[which, 1 - h, d],
            near_send.at[2 + h],
            near_recv.at[which, d // 2, 3 - h],
            (partner(d), row, col + step[h]),
        )

    def send_tip(which, v, h, d):
        return remote(
            tip.at[which, v, h],
            tip_in.at[which, 1 - v, 1 - h, d],
            near_send.at[4 + 2 * v + h],
            near_recv.at[which, d // 2, 4 + 2 * (1 - v) + 1 - h],
            (partner(d), row + step[v], col + step[h]),
        )

    def send_near(which, ds):
        for h in range(2):

            @pl.when(side[h])
            def _():
                for d in ds:
                    send_edge(which, h, d).start()

        for v in range(2):

            @pl.when(vert[v])
            def _():
                for d in ds:
                    send_rim(which, v, d).start()

        for v in range(2):
            for h in range(2):

                @pl.when(jnp.logical_and(vert[v], side[h]))
                def _():
                    for d in ds:
                        send_tip(which, v, h, d).start()

    for d in range(1, tmn):
        send_block(0, d).start()
    hear()
    tell()
    for ds in groups:
        send_near(0, ds[::-1])
    for ds in groups:
        send_near(1, ds[::-1])
        for d in ds[::-1]:
            if d:
                send_block(1, d).start()

    def sent(like, sem):
        remote(like, like, sem, sem, (tm, row, col)).wait_send()

    def receive(which, ds, dst):
        g, span = ds[0] // 2, pl.ds(ds[0], len(ds))
        if ds[-1]:
            arrived(gat.at[which, max(ds[0], 1) : ds[-1] + 1], blk_recv.at[which, g])
        for h in range(2):

            @pl.when(side[h])
            def _():
                arrived(edge_in.at[which, h, span], near_recv.at[which, g, 2 + h])

        for v in range(2):

            @pl.when(vert[v])
            def _():
                arrived(rim_in.at[which, v, span], near_recv.at[which, g, v])

        for v in range(2):
            for h in range(2):

                @pl.when(jnp.logical_and(vert[v], side[h]))
                def _():
                    arrived(tip_in.at[which, v, h, span], near_recv.at[which, g, 4 + 2 * v + h])

        for d in ds:
            spread(
                dst.at[d],
                gat[which, d].astype(f32),
                rim_in[which, 0, d].astype(f32),
                rim_in[which, 1, d].astype(f32),
                [edge_in[which, h, d].astype(f32) for h in range(2)],
                [[tip_in[which, v, h, d].astype(f32)[:1] for h in range(2)] for v in range(2)],
            )

    for tail in (sx, sc):
        for s in range(tmn):
            for e in range(3):
                tail[s, e, lift:, :] = jnp.zeros((tail.shape[2] - lift, C), f32)
    for s in range(tmn):
        c9[s, mp:, :] = jnp.zeros((kp - mp, 9 * C), bf)
        xt[s] = jnp.zeros(xt.shape[1:], bf)
    at[...] = jnp.zeros(at.shape, bf)
    for s in range(tmn + 2):
        ghb[s] = jnp.zeros((kp, C), bf)
    ghf[tmn * cells :, :] = jnp.zeros((2 * cells, C), f32)
    gf[...] = jnp.zeros(gf.shape, f32)
    for j in range(3):
        for e in range(3):
            sh[j, e, lift:, :] = jnp.zeros((sh.shape[2] - lift, C), f32)
    pp[taps:, :] = jnp.zeros((pp.shape[0] - taps, C), f32)
    picked = jnp.concatenate(
        [
            jnp.where(
                (lax.broadcasted_iota(jnp.int32, (chunk_pad, C), 1)
                 == (tm * rn + r) * chunk + lax.broadcasted_iota(jnp.int32, (chunk_pad, C), 0))
                & (lax.broadcasted_iota(jnp.int32, (chunk_pad, C), 0) < chunk),
                1.0, 0.0,
            )
            for r in range(rn)
        ],
        axis=0,
    ).astype(bf)

    def tall(src):
        return lax.dot_general(picked, src, NT, preferred_element_type=f32).astype(bf)

    def choose_x(ds):
        for d in ds:
            for e in range(3):
                got = lax.dot_general(picked, sx[d, e].astype(bf), NT, preferred_element_type=f32)
                for b in range(3):
                    q = 3 * b + e
                    xt[d, cwp * q : cwp * (q + 1), :mp] = got[:, cols * b : cols * b + mp].astype(bf)

    for ds in groups:
        receive(0, ds, sx)
        for d in ds:
            for q in range(9):
                b, e = q // 3, q % 3
                x9[d, :, C * q : C * (q + 1)] = sx[d, e, cols * b : cols * b + mp, :].astype(bf)
        if ds[0] == 0:
            pltpu.make_async_copy(r1, r1, w_sem.at[0]).wait()
        got = jnp.dot(
            x9[ds[0] : ds[-1] + 1].reshape(len(ds) * mp, 9 * C), r1[...], preferred_element_type=f32
        )
        for d in ds:
            conv[partner(d)] = got[(d - ds[0]) * mp : (d - ds[0] + 1) * mp]
        if ds is not groups[-1]:
            choose_x(ds)
    for t in range(tmn):
        hidden = conv[t, :cells, 2 * C :]
        for a in range(2):
            s = t - 2 + a
            if s >= 0:
                hidden = hidden + conv[s, :cells, C * a : C * (a + 1)]
        squash = jax.nn.sigmoid(hidden)
        gate[t] = squash * (1.0 + hidden * (1.0 - squash))
        at[(t + 2) * cwp : (t + 3) * cwp, :cells] = tall((hidden * squash).astype(bf))

    def send_pairs(tensor):
        for r in range(rn):

            @pl.when(row != r)
            def _():
                remote(
                    pstage.at[tensor, r],
                    pland.at[tensor, row],
                    pair_send.at[tensor],
                    pair_recv.at[tensor],
                    (tm, r, col),
                ).start()

    group = slots * chunk_pad // zn

    def scatter(tensor):
        pp[:taps, :] = part[tensor, row]
        if rn > 1:
            arrived(pland.at[tensor, : rn - 1], pair_recv.at[tensor])
        for r in range(rn):

            @pl.when(row != r)
            def _():
                pp[:taps, :] += pland[tensor, r].astype(f32)

        for z in range(zn):
            stage[tensor, z] = jnp.concatenate(
                [pp[group * q : group * (q + 1), ochunk * z : ochunk * (z + 1)] for q in range(zn)],
                axis=1,
            ).astype(bf)
        for z in range(zn):

            @pl.when(col != z)
            def _():
                remote(
                    stage.at[tensor, z],
                    landed.at[tensor, col],
                    rs_send.at[tensor],
                    rs_recv.at[tensor],
                    (tm, row, z),
                ).start()

    total = None
    for ds in groups:
        receive(1, ds, sc)
        for d in ds:
            for q in range(9):
                b, e = q // 3, q % 3
                c9[d, :mp, C * q : C * (q + 1)] = sc[d, 2 - e, cols * (2 - b) : cols * (2 - b) + mp, :].astype(bf)
        for d in ds:
            lines = pl.ds(pl.multiple_of(partner(d) * cwp, 16), 3 * cwp)
            got = jnp.dot(at[lines, :], c9[d], preferred_element_type=f32)
            total = got if total is None else total + got
    for a in range(3):
        for r in range(rn):
            for q in range(9):
                k = 9 * a + q
                piece = total[a * cwp + r * chunk_pad : a * cwp + (r + 1) * chunk_pad, C * q : C * (q + 1)]
                part[1, r, k * chunk_pad : (k + 1) * chunk_pad, :] = piece
                pstage[1, r, k * chunk_pad : (k + 1) * chunk_pad, :] = piece.astype(bf)
    send_pairs(1)

    for _ in range(max(0, zn - 4)):
        hear()
        tell()
    hear()

    pltpu.make_async_copy(r2, r2, w_sem.at[1]).wait()
    got = lax.dot_general(
        c9[:, :mp, :].reshape(tmn * mp, 9 * C), r2[...], NT, preferred_element_type=f32
    )
    for d in range(tmn):
        conv[partner(d)] = got[d * mp : (d + 1) * mp]
    scatter(1)

    for t in range(tmn):
        grad = conv[t, :cells, 2 * C :]
        for a in range(2):
            s = t + 2 - a
            if s < tmn:
                grad = grad + conv[s, :cells, C * a : C * (a + 1)]
        grad = (grad * gate[t]).astype(bf)
        ghb[t, :cells, :] = grad
        ghf[t * cells : (t + 1) * cells, :] = grad.astype(f32)

    own3[...] = ghf[pl.ds(pl.multiple_of(tm * cells, 8), 3 * cells), :]
    for h in range(2):
        gedge[h] = own3[pl.ds(h * (cols - 1), 3 * rows, stride=cols), :].astype(bf)
    for v in range(2):
        grim[v] = jnp.concatenate(
            [
                own3[j * cells + v * (cells - cols) : j * cells + v * (cells - cols) + cols, :]
                for j in range(3)
            ],
            axis=0,
        ).astype(bf)
    grims = near(grim, gedge, grim_in, gedge_in, gcorner_in, gnear_sem)
    start_all(grims)

    choose_x(groups[-1])

    total = None
    for d in range(tmn):
        s = partner(d)
        right_side = jnp.concatenate([ghb[s + 2], ghb[s + 1], ghb[s]], axis=1)
        got = jnp.dot(xt[d], right_side, preferred_element_type=f32)
        total = got if total is None else total + got
    for q in range(9):
        for r in range(rn):
            for a in range(3):
                k = 9 * a + q
                piece = total[q * cwp + r * chunk_pad : q * cwp + (r + 1) * chunk_pad, C * a : C * (a + 1)]
                part[0, r, k * chunk_pad : (k + 1) * chunk_pad, :] = piece
                pstage[0, r, k * chunk_pad : (k + 1) * chunk_pad, :] = piece.astype(bf)
    send_pairs(0)

    scatter(0)

    await_all(grims)
    assemble(gf, 3, grim_in, gedge_in, gcorner_in)
    for j in range(3):
        spread(
            sh.at[j],
            own3[j * cells : (j + 1) * cells, :],
            gf[j, :cols, :],
            gf[j, cols : 2 * cols, :],
            [gf[j, base + 1 : base + 1 + rows, :] for base in (left, right)],
            [[gf[j, base + put : base + put + 1, :] for base in (left, right)] for put in (0, rows + 1)],
        )
        for q in range(9):
            b, e = q // 3, q % 3
            lane = C * (3 * q + 2 - j)
            imc[:, lane : lane + C] = sh[j, 2 - e, cols * (2 - b) : cols * (2 - b) + mp, :].astype(bf)

    total = None
    for q in range(9):
        got = lax.dot_general(
            imc[:, 3 * C * q : 3 * C * (q + 1)], r1[C * q : C * (q + 1), :], NT, preferred_element_type=f32
        )
        total = got if total is None else total + got
    back_ref[...] = flat[1] + total[:cells]

    for tensor, out in ((1, two_ref), (0, one_ref)):
        landed[tensor, col] = stage[tensor, col]
        if zn > 1:
            arrived(landed.at[tensor, : zn - 1], rs_recv.at[tensor])
        got = landed[tensor, 0].astype(f32)
        for z in range(1, zn):
            got = got + landed[tensor, z].astype(f32)
        whole = jnp.concatenate(
            [got[:, ochunk * q : ochunk * (q + 1)] for q in range(zn)], axis=0
        ).reshape(slots, chunk_pad, ochunk)
        out[...] = whole[:27, :chunk, :]

    for which in range(2):
        if tmn > 1:
            sent(gat.at[which, 1:], blk_send.at[which])
        if rn > 1:
            sent(pstage.at[which, : rn - 1], pair_send.at[which])
        if zn > 1:
            sent(stage.at[which, : zn - 1], rs_send.at[which])
    for h in range(2):

        @pl.when(side[h])
        def _():
            sent(edge_in.at[:, h], near_send.at[2 + h])

    for v in range(2):

        @pl.when(vert[v])
        def _():
            sent(rim_in.at[:, v], near_send.at[v])

    for v in range(2):
        for h in range(2):

            @pl.when(jnp.logical_and(vert[v], side[h]))
            def _():
                sent(tip_in.at[:, v, h], near_send.at[4 + 2 * v + h])

    drain_all(grims)


def finish(back_ref, one_ref, two_ref, back_out, one_out, two_out, sem):
    pairs = ((back_ref, back_out), (one_ref, one_out), (two_ref, two_out))
    copies = [pltpu.make_async_copy(src, dst, sem.at[i]) for i, (src, dst) in enumerate(pairs)]
    for copy in copies:
        copy.start()
    for copy in copies:
        copy.wait()


def body(sizes, inputs, cotangent, weight_one, weight_two):
    tmn, rn, zn = sizes
    _, rows, cols, channels = inputs.shape
    cells = rows * cols
    chunk = channels // (tmn * rn)
    chunk_pad = max(16, chunk)
    slots = 28
    lift = (rows + 2) * cols
    mp = -(-cells // 16) * 16
    kp = -(-cells // 128) * 128
    hs = -(-(2 * cols + 2 * (-(-(rows + 2) // 8) * 8)) // 16) * 16
    cwp = rn * chunk_pad
    taps = 27 * chunk_pad
    dims = (tmn, rn, zn, rows, cols, chunk, chunk_pad, slots)
    vmem = pl.BlockSpec(memory_space=pltpu.VMEM)
    bf, f32 = jnp.bfloat16, jnp.float32
    group = slots * chunk_pad // zn
    dma = pltpu.SemaphoreType.DMA
    lifted = lift + mp - cells
    sums = (27, chunk, channels // zn)
    outs = pl.pallas_call(
        functools.partial(kernel, dims),
        out_shape=(
            pltpu.VMEM((cells, channels), f32),
            pltpu.VMEM(sums, f32),
            pltpu.VMEM(sums, f32),
        ),
        in_specs=[pl.BlockSpec(memory_space=pl.ANY)] * 4,
        out_specs=(vmem,) * 3,
        scratch_shapes=[
            pltpu.VMEM((2, tmn, cells, channels), bf),
            pltpu.VMEM((2, cells, channels), f32),
            pltpu.VMEM((tmn, 3, lifted, channels), f32),
            pltpu.VMEM((tmn, 3, lifted, channels), f32),
            pltpu.VMEM((tmn, mp, 9 * channels), bf),
            pltpu.VMEM((tmn, kp, 9 * channels), bf),
            pltpu.VMEM((9 * channels, 3 * channels), bf),
            pltpu.VMEM((3 * channels, 9 * channels), bf),
            pltpu.VMEM((tmn, mp, 3 * channels), f32),
            pltpu.VMEM((tmn, cells, channels), f32),
            pltpu.VMEM(((tmn + 2) * cwp, kp), bf),
            pltpu.VMEM((tmn, 9 * cwp, kp), bf),
            pltpu.VMEM((tmn + 2, kp, channels), bf),
            pltpu.VMEM(((tmn + 2) * cells, channels), f32),
            pltpu.VMEM((3 * cells, channels), f32),
            pltpu.VMEM((3, hs, channels), f32),
            pltpu.VMEM((3, 3, lifted, channels), f32),
            pltpu.VMEM((mp, 27 * channels), bf),
            pltpu.VMEM((2, rn, taps, channels), f32),
            pltpu.VMEM((2, rn, taps, channels), bf),
            pltpu.VMEM((2, rn, taps, channels), bf),
            pltpu.VMEM((slots * chunk_pad, channels), f32),
            pltpu.VMEM((2, zn, group, channels), bf),
            pltpu.VMEM((2, zn, group, channels), bf),
            pltpu.VMEM((2, 2, cols, channels), bf),
            pltpu.VMEM((2, 2, rows, channels), bf),
            pltpu.VMEM((2, 2, 2, 8, channels), bf),
            pltpu.VMEM((2, 2, tmn, cols, channels), bf),
            pltpu.VMEM((2, 2, tmn, rows, channels), bf),
            pltpu.VMEM((2, 2, 2, tmn, 8, channels), bf),
            pltpu.VMEM((2, 3 * cols, channels), bf),
            pltpu.VMEM((2, 3 * rows, channels), bf),
            pltpu.VMEM((2, 3 * cols, channels), bf),
            pltpu.VMEM((2, 3 * rows, channels), bf),
            pltpu.VMEM((2, 2, 3 * rows, channels), bf),
            dma((2,)),
            dma((2,)),
            dma((2,)),
            dma((2, -(-tmn // 2))),
            dma((8,)),
            dma((2, -(-tmn // 2), 8)),
            pltpu.SemaphoreType.REGULAR((2,)),
            dma((2, 8)),
            dma((2,)),
            dma((2,)),
            dma((2,)),
            dma((2,)),
        ],
        compiler_params=pltpu.CompilerParams(
            collective_id=0, has_side_effects=True, vmem_limit_bytes=60 * 1024 * 1024
        ),
    )(
        inputs.reshape(cells, channels),
        cotangent.reshape(cells, channels),
        weight_one.reshape(27 * channels, channels),
        weight_two.reshape(27 * channels, channels),
    )
    back, one, two = pl.pallas_call(
        finish,
        out_shape=(
            jax.ShapeDtypeStruct((cells, channels), f32),
            jax.ShapeDtypeStruct(sums, f32),
            jax.ShapeDtypeStruct(sums, f32),
        ),
        in_specs=[vmem] * 3,
        out_specs=(pl.BlockSpec(memory_space=pl.ANY),) * 3,
        scratch_shapes=[dma((3,))],
    )(*[pltpu.with_memory_space_constraint(out, pltpu.VMEM) for out in outs])
    return back.reshape(1, rows, cols, channels), one, two


def solution(mesh):
    sizes = (mesh.shape["tm"], mesh.shape["rows"], mesh.shape["cols"])
    placed = (P("tm", "rows", "cols", None), P("tm", "rows", "cols", None), P(), P())
    return jax.shard_map(
        functools.partial(body, sizes),
        mesh=mesh,
        in_specs=placed,
        out_specs=(
            P("tm", "rows", "cols", None),
            P(None, ("tm", "rows"), "cols"),
            P(None, ("tm", "rows"), "cols"),
        ),
        check_vma=False,
    )
```

```python
import functools

import jax
import jax.numpy as jnp
from jax import lax
from jax.experimental import pallas as pl
from jax.experimental.pallas import tpu as pltpu
from jax.sharding import PartitionSpec as P

MESH = pl.DeviceIdType.MESH
NT = (((1,), (1,)), ((), ()))
C = 128


def kernel(
    dims,
    x_ref,
    c_ref,
    w1_ref,
    w2_ref,
    back_ref,
    one_ref,
    two_ref,
    gat,
    flat,
    sx,
    sc,
    x9,
    c9,
    r1,
    r2,
    conv,
    gate,
    at,
    xt,
    ghb,
    ghf,
    own3,
    gf,
    sh,
    imc,
    part,
    pstage,
    pland,
    pp,
    stage,
    landed,
    rim,
    edge,
    tip,
    rim_in,
    edge_in,
    tip_in,
    grim,
    gedge,
    grim_in,
    gedge_in,
    gcorner_in,
    own_sem,
    w_sem,
    blk_send,
    blk_recv,
    near_send,
    near_recv,
    gnear_sem,
    pair_send,
    pair_recv,
    rs_send,
    rs_recv,
):
    tmn, rn, zn, rows, cols, chunk, chunk_pad, slots = dims
    cells = rows * cols
    lift = (rows + 2) * cols
    left = 2 * cols
    right = left + -(-(rows + 2) // 8) * 8
    mp, kp = x9.shape[1], c9.shape[1]
    taps = 27 * chunk_pad
    cwp = rn * chunk_pad
    ochunk = C // zn
    bf, f32 = jnp.bfloat16, jnp.float32
    tm, row, col = lax.axis_index("tm"), lax.axis_index("rows"), lax.axis_index("cols")
    vert = (row > 0, row < rn - 1)
    side = (col > 0, col < zn - 1)
    step = (-1, 1)

    def partner(d):
        got, bit = tm, 1
        while bit <= d:
            if d & bit:
                got = got + bit - 2 * bit * lax.rem(got // bit, 2)
            bit *= 2
        return got

    blocks = (x_ref, c_ref)

    def keep(which):
        return pltpu.make_async_copy(blocks[which], gat.at[which, 0], own_sem.at[which])

    keep(0).start()
    keep(1).start()
    barrier = pltpu.get_barrier_semaphore()

    def greet(place):
        pl.semaphore_signal(barrier, inc=1, device_id=place, device_id_type=MESH)

    for d in range(tmn - 1, 0, -1):
        greet((partner(d), row, col))
    for v in range(2):

        @pl.when(vert[v])
        def _():
            for d in range(tmn - 1, -1, -1):
                greet((partner(d), row + step[v], col))

    for h in range(2):

        @pl.when(side[h])
        def _():
            for d in range(tmn - 1, -1, -1):
                greet((partner(d), row, col + step[h]))

    for v in range(2):
        for h in range(2):

            @pl.when(jnp.logical_and(vert[v], side[h]))
            def _():
                for d in range(tmn - 1, -1, -1):
                    greet((partner(d), row + step[v], col + step[h]))

    for z in range(zn):

        @pl.when(jnp.logical_or(col - z > 1, z - col > 1))
        def _():
            greet((tm, row, z))

    for r in range(rn if rn > 2 else 0):

        @pl.when(jnp.logical_or(row - r > 1, r - row > 1))
        def _():
            greet((tm, r, col))

    def load_one(k):
        a, q = k // 9, k % 9
        return pltpu.make_async_copy(
            w1_ref.at[pl.ds(C * k, C), :], r1.at[pl.ds(C * q, C), pl.ds(C * a, C)], w_sem.at[0]
        )

    def load_two(k):
        a, q = k // 9, k % 9
        return pltpu.make_async_copy(
            w2_ref.at[pl.ds(C * k, C), :], r2.at[pl.ds(C * a, C), pl.ds(C * q, C)], w_sem.at[1]
        )

    for k in range(27):
        load_one(k).start()
    for k in range(27):
        load_two(k).start()

    for v in range(2):

        @pl.when(jnp.logical_not(vert[v]))
        def _():
            rim_in[:, v] = jnp.zeros((2, tmn, cols, C), bf)
            tip_in[:, v] = jnp.zeros((2, 2, tmn, 8, C), bf)

    for h in range(2):

        @pl.when(jnp.logical_not(side[h]))
        def _():
            edge_in[:, h] = jnp.zeros((2, tmn, rows, C), bf)
            tip_in[:, :, h] = jnp.zeros((2, 2, tmn, 8, C), bf)

    for which in range(2):
        keep(which).wait()
        flat[which] = gat[which, 0].astype(f32)
        for h in range(2):
            edge[which, h] = flat[which, pl.ds(h * (cols - 1), rows, stride=cols), :].astype(bf)
        for v in range(2):
            line = flat[which, v * (cells - cols) : v * (cells - cols) + cols, :]
            rim[which, v] = line.astype(bf)
            for h in range(2):
                tip[which, v, h] = jnp.broadcast_to(line[h * (cols - 1) : h * (cols - 1) + 1], (8, C)).astype(bf)

    def remote(src, dst, send, recv, place):
        return pltpu.make_async_remote_copy(
            src_ref=src, dst_ref=dst, send_sem=send, recv_sem=recv, device_id=place, device_id_type=MESH
        )

    def near(out_rim, out_edge, in_rim, in_edge, in_corner, sems):
        found = []
        for v in range(2):
            found.append((
                vert[v],
                lambda v=v: remote(
                    out_rim.at[v], in_rim.at[1 - v], sems.at[0, v], sems.at[1, 1 - v], (tm, row + step[v], col)
                ),
                in_rim.at[v],
                sems.at[1, v],
            ))
        for h in range(2):
            found.append((
                side[h],
                lambda h=h: remote(
                    out_edge.at[h], in_edge.at[1 - h], sems.at[0, 2 + h], sems.at[1, 3 - h], (tm, row, col + step[h])
                ),
                in_edge.at[h],
                sems.at[1, 2 + h],
            ))
        for v in range(2):
            for h in range(2):
                found.append((
                    jnp.logical_and(vert[v], side[h]),
                    lambda v=v, h=h: remote(
                        out_edge.at[h],
                        in_corner.at[1 - v, 1 - h],
                        sems.at[0, 4 + 2 * v + h],
                        sems.at[1, 4 + 2 * (1 - v) + 1 - h],
                        (tm, row + step[v], col + step[h]),
                    ),
                    in_corner.at[v, h],
                    sems.at[1, 4 + 2 * v + h],
                ))
        return found

    def start_all(found):
        for cond, copy, _, _ in found:

            @pl.when(cond)
            def _():
                copy().start()

    def drain_all(found):
        for cond, copy, _, _ in found:

            @pl.when(cond)
            def _():
                copy().wait_send()

    def arrived(dst, sem):
        remote(dst, dst, sem, sem, (tm, row, col)).wait_recv()

    def await_all(found):
        for cond, _, dst, sem in found:

            @pl.when(cond)
            def _():
                arrived(dst, sem)

    def assemble(dst, count, in_rim, in_edge, in_corner):
        for v in range(2):

            @pl.when(vert[v])
            def _():
                got = in_rim[v].astype(f32)
                for q in range(count):
                    dst[q, v * cols : (v + 1) * cols, :] = got[q * cols : (q + 1) * cols]

        for h, base in enumerate((left, right)):

            @pl.when(side[h])
            def _():
                got = in_edge[h].astype(f32)
                for q in range(count):
                    dst[q, base + 1 : base + 1 + rows, :] = got[q * rows : (q + 1) * rows]

            for v in range(2):

                @pl.when(jnp.logical_and(vert[v], side[h]))
                def _():
                    got = in_corner[v, h].astype(f32)
                    put = base + v * (rows + 1)
                    for q in range(count):
                        take = q * rows + (1 - v) * (rows - 1)
                        dst[q, put : put + 1, :] = got[take : take + 1]

    def spread(dst, v, top, bottom, sides, tips):
        dst[1, :cols, :] = top
        dst[1, cols : cols + cells, :] = v
        dst[1, cols + cells : lift, :] = bottom
        dst[0, 1 : cols + 1, :] = top
        dst[0, cols + 1 : cols + cells + 1, :] = v
        dst[0, cols + cells + 1 : lift, :] = bottom[: cols - 1]
        dst[0, :1, :] = tips[0][0]
        dst[0, pl.ds(cols, rows, stride=cols), :] = sides[0]
        dst[0, cols + cells : cols + cells + 1, :] = tips[1][0]
        dst[2, : cols - 1, :] = top[1:]
        dst[2, cols - 1 : cols + cells - 1, :] = v
        dst[2, cols + cells - 1 : lift - 1, :] = bottom
        dst[2, cols - 1 : cols, :] = tips[0][1]
        dst[2, pl.ds(2 * cols - 1, rows, stride=cols), :] = sides[1]
        dst[2, lift - 1 : lift, :] = tips[1][1]

    nv = vert[0].astype(jnp.int32) + vert[1].astype(jnp.int32)
    nh = side[0].astype(jnp.int32) + side[1].astype(jnp.int32)
    pl.semaphore_wait(barrier, tmn * (1 + nv) * (1 + nh) - 1 + zn - 1 - nh + rn - 1 - nv)

    groups = [list(range(d, min(d + 2, tmn))) for d in range(0, tmn, 2)]

    def send_block(which, d):
        return remote(
            gat.at[which, 0],
            gat.at[which, d],
            blk_send.at[which],
            blk_recv.at[which, d // 2],
            (partner(d), row, col),
        )

    def send_rim(which, v, d):
        return remote(
            rim.at[which, v],
            rim_in.at[which, 1 - v, d],
            near_send.at[v],
            near_recv.at[which, 1 - v],
            (partner(d), row + step[v], col),
        )

    def send_edge(which, h, d):
        return remote(
            edge.at[which, h],
            edge_in.at[which, 1 - h, d],
            near_send.at[2 + h],
            near_recv.at[which, 3 - h],
            (partner(d), row, col + step[h]),
        )

    def send_tip(which, v, h, d):
        return remote(
            tip.at[which, v, h],
            tip_in.at[which, 1 - v, 1 - h, d],
            near_send.at[4 + 2 * v + h],
            near_recv.at[which, 4 + 2 * (1 - v) + 1 - h],
            (partner(d), row + step[v], col + step[h]),
        )

    def send_near(which, ds):
        for h in range(2):

            @pl.when(side[h])
            def _():
                for d in ds:
                    send_edge(which, h, d).start()

        for v in range(2):

            @pl.when(vert[v])
            def _():
                for d in ds:
                    send_rim(which, v, d).start()

        for v in range(2):
            for h in range(2):

                @pl.when(jnp.logical_and(vert[v], side[h]))
                def _():
                    for d in ds:
                        send_tip(which, v, h, d).start()

    for which in range(2):
        send_near(which, range(tmn - 1, -1, -1))
        for ds in groups:
            for d in ds[::-1]:
                if d:
                    send_block(which, d).start()

    def sent(like, sem):
        remote(like, like, sem, sem, (tm, row, col)).wait_send()

    def receive(which, ds, dst):
        g = ds[0] // 2
        if ds[-1]:
            arrived(gat.at[which, max(ds[0], 1) : ds[-1] + 1], blk_recv.at[which, g])
        for h in range(2 if g == 0 else 0):

            @pl.when(side[h])
            def _():
                arrived(edge_in.at[which, h], near_recv.at[which, 2 + h])

        for v in range(2 if g == 0 else 0):

            @pl.when(vert[v])
            def _():
                arrived(rim_in.at[which, v], near_recv.at[which, v])

        for v in range(2 if g == 0 else 0):
            for h in range(2):

                @pl.when(jnp.logical_and(vert[v], side[h]))
                def _():
                    arrived(tip_in.at[which, v, h], near_recv.at[which, 4 + 2 * v + h])

        for d in ds:
            spread(
                dst.at[d],
                gat[which, d].astype(f32),
                rim_in[which, 0, d].astype(f32),
                rim_in[which, 1, d].astype(f32),
                [edge_in[which, h, d].astype(f32) for h in range(2)],
                [[tip_in[which, v, h, d].astype(f32)[:1] for h in range(2)] for v in range(2)],
            )

    for tail in (sx, sc):
        for s in range(tmn):
            for e in range(3):
                tail[s, e, lift:, :] = jnp.zeros((tail.shape[2] - lift, C), f32)
    for s in range(tmn):
        c9[s, mp:, :] = jnp.zeros((kp - mp, 9 * C), bf)
        xt[s] = jnp.zeros(xt.shape[1:], bf)
    at[...] = jnp.zeros(at.shape, bf)
    for s in range(tmn + 2):
        ghb[s] = jnp.zeros((kp, C), bf)
    ghf[tmn * cells :, :] = jnp.zeros((2 * cells, C), f32)
    gf[...] = jnp.zeros(gf.shape, f32)
    for j in range(3):
        for e in range(3):
            sh[j, e, lift:, :] = jnp.zeros((sh.shape[2] - lift, C), f32)
    pp[taps:, :] = jnp.zeros((pp.shape[0] - taps, C), f32)
    picked = jnp.concatenate(
        [
            jnp.where(
                (lax.broadcasted_iota(jnp.int32, (chunk_pad, C), 1)
                 == (tm * rn + r) * chunk + lax.broadcasted_iota(jnp.int32, (chunk_pad, C), 0))
                & (lax.broadcasted_iota(jnp.int32, (chunk_pad, C), 0) < chunk),
                1.0, 0.0,
            )
            for r in range(rn)
        ],
        axis=0,
    ).astype(bf)

    def tall(src):
        return lax.dot_general(picked, src, NT, preferred_element_type=f32).astype(bf)

    def choose_x(ds):
        for d in ds:
            for e in range(3):
                got = lax.dot_general(picked, sx[d, e].astype(bf), NT, preferred_element_type=f32)
                for b in range(3):
                    q = 3 * b + e
                    xt[d, cwp * q : cwp * (q + 1), :mp] = got[:, cols * b : cols * b + mp].astype(bf)

    for ds in groups:
        receive(0, ds, sx)
        for d in ds:
            for q in range(9):
                b, e = q // 3, q % 3
                x9[d, :, C * q : C * (q + 1)] = sx[d, e, cols * b : cols * b + mp, :].astype(bf)
        if ds[0] == 0:
            pltpu.make_async_copy(r1, r1, w_sem.at[0]).wait()
        got = jnp.dot(
            x9[ds[0] : ds[-1] + 1].reshape(len(ds) * mp, 9 * C), r1[...], preferred_element_type=f32
        )
        for d in ds:
            conv[partner(d)] = got[(d - ds[0]) * mp : (d - ds[0] + 1) * mp]
        if ds is not groups[-1]:
            choose_x(ds)
    for t in range(tmn):
        hidden = conv[t, :cells, 2 * C :]
        for a in range(2):
            s = t - 2 + a
            if s >= 0:
                hidden = hidden + conv[s, :cells, C * a : C * (a + 1)]
        squash = jax.nn.sigmoid(hidden)
        gate[t] = squash * (1.0 + hidden * (1.0 - squash))
        at[(t + 2) * cwp : (t + 3) * cwp, :cells] = tall((hidden * squash).astype(bf))

    def send_pairs(tensor):
        for r in range(rn):

            @pl.when(row != r)
            def _():
                remote(
                    pstage.at[tensor, r],
                    pland.at[tensor, row],
                    pair_send.at[tensor],
                    pair_recv.at[tensor],
                    (tm, r, col),
                ).start()

    group = slots * chunk_pad // zn

    def scatter(tensor):
        pp[:taps, :] = part[tensor, row]
        if rn > 1:
            arrived(pland.at[tensor, : rn - 1], pair_recv.at[tensor])
        for r in range(rn):

            @pl.when(row != r)
            def _():
                pp[:taps, :] += pland[tensor, r].astype(f32)

        for z in range(zn):
            stage[tensor, z] = jnp.concatenate(
                [pp[group * q : group * (q + 1), ochunk * z : ochunk * (z + 1)] for q in range(zn)],
                axis=1,
            ).astype(bf)

            @pl.when(col != z)
            def _():
                remote(
                    stage.at[tensor, z],
                    landed.at[tensor, col],
                    rs_send.at[tensor],
                    rs_recv.at[tensor],
                    (tm, row, z),
                ).start()

    total = None
    for ds in groups:
        receive(1, ds, sc)
        for d in ds:
            for q in range(9):
                b, e = q // 3, q % 3
                c9[d, :mp, C * q : C * (q + 1)] = sc[d, 2 - e, cols * (2 - b) : cols * (2 - b) + mp, :].astype(bf)
        for d in ds:
            lines = pl.ds(pl.multiple_of(partner(d) * cwp, 16), 3 * cwp)
            got = jnp.dot(at[lines, :mp], c9[d, :mp], preferred_element_type=f32)
            total = got if total is None else total + got
    for a in range(3):
        for r in range(rn):
            for q in range(9):
                k = 9 * a + q
                piece = total[a * cwp + r * chunk_pad : a * cwp + (r + 1) * chunk_pad, C * q : C * (q + 1)]
                part[1, r, k * chunk_pad : (k + 1) * chunk_pad, :] = piece
                pstage[1, r, k * chunk_pad : (k + 1) * chunk_pad, :] = piece.astype(bf)
    send_pairs(1)

    pltpu.make_async_copy(r2, r2, w_sem.at[1]).wait()
    got = lax.dot_general(
        c9[:, :mp, :].reshape(tmn * mp, 9 * C), r2[...], NT, preferred_element_type=f32
    )
    for d in range(tmn):
        conv[partner(d)] = got[d * mp : (d + 1) * mp]
    for t in range(tmn):
        grad = conv[t, :cells, 2 * C :]
        for a in range(2):
            s = t + 2 - a
            if s < tmn:
                grad = grad + conv[s, :cells, C * a : C * (a + 1)]
        grad = (grad * gate[t]).astype(bf)
        ghb[t, :cells, :] = grad
        ghf[t * cells : (t + 1) * cells, :] = grad.astype(f32)

    own3[...] = ghf[pl.ds(pl.multiple_of(tm * cells, 8), 3 * cells), :]
    for h in range(2):
        gedge[h] = own3[pl.ds(h * (cols - 1), 3 * rows, stride=cols), :].astype(bf)
    for v in range(2):
        grim[v] = jnp.concatenate(
            [
                own3[j * cells + v * (cells - cols) : j * cells + v * (cells - cols) + cols, :]
                for j in range(3)
            ],
            axis=0,
        ).astype(bf)
    grims = near(grim, gedge, grim_in, gedge_in, gcorner_in, gnear_sem)
    start_all(grims)

    scatter(1)

    choose_x(groups[-1])

    total = None
    for d in range(tmn):
        s = partner(d)
        right_side = jnp.concatenate([ghb[s + 2, :mp], ghb[s + 1, :mp], ghb[s, :mp]], axis=1)
        got = jnp.dot(xt[d, :, :mp], right_side, preferred_element_type=f32)
        total = got if total is None else total + got
    for q in range(9):
        for r in range(rn):
            for a in range(3):
                k = 9 * a + q
                piece = total[q * cwp + r * chunk_pad : q * cwp + (r + 1) * chunk_pad, C * a : C * (a + 1)]
                part[0, r, k * chunk_pad : (k + 1) * chunk_pad, :] = piece
                pstage[0, r, k * chunk_pad : (k + 1) * chunk_pad, :] = piece.astype(bf)
    send_pairs(0)

    scatter(0)

    await_all(grims)
    assemble(gf, 3, grim_in, gedge_in, gcorner_in)
    for j in range(3):
        spread(
            sh.at[j],
            own3[j * cells : (j + 1) * cells, :],
            gf[j, :cols, :],
            gf[j, cols : 2 * cols, :],
            [gf[j, base + 1 : base + 1 + rows, :] for base in (left, right)],
            [[gf[j, base + put : base + put + 1, :] for base in (left, right)] for put in (0, rows + 1)],
        )
        for q in range(9):
            b, e = q // 3, q % 3
            lane = C * (3 * q + 2 - j)
            imc[:, lane : lane + C] = sh[j, 2 - e, cols * (2 - b) : cols * (2 - b) + mp, :].astype(bf)

    total = None
    for q in range(9):
        got = lax.dot_general(
            imc[:, 3 * C * q : 3 * C * (q + 1)], r1[C * q : C * (q + 1), :], NT, preferred_element_type=f32
        )
        total = got if total is None else total + got
    back_ref[...] = flat[1] + total[:cells]

    for tensor, out in ((1, two_ref), (0, one_ref)):
        landed[tensor, col] = stage[tensor, col]
        if zn > 1:
            arrived(landed.at[tensor, : zn - 1], rs_recv.at[tensor])
        got = landed[tensor, 0].astype(f32)
        for z in range(1, zn):
            got = got + landed[tensor, z].astype(f32)
        whole = jnp.concatenate(
            [got[:, ochunk * q : ochunk * (q + 1)] for q in range(zn)], axis=0
        ).reshape(slots, chunk_pad, ochunk)
        out[...] = whole[:27, :chunk, :]

    for which in range(2):
        if tmn > 1:
            sent(gat.at[which, 1:], blk_send.at[which])
        if rn > 1:
            sent(pstage.at[which, : rn - 1], pair_send.at[which])
        if zn > 1:
            sent(stage.at[which, : zn - 1], rs_send.at[which])
    for h in range(2):

        @pl.when(side[h])
        def _():
            sent(edge_in.at[:, h], near_send.at[2 + h])

    for v in range(2):

        @pl.when(vert[v])
        def _():
            sent(rim_in.at[:, v], near_send.at[v])

    for v in range(2):
        for h in range(2):

            @pl.when(jnp.logical_and(vert[v], side[h]))
            def _():
                sent(tip_in.at[:, v, h], near_send.at[4 + 2 * v + h])

    drain_all(grims)


def finish(back_ref, one_ref, two_ref, back_out, one_out, two_out, sem):
    pairs = ((back_ref, back_out), (one_ref, one_out), (two_ref, two_out))
    copies = [pltpu.make_async_copy(src, dst, sem.at[i]) for i, (src, dst) in enumerate(pairs)]
    for copy in copies:
        copy.start()
    for copy in copies:
        copy.wait()


def body(sizes, inputs, cotangent, weight_one, weight_two):
    tmn, rn, zn = sizes
    _, rows, cols, channels = inputs.shape
    cells = rows * cols
    chunk = channels // (tmn * rn)
    chunk_pad = max(16, chunk)
    slots = 28
    lift = (rows + 2) * cols
    mp = -(-cells // 16) * 16
    kp = -(-cells // 128) * 128
    hs = -(-(2 * cols + 2 * (-(-(rows + 2) // 8) * 8)) // 16) * 16
    cwp = rn * chunk_pad
    taps = 27 * chunk_pad
    dims = (tmn, rn, zn, rows, cols, chunk, chunk_pad, slots)
    vmem = pl.BlockSpec(memory_space=pltpu.VMEM)
    bf, f32 = jnp.bfloat16, jnp.float32
    group = slots * chunk_pad // zn
    dma = pltpu.SemaphoreType.DMA
    lifted = lift + mp - cells
    sums = (27, chunk, channels // zn)
    outs = pl.pallas_call(
        functools.partial(kernel, dims),
        out_shape=(
            pltpu.VMEM((cells, channels), f32),
            pltpu.VMEM(sums, f32),
            pltpu.VMEM(sums, f32),
        ),
        in_specs=[pl.BlockSpec(memory_space=pl.ANY)] * 4,
        out_specs=(vmem,) * 3,
        scratch_shapes=[
            pltpu.VMEM((2, tmn, cells, channels), bf),
            pltpu.VMEM((2, cells, channels), f32),
            pltpu.VMEM((tmn, 3, lifted, channels), f32),
            pltpu.VMEM((tmn, 3, lifted, channels), f32),
            pltpu.VMEM((tmn, mp, 9 * channels), bf),
            pltpu.VMEM((tmn, kp, 9 * channels), bf),
            pltpu.VMEM((9 * channels, 3 * channels), bf),
            pltpu.VMEM((3 * channels, 9 * channels), bf),
            pltpu.VMEM((tmn, mp, 3 * channels), f32),
            pltpu.VMEM((tmn, cells, channels), f32),
            pltpu.VMEM(((tmn + 2) * cwp, kp), bf),
            pltpu.VMEM((tmn, 9 * cwp, kp), bf),
            pltpu.VMEM((tmn + 2, kp, channels), bf),
            pltpu.VMEM(((tmn + 2) * cells, channels), f32),
            pltpu.VMEM((3 * cells, channels), f32),
            pltpu.VMEM((3, hs, channels), f32),
            pltpu.VMEM((3, 3, lifted, channels), f32),
            pltpu.VMEM((mp, 27 * channels), bf),
            pltpu.VMEM((2, rn, taps, channels), f32),
            pltpu.VMEM((2, rn, taps, channels), bf),
            pltpu.VMEM((2, rn, taps, channels), bf),
            pltpu.VMEM((slots * chunk_pad, channels), f32),
            pltpu.VMEM((2, zn, group, channels), bf),
            pltpu.VMEM((2, zn, group, channels), bf),
            pltpu.VMEM((2, 2, cols, channels), bf),
            pltpu.VMEM((2, 2, rows, channels), bf),
            pltpu.VMEM((2, 2, 2, 8, channels), bf),
            pltpu.VMEM((2, 2, tmn, cols, channels), bf),
            pltpu.VMEM((2, 2, tmn, rows, channels), bf),
            pltpu.VMEM((2, 2, 2, tmn, 8, channels), bf),
            pltpu.VMEM((2, 3 * cols, channels), bf),
            pltpu.VMEM((2, 3 * rows, channels), bf),
            pltpu.VMEM((2, 3 * cols, channels), bf),
            pltpu.VMEM((2, 3 * rows, channels), bf),
            pltpu.VMEM((2, 2, 3 * rows, channels), bf),
            dma((2,)),
            dma((2,)),
            dma((2,)),
            dma((2, -(-tmn // 2))),
            dma((8,)),
            dma((2, 8)),
            dma((2, 8)),
            dma((2,)),
            dma((2,)),
            dma((2,)),
            dma((2,)),
        ],
        compiler_params=pltpu.CompilerParams(
            collective_id=0, has_side_effects=True, vmem_limit_bytes=60 * 1024 * 1024
        ),
    )(
        inputs.reshape(cells, channels),
        cotangent.reshape(cells, channels),
        weight_one.reshape(27 * channels, channels),
        weight_two.reshape(27 * channels, channels),
    )
    back, one, two = pl.pallas_call(
        finish,
        out_shape=(
            jax.ShapeDtypeStruct((cells, channels), f32),
            jax.ShapeDtypeStruct(sums, f32),
            jax.ShapeDtypeStruct(sums, f32),
        ),
        in_specs=[vmem] * 3,
        out_specs=(pl.BlockSpec(memory_space=pl.ANY),) * 3,
        scratch_shapes=[dma((3,))],
    )(*[pltpu.with_memory_space_constraint(out, pltpu.VMEM) for out in outs])
    return back.reshape(1, rows, cols, channels), one, two


def solution(mesh):
    sizes = (mesh.shape["tm"], mesh.shape["rows"], mesh.shape["cols"])
    placed = (P("tm", "rows", "cols", None), P("tm", "rows", "cols", None), P(), P())
    return jax.shard_map(
        functools.partial(body, sizes),
        mesh=mesh,
        in_specs=placed,
        out_specs=(
            P("tm", "rows", "cols", None),
            P(None, ("tm", "rows"), "cols"),
            P(None, ("tm", "rows"), "cols"),
        ),
        check_vma=False,
    )
```

```python
import functools

import jax
import jax.numpy as jnp
from jax import lax
from jax.experimental import pallas as pl
from jax.experimental.pallas import tpu as pltpu
from jax.sharding import PartitionSpec as P

MESH = pl.DeviceIdType.MESH
NT = (((1,), (1,)), ((), ()))
C = 128


def kernel(
    dims,
    x_ref,
    c_ref,
    w1_ref,
    w2_ref,
    back_ref,
    one_ref,
    two_ref,
    gat,
    flat,
    sx,
    sc,
    x9,
    c9,
    r1,
    r2,
    conv,
    gate,
    at,
    xt,
    ghb,
    ghf,
    own3,
    gf,
    sh,
    imc,
    part,
    pstage,
    pland,
    pp,
    stage,
    landed,
    rim,
    edge,
    tip,
    rim_in,
    edge_in,
    tip_in,
    grim,
    gedge,
    grim_in,
    gedge_in,
    gcorner_in,
    own_sem,
    w_sem,
    blk_send,
    blk_recv,
    near_send,
    near_recv,
    gnear_sem,
    pair_send,
    pair_recv,
    rs_send,
    rs_recv,
):
    tmn, rn, zn, rows, cols, chunk, chunk_pad, slots = dims
    cells = rows * cols
    lift = (rows + 2) * cols
    left = 2 * cols
    right = left + -(-(rows + 2) // 8) * 8
    mp, kp = x9.shape[1], c9.shape[1]
    taps = 27 * chunk_pad
    cwp = rn * chunk_pad
    ochunk = C // zn
    bf, f32 = jnp.bfloat16, jnp.float32
    tm, row, col = lax.axis_index("tm"), lax.axis_index("rows"), lax.axis_index("cols")
    vert = (row > 0, row < rn - 1)
    side = (col > 0, col < zn - 1)
    step = (-1, 1)

    def partner(d):
        got, bit = tm, 1
        while bit <= d:
            if d & bit:
                got = got + bit - 2 * bit * lax.rem(got // bit, 2)
            bit *= 2
        return got

    blocks = (x_ref, c_ref)

    def keep(which):
        return pltpu.make_async_copy(blocks[which], gat.at[which, 0], own_sem.at[which])

    keep(0).start()
    keep(1).start()
    barrier = pltpu.get_barrier_semaphore()

    def greet(place):
        pl.semaphore_signal(barrier, inc=1, device_id=place, device_id_type=MESH)

    for d in range(tmn - 1, 0, -1):
        greet((partner(d), row, col))
    for v in range(2):

        @pl.when(vert[v])
        def _():
            for d in range(tmn - 1, -1, -1):
                greet((partner(d), row + step[v], col))

    for h in range(2):

        @pl.when(side[h])
        def _():
            for d in range(tmn - 1, -1, -1):
                greet((partner(d), row, col + step[h]))

    for v in range(2):
        for h in range(2):

            @pl.when(jnp.logical_and(vert[v], side[h]))
            def _():
                for d in range(tmn - 1, -1, -1):
                    greet((partner(d), row + step[v], col + step[h]))

    for z in range(zn):

        @pl.when(jnp.logical_or(col - z > 1, z - col > 1))
        def _():
            greet((tm, row, z))

    for r in range(rn if rn > 2 else 0):

        @pl.when(jnp.logical_or(row - r > 1, r - row > 1))
        def _():
            greet((tm, r, col))

    def load_one(k):
        a, q = k // 9, k % 9
        return pltpu.make_async_copy(
            w1_ref.at[pl.ds(C * k, C), :], r1.at[pl.ds(C * q, C), pl.ds(C * a, C)], w_sem.at[0]
        )

    def load_two(k):
        a, q = k // 9, k % 9
        return pltpu.make_async_copy(
            w2_ref.at[pl.ds(C * k, C), :], r2.at[pl.ds(C * a, C), pl.ds(C * q, C)], w_sem.at[1]
        )

    for k in range(27):
        load_one(k).start()
    for k in range(27):
        load_two(k).start()

    for v in range(2):

        @pl.when(jnp.logical_not(vert[v]))
        def _():
            rim_in[:, v] = jnp.zeros((2, tmn, cols, C), bf)
            tip_in[:, v] = jnp.zeros((2, 2, tmn, 8, C), bf)

    for h in range(2):

        @pl.when(jnp.logical_not(side[h]))
        def _():
            edge_in[:, h] = jnp.zeros((2, tmn, rows, C), bf)
            tip_in[:, :, h] = jnp.zeros((2, 2, tmn, 8, C), bf)

    for which in range(2):
        keep(which).wait()
        flat[which] = gat[which, 0].astype(f32)
        for h in range(2):
            edge[which, h] = flat[which, pl.ds(h * (cols - 1), rows, stride=cols), :].astype(bf)
        for v in range(2):
            line = flat[which, v * (cells - cols) : v * (cells - cols) + cols, :]
            rim[which, v] = line.astype(bf)
            for h in range(2):
                tip[which, v, h] = jnp.broadcast_to(line[h * (cols - 1) : h * (cols - 1) + 1], (8, C)).astype(bf)

    def remote(src, dst, send, recv, place):
        return pltpu.make_async_remote_copy(
            src_ref=src, dst_ref=dst, send_sem=send, recv_sem=recv, device_id=place, device_id_type=MESH
        )

    def near(out_rim, out_edge, in_rim, in_edge, in_corner, sems):
        found = []
        for v in range(2):
            found.append((
                vert[v],
                lambda v=v: remote(
                    out_rim.at[v], in_rim.at[1 - v], sems.at[0, v], sems.at[1, 1 - v], (tm, row + step[v], col)
                ),
                in_rim.at[v],
                sems.at[1, v],
            ))
        for h in range(2):
            found.append((
                side[h],
                lambda h=h: remote(
                    out_edge.at[h], in_edge.at[1 - h], sems.at[0, 2 + h], sems.at[1, 3 - h], (tm, row, col + step[h])
                ),
                in_edge.at[h],
                sems.at[1, 2 + h],
            ))
        for v in range(2):
            for h in range(2):
                found.append((
                    jnp.logical_and(vert[v], side[h]),
                    lambda v=v, h=h: remote(
                        out_edge.at[h],
                        in_corner.at[1 - v, 1 - h],
                        sems.at[0, 4 + 2 * v + h],
                        sems.at[1, 4 + 2 * (1 - v) + 1 - h],
                        (tm, row + step[v], col + step[h]),
                    ),
                    in_corner.at[v, h],
                    sems.at[1, 4 + 2 * v + h],
                ))
        return found

    def start_all(found):
        for cond, copy, _, _ in found:

            @pl.when(cond)
            def _():
                copy().start()

    def drain_all(found):
        for cond, copy, _, _ in found:

            @pl.when(cond)
            def _():
                copy().wait_send()

    def arrived(dst, sem):
        remote(dst, dst, sem, sem, (tm, row, col)).wait_recv()

    def await_all(found):
        for cond, _, dst, sem in found:

            @pl.when(cond)
            def _():
                arrived(dst, sem)

    def assemble(dst, count, in_rim, in_edge, in_corner):
        for v in range(2):

            @pl.when(vert[v])
            def _():
                got = in_rim[v].astype(f32)
                for q in range(count):
                    dst[q, v * cols : (v + 1) * cols, :] = got[q * cols : (q + 1) * cols]

        for h, base in enumerate((left, right)):

            @pl.when(side[h])
            def _():
                got = in_edge[h].astype(f32)
                for q in range(count):
                    dst[q, base + 1 : base + 1 + rows, :] = got[q * rows : (q + 1) * rows]

            for v in range(2):

                @pl.when(jnp.logical_and(vert[v], side[h]))
                def _():
                    got = in_corner[v, h].astype(f32)
                    put = base + v * (rows + 1)
                    for q in range(count):
                        take = q * rows + (1 - v) * (rows - 1)
                        dst[q, put : put + 1, :] = got[take : take + 1]

    def spread(dst, v, top, bottom, sides, tips):
        dst[1, :cols, :] = top
        dst[1, cols : cols + cells, :] = v
        dst[1, cols + cells : lift, :] = bottom
        dst[0, 1 : cols + 1, :] = top
        dst[0, cols + 1 : cols + cells + 1, :] = v
        dst[0, cols + cells + 1 : lift, :] = bottom[: cols - 1]
        dst[0, :1, :] = tips[0][0]
        dst[0, pl.ds(cols, rows, stride=cols), :] = sides[0]
        dst[0, cols + cells : cols + cells + 1, :] = tips[1][0]
        dst[2, : cols - 1, :] = top[1:]
        dst[2, cols - 1 : cols + cells - 1, :] = v
        dst[2, cols + cells - 1 : lift - 1, :] = bottom
        dst[2, cols - 1 : cols, :] = tips[0][1]
        dst[2, pl.ds(2 * cols - 1, rows, stride=cols), :] = sides[1]
        dst[2, lift - 1 : lift, :] = tips[1][1]

    nv = vert[0].astype(jnp.int32) + vert[1].astype(jnp.int32)
    nh = side[0].astype(jnp.int32) + side[1].astype(jnp.int32)
    pl.semaphore_wait(barrier, tmn * (1 + nv) * (1 + nh) - 1 + zn - 1 - nh + rn - 1 - nv)

    groups = [list(range(d, min(d + 2, tmn))) for d in range(0, tmn, 2)]

    def send_block(which, d):
        return remote(
            gat.at[which, 0],
            gat.at[which, d],
            blk_send.at[which],
            blk_recv.at[which, d // 2],
            (partner(d), row, col),
        )

    def send_rim(which, v, d):
        return remote(
            rim.at[which, v],
            rim_in.at[which, 1 - v, d],
            near_send.at[v],
            near_recv.at[which, 1 - v],
            (partner(d), row + step[v], col),
        )

    def send_edge(which, h, d):
        return remote(
            edge.at[which, h],
            edge_in.at[which, 1 - h, d],
            near_send.at[2 + h],
            near_recv.at[which, 3 - h],
            (partner(d), row, col + step[h]),
        )

    def send_tip(which, v, h, d):
        return remote(
            tip.at[which, v, h],
            tip_in.at[which, 1 - v, 1 - h, d],
            near_send.at[4 + 2 * v + h],
            near_recv.at[which, 4 + 2 * (1 - v) + 1 - h],
            (partner(d), row + step[v], col + step[h]),
        )

    def send_near(which, ds):
        for h in range(2):

            @pl.when(side[h])
            def _():
                for d in ds:
                    send_edge(which, h, d).start()

        for v in range(2):

            @pl.when(vert[v])
            def _():
                for d in ds:
                    send_rim(which, v, d).start()

        for v in range(2):
            for h in range(2):

                @pl.when(jnp.logical_and(vert[v], side[h]))
                def _():
                    for d in ds:
                        send_tip(which, v, h, d).start()

    for which in range(2):
        send_near(which, range(tmn - 1, -1, -1))
        for ds in groups:
            for d in ds[::-1]:
                if d:
                    send_block(which, d).start()

    def sent(like, sem):
        remote(like, like, sem, sem, (tm, row, col)).wait_send()

    def receive(which, ds, dst):
        g = ds[0] // 2
        if ds[-1]:
            arrived(gat.at[which, max(ds[0], 1) : ds[-1] + 1], blk_recv.at[which, g])
        for h in range(2 if g == 0 else 0):

            @pl.when(side[h])
            def _():
                arrived(edge_in.at[which, h], near_recv.at[which, 2 + h])

        for v in range(2 if g == 0 else 0):

            @pl.when(vert[v])
            def _():
                arrived(rim_in.at[which, v], near_recv.at[which, v])

        for v in range(2 if g == 0 else 0):
            for h in range(2):

                @pl.when(jnp.logical_and(vert[v], side[h]))
                def _():
                    arrived(tip_in.at[which, v, h], near_recv.at[which, 4 + 2 * v + h])

        for d in ds:
            spread(
                dst.at[d],
                gat[which, d].astype(f32),
                rim_in[which, 0, d].astype(f32),
                rim_in[which, 1, d].astype(f32),
                [edge_in[which, h, d].astype(f32) for h in range(2)],
                [[tip_in[which, v, h, d].astype(f32)[:1] for h in range(2)] for v in range(2)],
            )

    for tail in (sx, sc):
        for s in range(tmn):
            for e in range(3):
                tail[s, e, lift:, :] = jnp.zeros((tail.shape[2] - lift, C), f32)
    for s in range(tmn):
        c9[s, mp:, :] = jnp.zeros((kp - mp, 9 * C), bf)
        xt[s] = jnp.zeros(xt.shape[1:], bf)
    at[...] = jnp.zeros(at.shape, bf)
    for s in range(tmn + 2):
        ghb[s] = jnp.zeros((kp, C), bf)
    ghf[tmn * cells :, :] = jnp.zeros((2 * cells, C), f32)
    gf[...] = jnp.zeros(gf.shape, f32)
    for j in range(3):
        for e in range(3):
            sh[j, e, lift:, :] = jnp.zeros((sh.shape[2] - lift, C), f32)
    pp[taps:, :] = jnp.zeros((pp.shape[0] - taps, C), f32)
    picked = jnp.concatenate(
        [
            jnp.where(
                (lax.broadcasted_iota(jnp.int32, (chunk_pad, C), 1)
                 == (tm * rn + r) * chunk + lax.broadcasted_iota(jnp.int32, (chunk_pad, C), 0))
                & (lax.broadcasted_iota(jnp.int32, (chunk_pad, C), 0) < chunk),
                1.0, 0.0,
            )
            for r in range(rn)
        ],
        axis=0,
    ).astype(bf)

    def tall(src):
        return lax.dot_general(picked, src, NT, preferred_element_type=f32).astype(bf)

    def choose_x(ds):
        for d in ds:
            for e in range(3):
                got = lax.dot_general(picked, sx[d, e].astype(bf), NT, preferred_element_type=f32)
                for b in range(3):
                    q = 3 * b + e
                    xt[d, cwp * q : cwp * (q + 1), :mp] = got[:, cols * b : cols * b + mp].astype(bf)

    for ds in groups:
        receive(0, ds, sx)
        for d in ds:
            for q in range(9):
                b, e = q // 3, q % 3
                x9[d, :, C * q : C * (q + 1)] = sx[d, e, cols * b : cols * b + mp, :].astype(bf)
        if ds[0] == 0:
            pltpu.make_async_copy(r1, r1, w_sem.at[0]).wait()
        got = jnp.dot(
            x9[ds[0] : ds[-1] + 1].reshape(len(ds) * mp, 9 * C), r1[...], preferred_element_type=f32
        )
        for d in ds:
            conv[partner(d)] = got[(d - ds[0]) * mp : (d - ds[0] + 1) * mp]
    for t in range(tmn):
        hidden = conv[t, :cells, 2 * C :]
        for a in range(2):
            s = t - 2 + a
            if s >= 0:
                hidden = hidden + conv[s, :cells, C * a : C * (a + 1)]
        squash = jax.nn.sigmoid(hidden)
        gate[t] = squash * (1.0 + hidden * (1.0 - squash))
        at[(t + 2) * cwp : (t + 3) * cwp, :cells] = tall((hidden * squash).astype(bf))

    def send_pairs(tensor, lo, hi):
        for d in range(1, rn):
            r = lax.rem(row + d, rn)
            remote(
                pstage.at[tensor, r, lo:hi],
                pland.at[tensor, row, lo:hi],
                pair_send.at[tensor],
                pair_recv.at[tensor],
                (tm, r, col),
            ).start()

    group = slots * chunk_pad // zn

    def scatter(tensor):
        if rn > 1:
            arrived(pland.at[tensor, : rn - 1], pair_recv.at[tensor])
        got = part[tensor, row]
        for d in range(1, rn):
            got = got + pland[tensor, lax.rem(row + d, rn)].astype(f32)
        pp[:taps, :] = got
        for z in range(zn):
            stage[tensor, z] = jnp.concatenate(
                [pp[group * q : group * (q + 1), ochunk * z : ochunk * (z + 1)] for q in range(zn)],
                axis=1,
            ).astype(bf)
        for d in range(1, zn):
            z = lax.rem(col + d, zn)
            remote(
                stage.at[tensor, z],
                landed.at[tensor, col],
                rs_send.at[tensor],
                rs_recv.at[tensor],
                (tm, row, z),
            ).start()

    total = None
    for ds in groups:
        receive(1, ds, sc)
        for d in ds:
            for q in range(9):
                b, e = q // 3, q % 3
                c9[d, :mp, C * q : C * (q + 1)] = sc[d, 2 - e, cols * (2 - b) : cols * (2 - b) + mp, :].astype(bf)
        for d in ds:
            lines = pl.ds(pl.multiple_of(partner(d) * cwp, 16), 3 * cwp)
            got = jnp.dot(at[lines, :mp], c9[d, :mp], preferred_element_type=f32)
            total = got if total is None else total + got
    for a in range(3):
        for r in range(rn):
            for q in range(9):
                k = 9 * a + q
                piece = total[a * cwp + r * chunk_pad : a * cwp + (r + 1) * chunk_pad, C * q : C * (q + 1)]
                part[1, r, k * chunk_pad : (k + 1) * chunk_pad, :] = piece
                pstage[1, r, k * chunk_pad : (k + 1) * chunk_pad, :] = piece.astype(bf)
    send_pairs(1, 0, taps)

    pltpu.make_async_copy(r2, r2, w_sem.at[1]).wait()
    got = lax.dot_general(
        c9[:, :mp, :].reshape(tmn * mp, 9 * C), r2[...], NT, preferred_element_type=f32
    )
    for d in range(tmn):
        conv[partner(d)] = got[d * mp : (d + 1) * mp]
    for t in range(tmn):
        grad = conv[t, :cells, 2 * C :]
        for a in range(2):
            s = t + 2 - a
            if s < tmn:
                grad = grad + conv[s, :cells, C * a : C * (a + 1)]
        grad = (grad * gate[t]).astype(bf)
        ghb[t, :cells, :] = grad
        ghf[t * cells : (t + 1) * cells, :] = grad.astype(f32)

    own3[...] = ghf[pl.ds(pl.multiple_of(tm * cells, 8), 3 * cells), :]
    for h in range(2):
        gedge[h] = own3[pl.ds(h * (cols - 1), 3 * rows, stride=cols), :].astype(bf)
    for v in range(2):
        grim[v] = jnp.concatenate(
            [
                own3[j * cells + v * (cells - cols) : j * cells + v * (cells - cols) + cols, :]
                for j in range(3)
            ],
            axis=0,
        ).astype(bf)
    grims = near(grim, gedge, grim_in, gedge_in, gcorner_in, gnear_sem)
    start_all(grims)

    scatter(1)

    choose_x(range(tmn))

    for lo, hi in ((0, 2), (2, 3)):
        total = None
        for d in range(tmn):
            s = partner(d)
            right_side = jnp.concatenate([ghb[s + 2 - a, :mp] for a in range(lo, hi)], axis=1)
            got = jnp.dot(xt[d, :, :mp], right_side, preferred_element_type=f32)
            total = got if total is None else total + got
        for a in range(lo, hi):
            for r in range(rn):
                for q in range(9):
                    k = 9 * a + q
                    base = q * cwp + r * chunk_pad
                    piece = total[base : base + chunk_pad, C * (a - lo) : C * (a - lo + 1)]
                    part[0, r, k * chunk_pad : (k + 1) * chunk_pad, :] = piece
                    pstage[0, r, k * chunk_pad : (k + 1) * chunk_pad, :] = piece.astype(bf)
        send_pairs(0, 9 * lo * chunk_pad, 9 * hi * chunk_pad)

    scatter(0)

    await_all(grims)
    assemble(gf, 3, grim_in, gedge_in, gcorner_in)
    for j in range(3):
        spread(
            sh.at[j],
            own3[j * cells : (j + 1) * cells, :],
            gf[j, :cols, :],
            gf[j, cols : 2 * cols, :],
            [gf[j, base + 1 : base + 1 + rows, :] for base in (left, right)],
            [[gf[j, base + put : base + put + 1, :] for base in (left, right)] for put in (0, rows + 1)],
        )
        for q in range(9):
            b, e = q // 3, q % 3
            lane = C * (3 * q + 2 - j)
            imc[:, lane : lane + C] = sh[j, 2 - e, cols * (2 - b) : cols * (2 - b) + mp, :].astype(bf)

    total = None
    for q in range(9):
        got = lax.dot_general(
            imc[:, 3 * C * q : 3 * C * (q + 1)], r1[C * q : C * (q + 1), :], NT, preferred_element_type=f32
        )
        total = got if total is None else total + got
    back_ref[...] = flat[1] + total[:cells]

    for tensor, out in ((1, two_ref), (0, one_ref)):
        landed[tensor, col] = stage[tensor, col]
        if zn > 1:
            arrived(landed.at[tensor, : zn - 1], rs_recv.at[tensor])
        got = landed[tensor, 0].astype(f32)
        for z in range(1, zn):
            got = got + landed[tensor, z].astype(f32)
        whole = jnp.concatenate(
            [got[:, ochunk * q : ochunk * (q + 1)] for q in range(zn)], axis=0
        ).reshape(slots, chunk_pad, ochunk)
        out[...] = whole[:27, :chunk, :]

    for which in range(2):
        if tmn > 1:
            sent(gat.at[which, 1:], blk_send.at[which])
        if rn > 1:
            sent(pstage.at[which, : rn - 1], pair_send.at[which])
        if zn > 1:
            sent(stage.at[which, : zn - 1], rs_send.at[which])
    for h in range(2):

        @pl.when(side[h])
        def _():
            sent(edge_in.at[:, h], near_send.at[2 + h])

    for v in range(2):

        @pl.when(vert[v])
        def _():
            sent(rim_in.at[:, v], near_send.at[v])

    for v in range(2):
        for h in range(2):

            @pl.when(jnp.logical_and(vert[v], side[h]))
            def _():
                sent(tip_in.at[:, v, h], near_send.at[4 + 2 * v + h])

    drain_all(grims)


def finish(back_ref, one_ref, two_ref, back_out, one_out, two_out, sem):
    pairs = ((back_ref, back_out), (one_ref, one_out), (two_ref, two_out))
    copies = [pltpu.make_async_copy(src, dst, sem.at[i]) for i, (src, dst) in enumerate(pairs)]
    for copy in copies:
        copy.start()
    for copy in copies:
        copy.wait()


def body(sizes, inputs, cotangent, weight_one, weight_two):
    tmn, rn, zn = sizes
    _, rows, cols, channels = inputs.shape
    cells = rows * cols
    chunk = channels // (tmn * rn)
    chunk_pad = max(16, chunk)
    slots = 28
    lift = (rows + 2) * cols
    mp = -(-cells // 16) * 16
    kp = -(-cells // 128) * 128
    hs = -(-(2 * cols + 2 * (-(-(rows + 2) // 8) * 8)) // 16) * 16
    cwp = rn * chunk_pad
    taps = 27 * chunk_pad
    dims = (tmn, rn, zn, rows, cols, chunk, chunk_pad, slots)
    vmem = pl.BlockSpec(memory_space=pltpu.VMEM)
    bf, f32 = jnp.bfloat16, jnp.float32
    group = slots * chunk_pad // zn
    dma = pltpu.SemaphoreType.DMA
    lifted = lift + mp - cells
    sums = (27, chunk, channels // zn)
    outs = pl.pallas_call(
        functools.partial(kernel, dims),
        out_shape=(
            pltpu.VMEM((cells, channels), f32),
            pltpu.VMEM(sums, f32),
            pltpu.VMEM(sums, f32),
        ),
        in_specs=[pl.BlockSpec(memory_space=pl.ANY)] * 4,
        out_specs=(vmem,) * 3,
        scratch_shapes=[
            pltpu.VMEM((2, tmn, cells, channels), bf),
            pltpu.VMEM((2, cells, channels), f32),
            pltpu.VMEM((tmn, 3, lifted, channels), f32),
            pltpu.VMEM((tmn, 3, lifted, channels), f32),
            pltpu.VMEM((tmn, mp, 9 * channels), bf),
            pltpu.VMEM((tmn, kp, 9 * channels), bf),
            pltpu.VMEM((9 * channels, 3 * channels), bf),
            pltpu.VMEM((3 * channels, 9 * channels), bf),
            pltpu.VMEM((tmn, mp, 3 * channels), f32),
            pltpu.VMEM((tmn, cells, channels), f32),
            pltpu.VMEM(((tmn + 2) * cwp, kp), bf),
            pltpu.VMEM((tmn, 9 * cwp, kp), bf),
            pltpu.VMEM((tmn + 2, kp, channels), bf),
            pltpu.VMEM(((tmn + 2) * cells, channels), f32),
            pltpu.VMEM((3 * cells, channels), f32),
            pltpu.VMEM((3, hs, channels), f32),
            pltpu.VMEM((3, 3, lifted, channels), f32),
            pltpu.VMEM((mp, 27 * channels), bf),
            pltpu.VMEM((2, rn, taps, channels), f32),
            pltpu.VMEM((2, rn, taps, channels), bf),
            pltpu.VMEM((2, rn, taps, channels), bf),
            pltpu.VMEM((slots * chunk_pad, channels), f32),
            pltpu.VMEM((2, zn, group, channels), bf),
            pltpu.VMEM((2, zn, group, channels), bf),
            pltpu.VMEM((2, 2, cols, channels), bf),
            pltpu.VMEM((2, 2, rows, channels), bf),
            pltpu.VMEM((2, 2, 2, 8, channels), bf),
            pltpu.VMEM((2, 2, tmn, cols, channels), bf),
            pltpu.VMEM((2, 2, tmn, rows, channels), bf),
            pltpu.VMEM((2, 2, 2, tmn, 8, channels), bf),
            pltpu.VMEM((2, 3 * cols, channels), bf),
            pltpu.VMEM((2, 3 * rows, channels), bf),
            pltpu.VMEM((2, 3 * cols, channels), bf),
            pltpu.VMEM((2, 3 * rows, channels), bf),
            pltpu.VMEM((2, 2, 3 * rows, channels), bf),
            dma((2,)),
            dma((2,)),
            dma((2,)),
            dma((2, -(-tmn // 2))),
            dma((8,)),
            dma((2, 8)),
            dma((2, 8)),
            dma((2,)),
            dma((2,)),
            dma((2,)),
            dma((2,)),
        ],
        compiler_params=pltpu.CompilerParams(
            collective_id=0, has_side_effects=True, vmem_limit_bytes=60 * 1024 * 1024
        ),
    )(
        inputs.reshape(cells, channels),
        cotangent.reshape(cells, channels),
        weight_one.reshape(27 * channels, channels),
        weight_two.reshape(27 * channels, channels),
    )
    back, one, two = pl.pallas_call(
        finish,
        out_shape=(
            jax.ShapeDtypeStruct((cells, channels), f32),
            jax.ShapeDtypeStruct(sums, f32),
            jax.ShapeDtypeStruct(sums, f32),
        ),
        in_specs=[vmem] * 3,
        out_specs=(pl.BlockSpec(memory_space=pl.ANY),) * 3,
        scratch_shapes=[dma((3,))],
    )(*[pltpu.with_memory_space_constraint(out, pltpu.VMEM) for out in outs])
    return back.reshape(1, rows, cols, channels), one, two


def solution(mesh):
    sizes = (mesh.shape["tm"], mesh.shape["rows"], mesh.shape["cols"])
    placed = (P("tm", "rows", "cols", None), P("tm", "rows", "cols", None), P(), P())
    return jax.shard_map(
        functools.partial(body, sizes),
        mesh=mesh,
        in_specs=placed,
        out_specs=(
            P("tm", "rows", "cols", None),
            P(None, ("tm", "rows"), "cols"),
            P(None, ("tm", "rows"), "cols"),
        ),
        check_vma=False,
    )
```

```python
import functools

import jax
import jax.numpy as jnp
from jax import lax
from jax.experimental import pallas as pl
from jax.experimental.pallas import tpu as pltpu
from jax.sharding import PartitionSpec as P

MESH = pl.DeviceIdType.MESH
NT = (((1,), (1,)), ((), ()))
C = 128


def kernel(
    dims,
    x_ref,
    c_ref,
    w1_ref,
    w2_ref,
    back_ref,
    one_ref,
    two_ref,
    gat,
    flat,
    sx,
    sc,
    x9,
    c9,
    r1,
    r2,
    conv,
    gate,
    at,
    xt,
    ghb,
    ghf,
    own3,
    gf,
    sh,
    imc,
    part,
    pstage,
    pland,
    pp,
    stage,
    landed,
    rim,
    edge,
    tip,
    rim_in,
    edge_in,
    tip_in,
    grim,
    gedge,
    grim_in,
    gedge_in,
    gcorner_in,
    own_sem,
    w_sem,
    blk_send,
    blk_recv,
    near_send,
    near_recv,
    gnear_sem,
    pair_send,
    pair_recv,
    rs_send,
    rs_recv,
):
    tmn, rn, zn, rows, cols, chunk, chunk_pad, slots = dims
    cells = rows * cols
    lift = (rows + 2) * cols
    left = 2 * cols
    right = left + -(-(rows + 2) // 8) * 8
    mp, kp = x9.shape[1], c9.shape[1]
    taps = 27 * chunk_pad
    cwp = rn * chunk_pad
    ochunk = C // zn
    bf, f32 = jnp.bfloat16, jnp.float32
    tm, row, col = lax.axis_index("tm"), lax.axis_index("rows"), lax.axis_index("cols")
    vert = (row > 0, row < rn - 1)
    side = (col > 0, col < zn - 1)
    step = (-1, 1)

    def partner(d):
        got, bit = tm, 1
        while bit <= d:
            if d & bit:
                got = got + bit - 2 * bit * lax.rem(got // bit, 2)
            bit *= 2
        return got

    blocks = (x_ref, c_ref)

    def keep(which):
        return pltpu.make_async_copy(blocks[which], gat.at[which, 0], own_sem.at[which])

    keep(0).start()
    keep(1).start()
    barrier = pltpu.get_barrier_semaphore()

    def greet(place):
        pl.semaphore_signal(barrier, inc=1, device_id=place, device_id_type=MESH)

    for d in range(tmn - 1, 0, -1):
        greet((partner(d), row, col))
    for v in range(2):

        @pl.when(vert[v])
        def _():
            for d in range(tmn - 1, -1, -1):
                greet((partner(d), row + step[v], col))

    for h in range(2):

        @pl.when(side[h])
        def _():
            for d in range(tmn - 1, -1, -1):
                greet((partner(d), row, col + step[h]))

    for v in range(2):
        for h in range(2):

            @pl.when(jnp.logical_and(vert[v], side[h]))
            def _():
                for d in range(tmn - 1, -1, -1):
                    greet((partner(d), row + step[v], col + step[h]))

    for z in range(zn):

        @pl.when(jnp.logical_or(col - z > 1, z - col > 1))
        def _():
            greet((tm, row, z))

    for r in range(rn if rn > 2 else 0):

        @pl.when(jnp.logical_or(row - r > 1, r - row > 1))
        def _():
            greet((tm, r, col))

    def load_one(k):
        a, q = k // 9, k % 9
        return pltpu.make_async_copy(
            w1_ref.at[pl.ds(C * k, C), :], r1.at[pl.ds(C * q, C), pl.ds(C * a, C)], w_sem.at[0]
        )

    def load_two(k):
        a, q = k // 9, k % 9
        return pltpu.make_async_copy(
            w2_ref.at[pl.ds(C * k, C), :], r2.at[pl.ds(C * a, C), pl.ds(C * q, C)], w_sem.at[1]
        )

    for k in range(27):
        load_one(k).start()
    for k in range(27):
        load_two(k).start()

    for v in range(2):

        @pl.when(jnp.logical_not(vert[v]))
        def _():
            rim_in[:, v] = jnp.zeros((2, tmn, cols, C), bf)
            tip_in[:, v] = jnp.zeros((2, 2, tmn, 8, C), bf)

    for h in range(2):

        @pl.when(jnp.logical_not(side[h]))
        def _():
            edge_in[:, h] = jnp.zeros((2, tmn, rows, C), bf)
            tip_in[:, :, h] = jnp.zeros((2, 2, tmn, 8, C), bf)

    for which in range(2):
        keep(which).wait()
        flat[which] = gat[which, 0].astype(f32)
        for h in range(2):
            edge[which, h] = flat[which, pl.ds(h * (cols - 1), rows, stride=cols), :].astype(bf)
        for v in range(2):
            line = flat[which, v * (cells - cols) : v * (cells - cols) + cols, :]
            rim[which, v] = line.astype(bf)
            for h in range(2):
                tip[which, v, h] = jnp.broadcast_to(line[h * (cols - 1) : h * (cols - 1) + 1], (8, C)).astype(bf)

    def remote(src, dst, send, recv, place):
        return pltpu.make_async_remote_copy(
            src_ref=src, dst_ref=dst, send_sem=send, recv_sem=recv, device_id=place, device_id_type=MESH
        )

    def near(out_rim, out_edge, in_rim, in_edge, in_corner, sems):
        found = []
        for v in range(2):
            found.append((
                vert[v],
                lambda v=v: remote(
                    out_rim.at[v], in_rim.at[1 - v], sems.at[0, v], sems.at[1, 1 - v], (tm, row + step[v], col)
                ),
                in_rim.at[v],
                sems.at[1, v],
            ))
        for h in range(2):
            found.append((
                side[h],
                lambda h=h: remote(
                    out_edge.at[h], in_edge.at[1 - h], sems.at[0, 2 + h], sems.at[1, 3 - h], (tm, row, col + step[h])
                ),
                in_edge.at[h],
                sems.at[1, 2 + h],
            ))
        for v in range(2):
            for h in range(2):
                found.append((
                    jnp.logical_and(vert[v], side[h]),
                    lambda v=v, h=h: remote(
                        out_edge.at[h],
                        in_corner.at[1 - v, 1 - h],
                        sems.at[0, 4 + 2 * v + h],
                        sems.at[1, 4 + 2 * (1 - v) + 1 - h],
                        (tm, row + step[v], col + step[h]),
                    ),
                    in_corner.at[v, h],
                    sems.at[1, 4 + 2 * v + h],
                ))
        return found

    def start_all(found):
        for cond, copy, _, _ in found:

            @pl.when(cond)
            def _():
                copy().start()

    def drain_all(found):
        for cond, copy, _, _ in found:

            @pl.when(cond)
            def _():
                copy().wait_send()

    def arrived(dst, sem):
        remote(dst, dst, sem, sem, (tm, row, col)).wait_recv()

    def await_all(found):
        for cond, _, dst, sem in found:

            @pl.when(cond)
            def _():
                arrived(dst, sem)

    def assemble(dst, count, in_rim, in_edge, in_corner):
        for v in range(2):

            @pl.when(vert[v])
            def _():
                got = in_rim[v].astype(f32)
                for q in range(count):
                    dst[q, v * cols : (v + 1) * cols, :] = got[q * cols : (q + 1) * cols]

        for h, base in enumerate((left, right)):

            @pl.when(side[h])
            def _():
                got = in_edge[h].astype(f32)
                for q in range(count):
                    dst[q, base + 1 : base + 1 + rows, :] = got[q * rows : (q + 1) * rows]

            for v in range(2):

                @pl.when(jnp.logical_and(vert[v], side[h]))
                def _():
                    got = in_corner[v, h].astype(f32)
                    put = base + v * (rows + 1)
                    for q in range(count):
                        take = q * rows + (1 - v) * (rows - 1)
                        dst[q, put : put + 1, :] = got[take : take + 1]

    def spread(dst, v, top, bottom, sides, tips):
        dst[1, :cols, :] = top
        dst[1, cols : cols + cells, :] = v
        dst[1, cols + cells : lift, :] = bottom
        dst[0, 1 : cols + 1, :] = top
        dst[0, cols + 1 : cols + cells + 1, :] = v
        dst[0, cols + cells + 1 : lift, :] = bottom[: cols - 1]
        dst[0, :1, :] = tips[0][0]
        dst[0, pl.ds(cols, rows, stride=cols), :] = sides[0]
        dst[0, cols + cells : cols + cells + 1, :] = tips[1][0]
        dst[2, : cols - 1, :] = top[1:]
        dst[2, cols - 1 : cols + cells - 1, :] = v
        dst[2, cols + cells - 1 : lift - 1, :] = bottom
        dst[2, cols - 1 : cols, :] = tips[0][1]
        dst[2, pl.ds(2 * cols - 1, rows, stride=cols), :] = sides[1]
        dst[2, lift - 1 : lift, :] = tips[1][1]

    nv = vert[0].astype(jnp.int32) + vert[1].astype(jnp.int32)
    nh = side[0].astype(jnp.int32) + side[1].astype(jnp.int32)
    pl.semaphore_wait(barrier, tmn * (1 + nv) * (1 + nh) - 1 + zn - 1 - nh + rn - 1 - nv)

    groups = [list(range(d, min(d + 2, tmn))) for d in range(0, tmn, 2)]

    def send_block(which, d):
        return remote(
            gat.at[which, 0],
            gat.at[which, d],
            blk_send.at[which],
            blk_recv.at[which, d // 2],
            (partner(d), row, col),
        )

    def send_rim(which, v, d):
        return remote(
            rim.at[which, v],
            rim_in.at[which, 1 - v, d],
            near_send.at[v],
            near_recv.at[which, 1 - v],
            (partner(d), row + step[v], col),
        )

    def send_edge(which, h, d):
        return remote(
            edge.at[which, h],
            edge_in.at[which, 1 - h, d],
            near_send.at[2 + h],
            near_recv.at[which, 3 - h],
            (partner(d), row, col + step[h]),
        )

    def send_tip(which, v, h, d):
        return remote(
            tip.at[which, v, h],
            tip_in.at[which, 1 - v, 1 - h, d],
            near_send.at[4 + 2 * v + h],
            near_recv.at[which, 4 + 2 * (1 - v) + 1 - h],
            (partner(d), row + step[v], col + step[h]),
        )

    def send_near(which, ds):
        for h in range(2):

            @pl.when(side[h])
            def _():
                for d in ds:
                    send_edge(which, h, d).start()

        for v in range(2):

            @pl.when(vert[v])
            def _():
                for d in ds:
                    send_rim(which, v, d).start()

        for v in range(2):
            for h in range(2):

                @pl.when(jnp.logical_and(vert[v], side[h]))
                def _():
                    for d in ds:
                        send_tip(which, v, h, d).start()

    for which in range(2):
        send_near(which, range(tmn - 1, -1, -1))
        for ds in groups:
            for d in ds[::-1]:
                if d:
                    send_block(which, d).start()

    def sent(like, sem):
        remote(like, like, sem, sem, (tm, row, col)).wait_send()

    def receive(which, ds, dst):
        g = ds[0] // 2
        if ds[-1]:
            arrived(gat.at[which, max(ds[0], 1) : ds[-1] + 1], blk_recv.at[which, g])
        for h in range(2 if g == 0 else 0):

            @pl.when(side[h])
            def _():
                arrived(edge_in.at[which, h], near_recv.at[which, 2 + h])

        for v in range(2 if g == 0 else 0):

            @pl.when(vert[v])
            def _():
                arrived(rim_in.at[which, v], near_recv.at[which, v])

        for v in range(2 if g == 0 else 0):
            for h in range(2):

                @pl.when(jnp.logical_and(vert[v], side[h]))
                def _():
                    arrived(tip_in.at[which, v, h], near_recv.at[which, 4 + 2 * v + h])

        for d in ds:
            spread(
                dst.at[d],
                gat[which, d].astype(f32),
                rim_in[which, 0, d].astype(f32),
                rim_in[which, 1, d].astype(f32),
                [edge_in[which, h, d].astype(f32) for h in range(2)],
                [[tip_in[which, v, h, d].astype(f32)[:1] for h in range(2)] for v in range(2)],
            )

    for tail in (sx, sc):
        for s in range(tmn):
            for e in range(3):
                tail[s, e, lift:, :] = jnp.zeros((tail.shape[2] - lift, C), f32)
    for s in range(tmn):
        c9[s, mp:, :] = jnp.zeros((kp - mp, 9 * C), bf)
        xt[s] = jnp.zeros(xt.shape[1:], bf)
    at[...] = jnp.zeros(at.shape, bf)
    for s in range(tmn + 2):
        ghb[s] = jnp.zeros((kp, C), bf)
    ghf[tmn * cells :, :] = jnp.zeros((2 * cells, C), f32)
    gf[...] = jnp.zeros(gf.shape, f32)
    for j in range(3):
        for e in range(3):
            sh[j, e, lift:, :] = jnp.zeros((sh.shape[2] - lift, C), f32)
    pp[taps:, :] = jnp.zeros((pp.shape[0] - taps, C), f32)
    picked = jnp.concatenate(
        [
            jnp.where(
                (lax.broadcasted_iota(jnp.int32, (chunk_pad, C), 1)
                 == (tm * rn + r) * chunk + lax.broadcasted_iota(jnp.int32, (chunk_pad, C), 0))
                & (lax.broadcasted_iota(jnp.int32, (chunk_pad, C), 0) < chunk),
                1.0, 0.0,
            )
            for r in range(rn)
        ],
        axis=0,
    ).astype(bf)

    def tall(src):
        return lax.dot_general(picked, src, NT, preferred_element_type=f32).astype(bf)

    def choose_x(ds):
        for d in ds:
            for e in range(3):
                got = lax.dot_general(picked, sx[d, e].astype(bf), NT, preferred_element_type=f32)
                for b in range(3):
                    q = 3 * b + e
                    xt[d, cwp * q : cwp * (q + 1), :mp] = got[:, cols * b : cols * b + mp].astype(bf)

    for ds in groups:
        receive(0, ds, sx)
        for d in ds:
            for q in range(9):
                b, e = q // 3, q % 3
                x9[d, :, C * q : C * (q + 1)] = sx[d, e, cols * b : cols * b + mp, :].astype(bf)
        if ds[0] == 0:
            pltpu.make_async_copy(r1, r1, w_sem.at[0]).wait()
        got = jnp.dot(
            x9[ds[0] : ds[-1] + 1].reshape(len(ds) * mp, 9 * C), r1[...], preferred_element_type=f32
        )
        for d in ds:
            conv[partner(d)] = got[(d - ds[0]) * mp : (d - ds[0] + 1) * mp]
        if ds is not groups[-1]:
            choose_x(ds)
    for t in range(tmn):
        hidden = conv[t, :cells, 2 * C :]
        for a in range(2):
            s = t - 2 + a
            if s >= 0:
                hidden = hidden + conv[s, :cells, C * a : C * (a + 1)]
        squash = jax.nn.sigmoid(hidden)
        gate[t] = squash * (1.0 + hidden * (1.0 - squash))
        at[(t + 2) * cwp : (t + 3) * cwp, :cells] = tall((hidden * squash).astype(bf))

    def send_pairs(tensor):
        for d in range(1, rn):
            r = lax.rem(row + d, rn)
            remote(
                pstage.at[tensor, r],
                pland.at[tensor, row],
                pair_send.at[tensor],
                pair_recv.at[tensor],
                (tm, r, col),
            ).start()

    group = slots * chunk_pad // zn

    def scatter(tensor):
        if rn > 1:
            arrived(pland.at[tensor, : rn - 1], pair_recv.at[tensor])
        got = part[tensor, row]
        for d in range(1, rn):
            got = got + pland[tensor, lax.rem(row + d, rn)].astype(f32)
        pp[:taps, :] = got
        for z in range(zn):
            stage[tensor, z] = jnp.concatenate(
                [pp[group * q : group * (q + 1), ochunk * z : ochunk * (z + 1)] for q in range(zn)],
                axis=1,
            ).astype(bf)
        for d in range(1, zn):
            z = lax.rem(col + d, zn)
            remote(
                stage.at[tensor, z],
                landed.at[tensor, col],
                rs_send.at[tensor],
                rs_recv.at[tensor],
                (tm, row, z),
            ).start()

    total = None
    for ds in groups:
        receive(1, ds, sc)
        for d in ds:
            for q in range(9):
                b, e = q // 3, q % 3
                c9[d, :mp, C * q : C * (q + 1)] = sc[d, 2 - e, cols * (2 - b) : cols * (2 - b) + mp, :].astype(bf)
        for d in ds:
            lines = pl.ds(pl.multiple_of(partner(d) * cwp, 16), 3 * cwp)
            got = jnp.dot(at[lines, :mp], c9[d, :mp], preferred_element_type=f32)
            total = got if total is None else total + got
    for a in range(3):
        for r in range(rn):
            for q in range(9):
                k = 9 * a + q
                piece = total[a * cwp + r * chunk_pad : a * cwp + (r + 1) * chunk_pad, C * q : C * (q + 1)]
                part[1, r, k * chunk_pad : (k + 1) * chunk_pad, :] = piece
                pstage[1, r, k * chunk_pad : (k + 1) * chunk_pad, :] = piece.astype(bf)
    send_pairs(1)

    pltpu.make_async_copy(r2, r2, w_sem.at[1]).wait()
    got = lax.dot_general(
        c9[:, :mp, :].reshape(tmn * mp, 9 * C), r2[...], NT, preferred_element_type=f32
    )
    for d in range(tmn):
        conv[partner(d)] = got[d * mp : (d + 1) * mp]
    for t in range(tmn):
        grad = conv[t, :cells, 2 * C :]
        for a in range(2):
            s = t + 2 - a
            if s < tmn:
                grad = grad + conv[s, :cells, C * a : C * (a + 1)]
        grad = (grad * gate[t]).astype(bf)
        ghb[t, :cells, :] = grad
        ghf[t * cells : (t + 1) * cells, :] = grad.astype(f32)

    own3[...] = ghf[pl.ds(pl.multiple_of(tm * cells, 8), 3 * cells), :]
    for h in range(2):
        gedge[h] = own3[pl.ds(h * (cols - 1), 3 * rows, stride=cols), :].astype(bf)
    for v in range(2):
        grim[v] = jnp.concatenate(
            [
                own3[j * cells + v * (cells - cols) : j * cells + v * (cells - cols) + cols, :]
                for j in range(3)
            ],
            axis=0,
        ).astype(bf)
    grims = near(grim, gedge, grim_in, gedge_in, gcorner_in, gnear_sem)
    start_all(grims)

    scatter(1)

    choose_x(groups[-1])

    total = None
    for d in range(tmn):
        s = partner(d)
        right_side = jnp.concatenate([ghb[s + 2 - a, :mp] for a in range(3)], axis=1)
        got = jnp.dot(xt[d, :, :mp], right_side, preferred_element_type=f32)
        total = got if total is None else total + got
    for q in range(9):
        for r in range(rn):
            for a in range(3):
                k = 9 * a + q
                piece = total[q * cwp + r * chunk_pad : q * cwp + (r + 1) * chunk_pad, C * a : C * (a + 1)]
                part[0, r, k * chunk_pad : (k + 1) * chunk_pad, :] = piece
                pstage[0, r, k * chunk_pad : (k + 1) * chunk_pad, :] = piece.astype(bf)
    send_pairs(0)

    scatter(0)

    await_all(grims)
    assemble(gf, 3, grim_in, gedge_in, gcorner_in)
    for j in range(3):
        spread(
            sh.at[j],
            own3[j * cells : (j + 1) * cells, :],
            gf[j, :cols, :],
            gf[j, cols : 2 * cols, :],
            [gf[j, base + 1 : base + 1 + rows, :] for base in (left, right)],
            [[gf[j, base + put : base + put + 1, :] for base in (left, right)] for put in (0, rows + 1)],
        )
        for q in range(9):
            b, e = q // 3, q % 3
            lane = C * (3 * q + 2 - j)
            imc[:, lane : lane + C] = sh[j, 2 - e, cols * (2 - b) : cols * (2 - b) + mp, :].astype(bf)

    total = None
    for q in range(9):
        got = lax.dot_general(
            imc[:, 3 * C * q : 3 * C * (q + 1)], r1[C * q : C * (q + 1), :], NT, preferred_element_type=f32
        )
        total = got if total is None else total + got
    back_ref[...] = flat[1] + total[:cells]

    for tensor, out in ((1, two_ref), (0, one_ref)):
        landed[tensor, col] = stage[tensor, col]
        if zn > 1:
            arrived(landed.at[tensor, : zn - 1], rs_recv.at[tensor])
        got = landed[tensor, 0].astype(f32)
        for z in range(1, zn):
            got = got + landed[tensor, z].astype(f32)
        whole = jnp.concatenate(
            [got[:, ochunk * q : ochunk * (q + 1)] for q in range(zn)], axis=0
        ).reshape(slots, chunk_pad, ochunk)
        out[...] = whole[:27, :chunk, :]

    for which in range(2):
        if tmn > 1:
            sent(gat.at[which, 1:], blk_send.at[which])
        if rn > 1:
            sent(pstage.at[which, : rn - 1], pair_send.at[which])
        if zn > 1:
            sent(stage.at[which, : zn - 1], rs_send.at[which])
    for h in range(2):

        @pl.when(side[h])
        def _():
            sent(edge_in.at[:, h], near_send.at[2 + h])

    for v in range(2):

        @pl.when(vert[v])
        def _():
            sent(rim_in.at[:, v], near_send.at[v])

    for v in range(2):
        for h in range(2):

            @pl.when(jnp.logical_and(vert[v], side[h]))
            def _():
                sent(tip_in.at[:, v, h], near_send.at[4 + 2 * v + h])

    drain_all(grims)


def finish(back_ref, one_ref, two_ref, back_out, one_out, two_out, sem):
    pairs = ((back_ref, back_out), (one_ref, one_out), (two_ref, two_out))
    copies = [pltpu.make_async_copy(src, dst, sem.at[i]) for i, (src, dst) in enumerate(pairs)]
    for copy in copies:
        copy.start()
    for copy in copies:
        copy.wait()


def body(sizes, inputs, cotangent, weight_one, weight_two):
    tmn, rn, zn = sizes
    _, rows, cols, channels = inputs.shape
    cells = rows * cols
    chunk = channels // (tmn * rn)
    chunk_pad = max(16, chunk)
    slots = 28
    lift = (rows + 2) * cols
    mp = -(-cells // 16) * 16
    kp = -(-cells // 128) * 128
    hs = -(-(2 * cols + 2 * (-(-(rows + 2) // 8) * 8)) // 16) * 16
    cwp = rn * chunk_pad
    taps = 27 * chunk_pad
    dims = (tmn, rn, zn, rows, cols, chunk, chunk_pad, slots)
    vmem = pl.BlockSpec(memory_space=pltpu.VMEM)
    bf, f32 = jnp.bfloat16, jnp.float32
    group = slots * chunk_pad // zn
    dma = pltpu.SemaphoreType.DMA
    lifted = lift + mp - cells
    sums = (27, chunk, channels // zn)
    outs = pl.pallas_call(
        functools.partial(kernel, dims),
        out_shape=(
            pltpu.VMEM((cells, channels), f32),
            pltpu.VMEM(sums, f32),
            pltpu.VMEM(sums, f32),
        ),
        in_specs=[pl.BlockSpec(memory_space=pl.ANY)] * 4,
        out_specs=(vmem,) * 3,
        scratch_shapes=[
            pltpu.VMEM((2, tmn, cells, channels), bf),
            pltpu.VMEM((2, cells, channels), f32),
            pltpu.VMEM((tmn, 3, lifted, channels), f32),
            pltpu.VMEM((tmn, 3, lifted, channels), f32),
            pltpu.VMEM((tmn, mp, 9 * channels), bf),
            pltpu.VMEM((tmn, kp, 9 * channels), bf),
            pltpu.VMEM((9 * channels, 3 * channels), bf),
            pltpu.VMEM((3 * channels, 9 * channels), bf),
            pltpu.VMEM((tmn, mp, 3 * channels), f32),
            pltpu.VMEM((tmn, cells, channels), f32),
            pltpu.VMEM(((tmn + 2) * cwp, kp), bf),
            pltpu.VMEM((tmn, 9 * cwp, kp), bf),
            pltpu.VMEM((tmn + 2, kp, channels), bf),
            pltpu.VMEM(((tmn + 2) * cells, channels), f32),
            pltpu.VMEM((3 * cells, channels), f32),
            pltpu.VMEM((3, hs, channels), f32),
            pltpu.VMEM((3, 3, lifted, channels), f32),
            pltpu.VMEM((mp, 27 * channels), bf),
            pltpu.VMEM((2, rn, taps, channels), f32),
            pltpu.VMEM((2, rn, taps, channels), bf),
            pltpu.VMEM((2, rn, taps, channels), bf),
            pltpu.VMEM((slots * chunk_pad, channels), f32),
            pltpu.VMEM((2, zn, group, channels), bf),
            pltpu.VMEM((2, zn, group, channels), bf),
            pltpu.VMEM((2, 2, cols, channels), bf),
            pltpu.VMEM((2, 2, rows, channels), bf),
            pltpu.VMEM((2, 2, 2, 8, channels), bf),
            pltpu.VMEM((2, 2, tmn, cols, channels), bf),
            pltpu.VMEM((2, 2, tmn, rows, channels), bf),
            pltpu.VMEM((2, 2, 2, tmn, 8, channels), bf),
            pltpu.VMEM((2, 3 * cols, channels), bf),
            pltpu.VMEM((2, 3 * rows, channels), bf),
            pltpu.VMEM((2, 3 * cols, channels), bf),
            pltpu.VMEM((2, 3 * rows, channels), bf),
            pltpu.VMEM((2, 2, 3 * rows, channels), bf),
            dma((2,)),
            dma((2,)),
            dma((2,)),
            dma((2, -(-tmn // 2))),
            dma((8,)),
            dma((2, 8)),
            dma((2, 8)),
            dma((2,)),
            dma((2,)),
            dma((2,)),
            dma((2,)),
        ],
        compiler_params=pltpu.CompilerParams(
            collective_id=0, has_side_effects=True, vmem_limit_bytes=60 * 1024 * 1024
        ),
    )(
        inputs.reshape(cells, channels),
        cotangent.reshape(cells, channels),
        weight_one.reshape(27 * channels, channels),
        weight_two.reshape(27 * channels, channels),
    )
    back, one, two = pl.pallas_call(
        finish,
        out_shape=(
            jax.ShapeDtypeStruct((cells, channels), f32),
            jax.ShapeDtypeStruct(sums, f32),
            jax.ShapeDtypeStruct(sums, f32),
        ),
        in_specs=[vmem] * 3,
        out_specs=(pl.BlockSpec(memory_space=pl.ANY),) * 3,
        scratch_shapes=[dma((3,))],
    )(*[pltpu.with_memory_space_constraint(out, pltpu.VMEM) for out in outs])
    return back.reshape(1, rows, cols, channels), one, two


def solution(mesh):
    sizes = (mesh.shape["tm"], mesh.shape["rows"], mesh.shape["cols"])
    placed = (P("tm", "rows", "cols", None), P("tm", "rows", "cols", None), P(), P())
    return jax.shard_map(
        functools.partial(body, sizes),
        mesh=mesh,
        in_specs=placed,
        out_specs=(
            P("tm", "rows", "cols", None),
            P(None, ("tm", "rows"), "cols"),
            P(None, ("tm", "rows"), "cols"),
        ),
        check_vma=False,
    )
```

```python
import functools

import jax
import jax.numpy as jnp
from jax import lax
from jax.experimental import pallas as pl
from jax.experimental.pallas import tpu as pltpu
from jax.sharding import PartitionSpec as P

MESH = pl.DeviceIdType.MESH
NT = (((1,), (1,)), ((), ()))
C = 128


def kernel(
    dims,
    x_ref,
    c_ref,
    w1_ref,
    w2_ref,
    back_ref,
    one_ref,
    two_ref,
    gat,
    flat,
    sx,
    sc,
    x9,
    c9,
    r1,
    r2,
    conv,
    gate,
    at,
    xt,
    ghb,
    ghf,
    own3,
    gf,
    sh,
    imc,
    part,
    pstage,
    pland,
    pp,
    stage,
    landed,
    rim,
    edge,
    tip,
    rim_in,
    edge_in,
    tip_in,
    grim,
    gedge,
    grim_in,
    gedge_in,
    gcorner_in,
    own_sem,
    w_sem,
    blk_send,
    blk_recv,
    near_send,
    near_recv,
    gnear_sem,
    pair_send,
    pair_recv,
    rs_send,
    rs_recv,
):
    tmn, rn, zn, rows, cols, chunk, chunk_pad, slots = dims
    cells = rows * cols
    lift = (rows + 2) * cols
    left = 2 * cols
    right = left + -(-(rows + 2) // 8) * 8
    mp, kp = x9.shape[1], c9.shape[1]
    taps = 27 * chunk_pad
    cwp = rn * chunk_pad
    ochunk = C // zn
    bf, f32 = jnp.bfloat16, jnp.float32
    tm, row, col = lax.axis_index("tm"), lax.axis_index("rows"), lax.axis_index("cols")
    vert = (row > 0, row < rn - 1)
    side = (col > 0, col < zn - 1)
    step = (-1, 1)

    def partner(d):
        got, bit = tm, 1
        while bit <= d:
            if d & bit:
                got = got + bit - 2 * bit * lax.rem(got // bit, 2)
            bit *= 2
        return got

    blocks = (x_ref, c_ref)

    def keep(which):
        return pltpu.make_async_copy(blocks[which], gat.at[which, 0], own_sem.at[which])

    keep(0).start()
    keep(1).start()
    barrier = pltpu.get_barrier_semaphore()

    def greet(place):
        pl.semaphore_signal(barrier, inc=1, device_id=place, device_id_type=MESH)

    for d in range(tmn - 1, 0, -1):
        greet((partner(d), row, col))
    for v in range(2):

        @pl.when(vert[v])
        def _():
            for d in range(tmn - 1, -1, -1):
                greet((partner(d), row + step[v], col))

    for h in range(2):

        @pl.when(side[h])
        def _():
            for d in range(tmn - 1, -1, -1):
                greet((partner(d), row, col + step[h]))

    for v in range(2):
        for h in range(2):

            @pl.when(jnp.logical_and(vert[v], side[h]))
            def _():
                for d in range(tmn - 1, -1, -1):
                    greet((partner(d), row + step[v], col + step[h]))

    for z in range(zn):

        @pl.when(jnp.logical_or(col - z > 1, z - col > 1))
        def _():
            greet((tm, row, z))

    for r in range(rn if rn > 2 else 0):

        @pl.when(jnp.logical_or(row - r > 1, r - row > 1))
        def _():
            greet((tm, r, col))

    def load_one(k):
        a, q = k // 9, k % 9
        return pltpu.make_async_copy(
            w1_ref.at[pl.ds(C * k, C), :], r1.at[pl.ds(C * q, C), pl.ds(C * a, C)], w_sem.at[0]
        )

    def load_two(k):
        a, q = k // 9, k % 9
        return pltpu.make_async_copy(
            w2_ref.at[pl.ds(C * k, C), :], r2.at[pl.ds(C * a, C), pl.ds(C * q, C)], w_sem.at[1]
        )

    for k in range(27):
        load_one(k).start()
    for k in range(27):
        load_two(k).start()

    for v in range(2):

        @pl.when(jnp.logical_not(vert[v]))
        def _():
            rim_in[:, v] = jnp.zeros((2, tmn, cols, C), bf)
            tip_in[:, v] = jnp.zeros((2, 2, tmn, 2, C), bf)

    for h in range(2):

        @pl.when(jnp.logical_not(side[h]))
        def _():
            edge_in[:, h] = jnp.zeros((2, tmn, rows, C), bf)
            tip_in[:, :, h] = jnp.zeros((2, 2, tmn, 2, C), bf)

    for which in range(2):
        keep(which).wait()
        flat[which] = gat[which, 0].astype(f32)
        for h in range(2):
            edge[which, h] = flat[which, pl.ds(h * (cols - 1), rows, stride=cols), :].astype(bf)
        for v in range(2):
            line = flat[which, v * (cells - cols) : v * (cells - cols) + cols, :]
            rim[which, v] = line.astype(bf)
            for h in range(2):
                tip[which, v, h] = jnp.broadcast_to(line[h * (cols - 1) : h * (cols - 1) + 1], (2, C)).astype(bf)

    def remote(src, dst, send, recv, place):
        return pltpu.make_async_remote_copy(
            src_ref=src, dst_ref=dst, send_sem=send, recv_sem=recv, device_id=place, device_id_type=MESH
        )

    def near(out_rim, out_edge, in_rim, in_edge, in_corner, sems):
        found = []
        for v in range(2):
            found.append((
                vert[v],
                lambda v=v: remote(
                    out_rim.at[v], in_rim.at[1 - v], sems.at[0, v], sems.at[1, 1 - v], (tm, row + step[v], col)
                ),
                in_rim.at[v],
                sems.at[1, v],
            ))
        for h in range(2):
            found.append((
                side[h],
                lambda h=h: remote(
                    out_edge.at[h], in_edge.at[1 - h], sems.at[0, 2 + h], sems.at[1, 3 - h], (tm, row, col + step[h])
                ),
                in_edge.at[h],
                sems.at[1, 2 + h],
            ))
        for v in range(2):
            for h in range(2):
                found.append((
                    jnp.logical_and(vert[v], side[h]),
                    lambda v=v, h=h: remote(
                        out_edge.at[h],
                        in_corner.at[1 - v, 1 - h],
                        sems.at[0, 4 + 2 * v + h],
                        sems.at[1, 4 + 2 * (1 - v) + 1 - h],
                        (tm, row + step[v], col + step[h]),
                    ),
                    in_corner.at[v, h],
                    sems.at[1, 4 + 2 * v + h],
                ))
        return found

    def start_all(found):
        for cond, copy, _, _ in found:

            @pl.when(cond)
            def _():
                copy().start()

    def drain_all(found):
        for cond, copy, _, _ in found:

            @pl.when(cond)
            def _():
                copy().wait_send()

    def arrived(dst, sem):
        remote(dst, dst, sem, sem, (tm, row, col)).wait_recv()

    def await_all(found):
        for cond, _, dst, sem in found:

            @pl.when(cond)
            def _():
                arrived(dst, sem)

    def assemble(dst, count, in_rim, in_edge, in_corner):
        for v in range(2):

            @pl.when(vert[v])
            def _():
                got = in_rim[v].astype(f32)
                for q in range(count):
                    dst[q, v * cols : (v + 1) * cols, :] = got[q * cols : (q + 1) * cols]

        for h, base in enumerate((left, right)):

            @pl.when(side[h])
            def _():
                got = in_edge[h].astype(f32)
                for q in range(count):
                    dst[q, base + 1 : base + 1 + rows, :] = got[q * rows : (q + 1) * rows]

            for v in range(2):

                @pl.when(jnp.logical_and(vert[v], side[h]))
                def _():
                    got = in_corner[v, h].astype(f32)
                    put = base + v * (rows + 1)
                    for q in range(count):
                        take = q * rows + (1 - v) * (rows - 1)
                        dst[q, put : put + 1, :] = got[take : take + 1]

    def spread(dst, v, top, bottom, sides, tips):
        dst[1, :cols, :] = top
        dst[1, cols : cols + cells, :] = v
        dst[1, cols + cells : lift, :] = bottom
        dst[0, 1 : cols + 1, :] = top
        dst[0, cols + 1 : cols + cells + 1, :] = v
        dst[0, cols + cells + 1 : lift, :] = bottom[: cols - 1]
        dst[0, :1, :] = tips[0][0]
        dst[0, pl.ds(cols, rows, stride=cols), :] = sides[0]
        dst[0, cols + cells : cols + cells + 1, :] = tips[1][0]
        dst[2, : cols - 1, :] = top[1:]
        dst[2, cols - 1 : cols + cells - 1, :] = v
        dst[2, cols + cells - 1 : lift - 1, :] = bottom
        dst[2, cols - 1 : cols, :] = tips[0][1]
        dst[2, pl.ds(2 * cols - 1, rows, stride=cols), :] = sides[1]
        dst[2, lift - 1 : lift, :] = tips[1][1]

    nv = vert[0].astype(jnp.int32) + vert[1].astype(jnp.int32)
    nh = side[0].astype(jnp.int32) + side[1].astype(jnp.int32)
    pl.semaphore_wait(barrier, tmn * (1 + nv) * (1 + nh) - 1 + zn - 1 - nh + rn - 1 - nv)

    groups = [list(range(d, min(d + 2, tmn))) for d in range(0, tmn, 2)]

    def send_block(which, d):
        return remote(
            gat.at[which, 0],
            gat.at[which, d],
            blk_send.at[which],
            blk_recv.at[which, d // 2],
            (partner(d), row, col),
        )

    def send_rim(which, v, d):
        return remote(
            rim.at[which, v],
            rim_in.at[which, 1 - v, d],
            near_send.at[v],
            near_recv.at[which, 1 - v],
            (partner(d), row + step[v], col),
        )

    def send_edge(which, h, d):
        return remote(
            edge.at[which, h],
            edge_in.at[which, 1 - h, d],
            near_send.at[2 + h],
            near_recv.at[which, 3 - h],
            (partner(d), row, col + step[h]),
        )

    def send_tip(which, v, h, d):
        return remote(
            tip.at[which, v, h],
            tip_in.at[which, 1 - v, 1 - h, d],
            near_send.at[4 + 2 * v + h],
            near_recv.at[which, 4 + 2 * (1 - v) + 1 - h],
            (partner(d), row + step[v], col + step[h]),
        )

    def send_near(which, ds):
        for h in range(2):

            @pl.when(side[h])
            def _():
                for d in ds:
                    send_edge(which, h, d).start()

        for v in range(2):

            @pl.when(vert[v])
            def _():
                for d in ds:
                    send_rim(which, v, d).start()

        for v in range(2):
            for h in range(2):

                @pl.when(jnp.logical_and(vert[v], side[h]))
                def _():
                    for d in ds:
                        send_tip(which, v, h, d).start()

    for which in range(2):
        send_near(which, range(tmn - 1, -1, -1))
        for ds in groups:
            for d in ds[::-1]:
                if d:
                    send_block(which, d).start()

    def sent(like, sem):
        remote(like, like, sem, sem, (tm, row, col)).wait_send()

    def receive(which, ds, dst):
        g = ds[0] // 2
        if ds[-1]:
            arrived(gat.at[which, max(ds[0], 1) : ds[-1] + 1], blk_recv.at[which, g])
        for h in range(2 if g == 0 else 0):

            @pl.when(side[h])
            def _():
                arrived(edge_in.at[which, h], near_recv.at[which, 2 + h])

        for v in range(2 if g == 0 else 0):

            @pl.when(vert[v])
            def _():
                arrived(rim_in.at[which, v], near_recv.at[which, v])

        for v in range(2 if g == 0 else 0):
            for h in range(2):

                @pl.when(jnp.logical_and(vert[v], side[h]))
                def _():
                    arrived(tip_in.at[which, v, h], near_recv.at[which, 4 + 2 * v + h])

        for d in ds:
            spread(
                dst.at[d],
                gat[which, d].astype(f32),
                rim_in[which, 0, d].astype(f32),
                rim_in[which, 1, d].astype(f32),
                [edge_in[which, h, d].astype(f32) for h in range(2)],
                [[tip_in[which, v, h, d].astype(f32)[:1] for h in range(2)] for v in range(2)],
            )

    for tail in (sx, sc):
        for s in range(tmn):
            for e in range(3):
                tail[s, e, lift:, :] = jnp.zeros((tail.shape[2] - lift, C), f32)
    for s in range(tmn):
        c9[s, mp:, :] = jnp.zeros((kp - mp, 9 * C), bf)
        xt[s] = jnp.zeros(xt.shape[1:], bf)
    at[...] = jnp.zeros(at.shape, bf)
    for s in range(tmn + 2):
        ghb[s] = jnp.zeros((kp, C), bf)
    ghf[tmn * cells :, :] = jnp.zeros((2 * cells, C), f32)
    gf[...] = jnp.zeros(gf.shape, f32)
    for j in range(3):
        for e in range(3):
            sh[j, e, lift:, :] = jnp.zeros((sh.shape[2] - lift, C), f32)
    pp[taps:, :] = jnp.zeros((pp.shape[0] - taps, C), f32)
    picked = jnp.concatenate(
        [
            jnp.where(
                (lax.broadcasted_iota(jnp.int32, (chunk_pad, C), 1)
                 == (tm * rn + r) * chunk + lax.broadcasted_iota(jnp.int32, (chunk_pad, C), 0))
                & (lax.broadcasted_iota(jnp.int32, (chunk_pad, C), 0) < chunk),
                1.0, 0.0,
            )
            for r in range(rn)
        ],
        axis=0,
    ).astype(bf)

    def tall(src):
        return lax.dot_general(picked, src, NT, preferred_element_type=f32).astype(bf)

    def choose_x(ds):
        for d in ds:
            for e in range(3):
                got = lax.dot_general(picked, sx[d, e].astype(bf), NT, preferred_element_type=f32)
                for b in range(3):
                    q = 3 * b + e
                    xt[d, cwp * q : cwp * (q + 1), :mp] = got[:, cols * b : cols * b + mp].astype(bf)

    for ds in groups:
        receive(0, ds, sx)
        for d in ds:
            for q in range(9):
                b, e = q // 3, q % 3
                x9[d, :, C * q : C * (q + 1)] = sx[d, e, cols * b : cols * b + mp, :].astype(bf)
        if ds[0] == 0:
            pltpu.make_async_copy(r1, r1, w_sem.at[0]).wait()
        got = jnp.dot(
            x9[ds[0] : ds[-1] + 1].reshape(len(ds) * mp, 9 * C), r1[...], preferred_element_type=f32
        )
        for d in ds:
            conv[partner(d)] = got[(d - ds[0]) * mp : (d - ds[0] + 1) * mp]
        if ds is not groups[-1]:
            choose_x(ds)
    for t in range(tmn):
        hidden = conv[t, :cells, 2 * C :]
        for a in range(2):
            s = t - 2 + a
            if s >= 0:
                hidden = hidden + conv[s, :cells, C * a : C * (a + 1)]
        squash = jax.nn.sigmoid(hidden)
        gate[t] = squash * (1.0 + hidden * (1.0 - squash))
        at[(t + 2) * cwp : (t + 3) * cwp, :cells] = tall((hidden * squash).astype(bf))

    def send_pairs(tensor):
        for d in range(1, rn):
            r = lax.rem(row + d, rn)
            remote(
                pstage.at[tensor, r],
                pland.at[tensor, row],
                pair_send.at[tensor],
                pair_recv.at[tensor],
                (tm, r, col),
            ).start()

    group = slots * chunk_pad // zn

    def scatter(tensor):
        if rn > 1:
            arrived(pland.at[tensor, : rn - 1], pair_recv.at[tensor])
        got = part[tensor, row]
        for d in range(1, rn):
            got = got + pland[tensor, lax.rem(row + d, rn)].astype(f32)
        pp[:taps, :] = got
        for z in range(zn):
            stage[tensor, z] = jnp.concatenate(
                [pp[group * q : group * (q + 1), ochunk * z : ochunk * (z + 1)] for q in range(zn)],
                axis=1,
            ).astype(bf)
        for d in range(1, zn):
            z = lax.rem(col + d, zn)
            remote(
                stage.at[tensor, z],
                landed.at[tensor, col],
                rs_send.at[tensor],
                rs_recv.at[tensor],
                (tm, row, z),
            ).start()

    total = None
    for ds in groups:
        receive(1, ds, sc)
        for d in ds:
            for q in range(9):
                b, e = q // 3, q % 3
                c9[d, :mp, C * q : C * (q + 1)] = sc[d, 2 - e, cols * (2 - b) : cols * (2 - b) + mp, :].astype(bf)
        for d in ds:
            lines = pl.ds(pl.multiple_of(partner(d) * cwp, 16), 3 * cwp)
            got = jnp.dot(at[lines, :mp], c9[d, :mp], preferred_element_type=f32)
            total = got if total is None else total + got
    for a in range(3):
        for r in range(rn):
            for q in range(9):
                k = 9 * a + q
                piece = total[a * cwp + r * chunk_pad : a * cwp + (r + 1) * chunk_pad, C * q : C * (q + 1)]
                part[1, r, k * chunk_pad : (k + 1) * chunk_pad, :] = piece
                pstage[1, r, k * chunk_pad : (k + 1) * chunk_pad, :] = piece.astype(bf)
    send_pairs(1)

    pltpu.make_async_copy(r2, r2, w_sem.at[1]).wait()
    got = lax.dot_general(
        c9[:, :mp, :].reshape(tmn * mp, 9 * C), r2[...], NT, preferred_element_type=f32
    )
    for d in range(tmn):
        conv[partner(d)] = got[d * mp : (d + 1) * mp]
    for t in range(tmn):
        grad = conv[t, :cells, 2 * C :]
        for a in range(2):
            s = t + 2 - a
            if s < tmn:
                grad = grad + conv[s, :cells, C * a : C * (a + 1)]
        grad = (grad * gate[t]).astype(bf)
        ghb[t, :cells, :] = grad
        ghf[t * cells : (t + 1) * cells, :] = grad.astype(f32)

    own3[...] = ghf[pl.ds(pl.multiple_of(tm * cells, 8), 3 * cells), :]
    for h in range(2):
        gedge[h] = own3[pl.ds(h * (cols - 1), 3 * rows, stride=cols), :].astype(bf)
    for v in range(2):
        grim[v] = jnp.concatenate(
            [
                own3[j * cells + v * (cells - cols) : j * cells + v * (cells - cols) + cols, :]
                for j in range(3)
            ],
            axis=0,
        ).astype(bf)
    grims = near(grim, gedge, grim_in, gedge_in, gcorner_in, gnear_sem)
    start_all(grims)

    scatter(1)

    choose_x(groups[-1])

    total = None
    for d in range(tmn):
        s = partner(d)
        right_side = jnp.concatenate([ghb[s + 2 - a, :mp] for a in range(3)], axis=1)
        got = jnp.dot(xt[d, :, :mp], right_side, preferred_element_type=f32)
        total = got if total is None else total + got
    for q in range(9):
        for r in range(rn):
            for a in range(3):
                k = 9 * a + q
                piece = total[q * cwp + r * chunk_pad : q * cwp + (r + 1) * chunk_pad, C * a : C * (a + 1)]
                part[0, r, k * chunk_pad : (k + 1) * chunk_pad, :] = piece
                pstage[0, r, k * chunk_pad : (k + 1) * chunk_pad, :] = piece.astype(bf)
    send_pairs(0)

    scatter(0)

    await_all(grims)
    assemble(gf, 3, grim_in, gedge_in, gcorner_in)
    for j in range(3):
        spread(
            sh.at[j],
            own3[j * cells : (j + 1) * cells, :],
            gf[j, :cols, :],
            gf[j, cols : 2 * cols, :],
            [gf[j, base + 1 : base + 1 + rows, :] for base in (left, right)],
            [[gf[j, base + put : base + put + 1, :] for base in (left, right)] for put in (0, rows + 1)],
        )
        for q in range(9):
            b, e = q // 3, q % 3
            lane = C * (3 * q + 2 - j)
            imc[:, lane : lane + C] = sh[j, 2 - e, cols * (2 - b) : cols * (2 - b) + mp, :].astype(bf)

    total = None
    for q in range(9):
        got = lax.dot_general(
            imc[:, 3 * C * q : 3 * C * (q + 1)], r1[C * q : C * (q + 1), :], NT, preferred_element_type=f32
        )
        total = got if total is None else total + got
    back_ref[...] = flat[1] + total[:cells]

    for tensor, out in ((1, two_ref), (0, one_ref)):
        landed[tensor, col] = stage[tensor, col]
        if zn > 1:
            arrived(landed.at[tensor, : zn - 1], rs_recv.at[tensor])
        got = landed[tensor, 0].astype(f32)
        for z in range(1, zn):
            got = got + landed[tensor, z].astype(f32)
        whole = jnp.concatenate(
            [got[:, ochunk * q : ochunk * (q + 1)] for q in range(zn)], axis=0
        ).reshape(slots, chunk_pad, ochunk)
        out[...] = whole[:27, :chunk, :]

    for which in range(2):
        if tmn > 1:
            sent(gat.at[which, 1:], blk_send.at[which])
        if rn > 1:
            sent(pstage.at[which, : rn - 1], pair_send.at[which])
        if zn > 1:
            sent(stage.at[which, : zn - 1], rs_send.at[which])
    for h in range(2):

        @pl.when(side[h])
        def _():
            sent(edge_in.at[:, h], near_send.at[2 + h])

    for v in range(2):

        @pl.when(vert[v])
        def _():
            sent(rim_in.at[:, v], near_send.at[v])

    for v in range(2):
        for h in range(2):

            @pl.when(jnp.logical_and(vert[v], side[h]))
            def _():
                sent(tip_in.at[:, v, h], near_send.at[4 + 2 * v + h])

    drain_all(grims)


def finish(back_ref, one_ref, two_ref, back_out, one_out, two_out, sem):
    pairs = ((back_ref, back_out), (one_ref, one_out), (two_ref, two_out))
    copies = [pltpu.make_async_copy(src, dst, sem.at[i]) for i, (src, dst) in enumerate(pairs)]
    for copy in copies:
        copy.start()
    for copy in copies:
        copy.wait()


def body(sizes, inputs, cotangent, weight_one, weight_two):
    tmn, rn, zn = sizes
    _, rows, cols, channels = inputs.shape
    cells = rows * cols
    chunk = channels // (tmn * rn)
    chunk_pad = max(16, chunk)
    slots = 28
    lift = (rows + 2) * cols
    mp = -(-cells // 16) * 16
    kp = -(-cells // 128) * 128
    hs = -(-(2 * cols + 2 * (-(-(rows + 2) // 8) * 8)) // 16) * 16
    cwp = rn * chunk_pad
    taps = 27 * chunk_pad
    dims = (tmn, rn, zn, rows, cols, chunk, chunk_pad, slots)
    vmem = pl.BlockSpec(memory_space=pltpu.VMEM)
    bf, f32 = jnp.bfloat16, jnp.float32
    group = slots * chunk_pad // zn
    dma = pltpu.SemaphoreType.DMA
    lifted = lift + mp - cells
    sums = (27, chunk, channels // zn)
    outs = pl.pallas_call(
        functools.partial(kernel, dims),
        out_shape=(
            pltpu.VMEM((cells, channels), f32),
            pltpu.VMEM(sums, f32),
            pltpu.VMEM(sums, f32),
        ),
        in_specs=[pl.BlockSpec(memory_space=pl.ANY)] * 4,
        out_specs=(vmem,) * 3,
        scratch_shapes=[
            pltpu.VMEM((2, tmn, cells, channels), bf),
            pltpu.VMEM((2, cells, channels), f32),
            pltpu.VMEM((tmn, 3, lifted, channels), f32),
            pltpu.VMEM((tmn, 3, lifted, channels), f32),
            pltpu.VMEM((tmn, mp, 9 * channels), bf),
            pltpu.VMEM((tmn, kp, 9 * channels), bf),
            pltpu.VMEM((9 * channels, 3 * channels), bf),
            pltpu.VMEM((3 * channels, 9 * channels), bf),
            pltpu.VMEM((tmn, mp, 3 * channels), f32),
            pltpu.VMEM((tmn, cells, channels), f32),
            pltpu.VMEM(((tmn + 2) * cwp, kp), bf),
            pltpu.VMEM((tmn, 9 * cwp, kp), bf),
            pltpu.VMEM((tmn + 2, kp, channels), bf),
            pltpu.VMEM(((tmn + 2) * cells, channels), f32),
            pltpu.VMEM((3 * cells, channels), f32),
            pltpu.VMEM((3, hs, channels), f32),
            pltpu.VMEM((3, 3, lifted, channels), f32),
            pltpu.VMEM((mp, 27 * channels), bf),
            pltpu.VMEM((2, rn, taps, channels), f32),
            pltpu.VMEM((2, rn, taps, channels), bf),
            pltpu.VMEM((2, rn, taps, channels), bf),
            pltpu.VMEM((slots * chunk_pad, channels), f32),
            pltpu.VMEM((2, zn, group, channels), bf),
            pltpu.VMEM((2, zn, group, channels), bf),
            pltpu.VMEM((2, 2, cols, channels), bf),
            pltpu.VMEM((2, 2, rows, channels), bf),
            pltpu.VMEM((2, 2, 2, 2, channels), bf),
            pltpu.VMEM((2, 2, tmn, cols, channels), bf),
            pltpu.VMEM((2, 2, tmn, rows, channels), bf),
            pltpu.VMEM((2, 2, 2, tmn, 2, channels), bf),
            pltpu.VMEM((2, 3 * cols, channels), bf),
            pltpu.VMEM((2, 3 * rows, channels), bf),
            pltpu.VMEM((2, 3 * cols, channels), bf),
            pltpu.VMEM((2, 3 * rows, channels), bf),
            pltpu.VMEM((2, 2, 3 * rows, channels), bf),
            dma((2,)),
            dma((2,)),
            dma((2,)),
            dma((2, -(-tmn // 2))),
            dma((8,)),
            dma((2, 8)),
            dma((2, 8)),
            dma((2,)),
            dma((2,)),
            dma((2,)),
            dma((2,)),
        ],
        compiler_params=pltpu.CompilerParams(
            collective_id=0, has_side_effects=True, vmem_limit_bytes=60 * 1024 * 1024
        ),
    )(
        inputs.reshape(cells, channels),
        cotangent.reshape(cells, channels),
        weight_one.reshape(27 * channels, channels),
        weight_two.reshape(27 * channels, channels),
    )
    back, one, two = pl.pallas_call(
        finish,
        out_shape=(
            jax.ShapeDtypeStruct((cells, channels), f32),
            jax.ShapeDtypeStruct(sums, f32),
            jax.ShapeDtypeStruct(sums, f32),
        ),
        in_specs=[vmem] * 3,
        out_specs=(pl.BlockSpec(memory_space=pl.ANY),) * 3,
        scratch_shapes=[dma((3,))],
    )(*[pltpu.with_memory_space_constraint(out, pltpu.VMEM) for out in outs])
    return back.reshape(1, rows, cols, channels), one, two


def solution(mesh):
    sizes = (mesh.shape["tm"], mesh.shape["rows"], mesh.shape["cols"])
    placed = (P("tm", "rows", "cols", None), P("tm", "rows", "cols", None), P(), P())
    return jax.shard_map(
        functools.partial(body, sizes),
        mesh=mesh,
        in_specs=placed,
        out_specs=(
            P("tm", "rows", "cols", None),
            P(None, ("tm", "rows"), "cols"),
            P(None, ("tm", "rows"), "cols"),
        ),
        check_vma=False,
    )
```

```python
import functools

import jax
import jax.numpy as jnp
from jax import lax
from jax.experimental import pallas as pl
from jax.experimental.pallas import tpu as pltpu
from jax.sharding import PartitionSpec as P

MESH = pl.DeviceIdType.MESH
NT = (((1,), (1,)), ((), ()))
C = 128


def kernel(
    dims,
    x_ref,
    c_ref,
    w1_ref,
    w2_ref,
    back_ref,
    one_ref,
    two_ref,
    gat,
    flat,
    sx,
    sc,
    x9,
    c9,
    r1,
    r2,
    conv,
    gate,
    at,
    xt,
    ghb,
    ghf,
    own3,
    gf,
    sh,
    imc,
    part,
    pstage,
    pland,
    pp,
    stage,
    landed,
    rim,
    edge,
    tip,
    rim_in,
    edge_in,
    tip_in,
    grim,
    gedge,
    grim_in,
    gedge_in,
    gcorner_in,
    own_sem,
    w_sem,
    blk_send,
    blk_recv,
    near_send,
    near_recv,
    gnear_sem,
    pair_send,
    pair_recv,
    rs_send,
    rs_recv,
):
    tmn, rn, zn, rows, cols, chunk, chunk_pad, slots = dims
    cells = rows * cols
    lift = (rows + 2) * cols
    left = 2 * cols
    right = left + -(-(rows + 2) // 8) * 8
    mp, kp = x9.shape[1], c9.shape[1]
    taps = 27 * chunk_pad
    cwp = rn * chunk_pad
    ochunk = C // zn
    bf, f32 = jnp.bfloat16, jnp.float32
    tm, row, col = lax.axis_index("tm"), lax.axis_index("rows"), lax.axis_index("cols")
    vert = (row > 0, row < rn - 1)
    side = (col > 0, col < zn - 1)
    step = (-1, 1)

    def partner(d):
        got, bit = tm, 1
        while bit <= d:
            if d & bit:
                got = got + bit - 2 * bit * lax.rem(got // bit, 2)
            bit *= 2
        return got

    blocks = (x_ref, c_ref)

    def keep(which):
        return pltpu.make_async_copy(blocks[which], gat.at[which, 0], own_sem.at[which])

    keep(0).start()
    keep(1).start()
    barrier = pltpu.get_barrier_semaphore()

    def greet(place):
        pl.semaphore_signal(barrier, inc=1, device_id=place, device_id_type=MESH)

    for d in range(tmn - 1, 0, -1):
        greet((partner(d), row, col))
    for v in range(2):

        @pl.when(vert[v])
        def _():
            for d in range(tmn - 1, -1, -1):
                greet((partner(d), row + step[v], col))

    for h in range(2):

        @pl.when(side[h])
        def _():
            for d in range(tmn - 1, -1, -1):
                greet((partner(d), row, col + step[h]))

    for v in range(2):
        for h in range(2):

            @pl.when(jnp.logical_and(vert[v], side[h]))
            def _():
                for d in range(tmn - 1, -1, -1):
                    greet((partner(d), row + step[v], col + step[h]))

    for z in range(zn):

        @pl.when(jnp.logical_or(col - z > 1, z - col > 1))
        def _():
            greet((tm, row, z))

    for r in range(rn if rn > 2 else 0):

        @pl.when(jnp.logical_or(row - r > 1, r - row > 1))
        def _():
            greet((tm, r, col))

    def load_one(k):
        a, q = k // 9, k % 9
        return pltpu.make_async_copy(
            w1_ref.at[pl.ds(C * k, C), :], r1.at[pl.ds(C * q, C), pl.ds(C * a, C)], w_sem.at[0]
        )

    def load_two(k):
        a, q = k // 9, k % 9
        return pltpu.make_async_copy(
            w2_ref.at[pl.ds(C * k, C), :], r2.at[pl.ds(C * a, C), pl.ds(C * q, C)], w_sem.at[1]
        )

    for k in range(27):
        load_one(k).start()
    for k in range(27):
        load_two(k).start()

    for v in range(2):

        @pl.when(jnp.logical_not(vert[v]))
        def _():
            rim_in[:, v] = jnp.zeros((2, tmn, cols, C), bf)
            tip_in[:, v] = jnp.zeros((2, 2, tmn, 2, C), bf)

    for h in range(2):

        @pl.when(jnp.logical_not(side[h]))
        def _():
            edge_in[:, h] = jnp.zeros((2, tmn, rows, C), bf)
            tip_in[:, :, h] = jnp.zeros((2, 2, tmn, 2, C), bf)

    for which in range(2):
        keep(which).wait()
        flat[which] = gat[which, 0].astype(f32)
        for h in range(2):
            edge[which, h] = flat[which, pl.ds(h * (cols - 1), rows, stride=cols), :].astype(bf)
        for v in range(2):
            line = flat[which, v * (cells - cols) : v * (cells - cols) + cols, :]
            rim[which, v] = line.astype(bf)
            for h in range(2):
                tip[which, v, h] = jnp.broadcast_to(line[h * (cols - 1) : h * (cols - 1) + 1], (2, C)).astype(bf)

    def remote(src, dst, send, recv, place):
        return pltpu.make_async_remote_copy(
            src_ref=src, dst_ref=dst, send_sem=send, recv_sem=recv, device_id=place, device_id_type=MESH
        )

    def near(out_rim, out_edge, in_rim, in_edge, in_corner, sems):
        found = []
        for v in range(2):
            found.append((
                vert[v],
                lambda v=v: remote(
                    out_rim.at[v], in_rim.at[1 - v], sems.at[0, v], sems.at[1, 1 - v], (tm, row + step[v], col)
                ),
                in_rim.at[v],
                sems.at[1, v],
            ))
        for h in range(2):
            found.append((
                side[h],
                lambda h=h: remote(
                    out_edge.at[h], in_edge.at[1 - h], sems.at[0, 2 + h], sems.at[1, 3 - h], (tm, row, col + step[h])
                ),
                in_edge.at[h],
                sems.at[1, 2 + h],
            ))
        for v in range(2):
            for h in range(2):
                found.append((
                    jnp.logical_and(vert[v], side[h]),
                    lambda v=v, h=h: remote(
                        out_edge.at[h],
                        in_corner.at[1 - v, 1 - h],
                        sems.at[0, 4 + 2 * v + h],
                        sems.at[1, 4 + 2 * (1 - v) + 1 - h],
                        (tm, row + step[v], col + step[h]),
                    ),
                    in_corner.at[v, h],
                    sems.at[1, 4 + 2 * v + h],
                ))
        return found

    def start_all(found):
        for cond, copy, _, _ in found:

            @pl.when(cond)
            def _():
                copy().start()

    def drain_all(found):
        for cond, copy, _, _ in found:

            @pl.when(cond)
            def _():
                copy().wait_send()

    def arrived(dst, sem):
        remote(dst, dst, sem, sem, (tm, row, col)).wait_recv()

    def await_all(found):
        for cond, _, dst, sem in found:

            @pl.when(cond)
            def _():
                arrived(dst, sem)

    def assemble(dst, count, in_rim, in_edge, in_corner):
        for v in range(2):

            @pl.when(vert[v])
            def _():
                got = in_rim[v].astype(f32)
                for q in range(count):
                    dst[q, v * cols : (v + 1) * cols, :] = got[q * cols : (q + 1) * cols]

        for h, base in enumerate((left, right)):

            @pl.when(side[h])
            def _():
                got = in_edge[h].astype(f32)
                for q in range(count):
                    dst[q, base + 1 : base + 1 + rows, :] = got[q * rows : (q + 1) * rows]

            for v in range(2):

                @pl.when(jnp.logical_and(vert[v], side[h]))
                def _():
                    got = in_corner[v, h].astype(f32)
                    put = base + v * (rows + 1)
                    for q in range(count):
                        take = q * rows + (1 - v) * (rows - 1)
                        dst[q, put : put + 1, :] = got[take : take + 1]

    def spread(dst, v, top, bottom, sides, tips):
        dst[1, :cols, :] = top
        dst[1, cols : cols + cells, :] = v
        dst[1, cols + cells : lift, :] = bottom
        dst[0, 1 : cols + 1, :] = top
        dst[0, cols + 1 : cols + cells + 1, :] = v
        dst[0, cols + cells + 1 : lift, :] = bottom[: cols - 1]
        dst[0, :1, :] = tips[0][0]
        dst[0, pl.ds(cols, rows, stride=cols), :] = sides[0]
        dst[0, cols + cells : cols + cells + 1, :] = tips[1][0]
        dst[2, : cols - 1, :] = top[1:]
        dst[2, cols - 1 : cols + cells - 1, :] = v
        dst[2, cols + cells - 1 : lift - 1, :] = bottom
        dst[2, cols - 1 : cols, :] = tips[0][1]
        dst[2, pl.ds(2 * cols - 1, rows, stride=cols), :] = sides[1]
        dst[2, lift - 1 : lift, :] = tips[1][1]

    nv = vert[0].astype(jnp.int32) + vert[1].astype(jnp.int32)
    nh = side[0].astype(jnp.int32) + side[1].astype(jnp.int32)
    pl.semaphore_wait(barrier, tmn * (1 + nv) * (1 + nh) - 1 + zn - 1 - nh + rn - 1 - nv)

    groups = [list(range(d, min(d + 2, tmn))) for d in range(0, tmn, 2)]

    def send_block(which, d):
        return remote(
            gat.at[which, 0],
            gat.at[which, d],
            blk_send.at[which],
            blk_recv.at[which, d // 2],
            (partner(d), row, col),
        )

    def send_rim(which, v, d):
        return remote(
            rim.at[which, v],
            rim_in.at[which, 1 - v, d],
            near_send.at[v],
            near_recv.at[which, 1 - v],
            (partner(d), row + step[v], col),
        )

    def send_edge(which, h, d):
        return remote(
            edge.at[which, h],
            edge_in.at[which, 1 - h, d],
            near_send.at[2 + h],
            near_recv.at[which, 3 - h],
            (partner(d), row, col + step[h]),
        )

    def send_tip(which, v, h, d):
        return remote(
            tip.at[which, v, h],
            tip_in.at[which, 1 - v, 1 - h, d],
            near_send.at[4 + 2 * v + h],
            near_recv.at[which, 4 + 2 * (1 - v) + 1 - h],
            (partner(d), row + step[v], col + step[h]),
        )

    def send_near(which, ds):
        for h in range(2):

            @pl.when(side[h])
            def _():
                for d in ds:
                    send_edge(which, h, d).start()

        for v in range(2):

            @pl.when(vert[v])
            def _():
                for d in ds:
                    send_rim(which, v, d).start()

        for v in range(2):
            for h in range(2):

                @pl.when(jnp.logical_and(vert[v], side[h]))
                def _():
                    for d in ds:
                        send_tip(which, v, h, d).start()

    for which in range(2):
        send_near(which, range(tmn - 1, -1, -1))
        for ds in groups:
            for d in ds[::-1]:
                if d:
                    send_block(which, d).start()

    def sent(like, sem):
        remote(like, like, sem, sem, (tm, row, col)).wait_send()

    def receive(which, ds, dst):
        g = ds[0] // 2
        if ds[-1]:
            arrived(gat.at[which, max(ds[0], 1) : ds[-1] + 1], blk_recv.at[which, g])
        for h in range(2 if g == 0 else 0):

            @pl.when(side[h])
            def _():
                arrived(edge_in.at[which, h], near_recv.at[which, 2 + h])

        for v in range(2 if g == 0 else 0):

            @pl.when(vert[v])
            def _():
                arrived(rim_in.at[which, v], near_recv.at[which, v])

        for v in range(2 if g == 0 else 0):
            for h in range(2):

                @pl.when(jnp.logical_and(vert[v], side[h]))
                def _():
                    arrived(tip_in.at[which, v, h], near_recv.at[which, 4 + 2 * v + h])

        for d in ds:
            spread(
                dst.at[d],
                gat[which, d].astype(f32),
                rim_in[which, 0, d].astype(f32),
                rim_in[which, 1, d].astype(f32),
                [edge_in[which, h, d].astype(f32) for h in range(2)],
                [[tip_in[which, v, h, d].astype(f32)[:1] for h in range(2)] for v in range(2)],
            )

    for tail in (sx, sc):
        for s in range(tmn):
            for e in range(3):
                tail[s, e, lift:, :] = jnp.zeros((tail.shape[2] - lift, C), f32)
    for s in range(tmn):
        c9[s, mp:, :] = jnp.zeros((kp - mp, 9 * C), bf)
        xt[s] = jnp.zeros(xt.shape[1:], bf)
    at[...] = jnp.zeros(at.shape, bf)
    for s in range(tmn + 2):
        ghb[s] = jnp.zeros((kp, C), bf)
    ghf[tmn * cells :, :] = jnp.zeros((2 * cells, C), f32)
    gf[...] = jnp.zeros(gf.shape, f32)
    for j in range(3):
        for e in range(3):
            sh[j, e, lift:, :] = jnp.zeros((sh.shape[2] - lift, C), f32)
    pp[taps:, :] = jnp.zeros((pp.shape[0] - taps, C), f32)
    picked = jnp.concatenate(
        [
            jnp.where(
                (lax.broadcasted_iota(jnp.int32, (chunk_pad, C), 1)
                 == (tm * rn + r) * chunk + lax.broadcasted_iota(jnp.int32, (chunk_pad, C), 0))
                & (lax.broadcasted_iota(jnp.int32, (chunk_pad, C), 0) < chunk),
                1.0, 0.0,
            )
            for r in range(rn)
        ],
        axis=0,
    ).astype(bf)

    def tall(src):
        return lax.dot_general(picked, src, NT, preferred_element_type=f32).astype(bf)

    def choose_x(ds):
        for d in ds:
            for e in range(3):
                got = lax.dot_general(picked, sx[d, e].astype(bf), NT, preferred_element_type=f32)
                for b in range(3):
                    q = 3 * b + e
                    xt[d, cwp * q : cwp * (q + 1), :mp] = got[:, cols * b : cols * b + mp].astype(bf)

    for ds in groups:
        receive(0, ds, sx)
        for d in ds:
            for q in range(9):
                b, e = q // 3, q % 3
                x9[d, :, C * q : C * (q + 1)] = sx[d, e, cols * b : cols * b + mp, :].astype(bf)
        if ds[0] == 0:
            pltpu.make_async_copy(r1, r1, w_sem.at[0]).wait()
        got = jnp.dot(
            x9[ds[0] : ds[-1] + 1].reshape(len(ds) * mp, 9 * C), r1[...], preferred_element_type=f32
        )
        for d in ds:
            conv[partner(d)] = got[(d - ds[0]) * mp : (d - ds[0] + 1) * mp]
    for t in range(tmn):
        hidden = conv[t, :cells, 2 * C :]
        for a in range(2):
            s = t - 2 + a
            if s >= 0:
                hidden = hidden + conv[s, :cells, C * a : C * (a + 1)]
        squash = jax.nn.sigmoid(hidden)
        gate[t] = squash * (1.0 + hidden * (1.0 - squash))
        at[(t + 2) * cwp : (t + 3) * cwp, :cells] = tall((hidden * squash).astype(bf))

    def send_pairs(tensor):
        for d in range(1, rn):
            r = lax.rem(row + d, rn)
            remote(
                pstage.at[tensor, r],
                pland.at[tensor, row],
                pair_send.at[tensor],
                pair_recv.at[tensor],
                (tm, r, col),
            ).start()

    group = slots * chunk_pad // zn

    def scatter(tensor):
        if rn > 1:
            arrived(pland.at[tensor, : rn - 1], pair_recv.at[tensor])
        got = part[tensor, row]
        for d in range(1, rn):
            got = got + pland[tensor, lax.rem(row + d, rn)].astype(f32)
        pp[:taps, :] = got
        for z in range(zn):
            stage[tensor, z] = jnp.concatenate(
                [pp[group * q : group * (q + 1), ochunk * z : ochunk * (z + 1)] for q in range(zn)],
                axis=1,
            ).astype(bf)
        for d in range(1, zn):
            z = lax.rem(col + d, zn)
            remote(
                stage.at[tensor, z],
                landed.at[tensor, col],
                rs_send.at[tensor],
                rs_recv.at[tensor],
                (tm, row, z),
            ).start()

    total = None
    for ds in groups:
        receive(1, ds, sc)
        for d in ds:
            for q in range(9):
                b, e = q // 3, q % 3
                c9[d, :mp, C * q : C * (q + 1)] = sc[d, 2 - e, cols * (2 - b) : cols * (2 - b) + mp, :].astype(bf)
        for d in ds:
            lines = pl.ds(pl.multiple_of(partner(d) * cwp, 16), 3 * cwp)
            got = jnp.dot(at[lines, :mp], c9[d, :mp], preferred_element_type=f32)
            total = got if total is None else total + got
    for a in range(3):
        for r in range(rn):
            for q in range(9):
                k = 9 * a + q
                piece = total[a * cwp + r * chunk_pad : a * cwp + (r + 1) * chunk_pad, C * q : C * (q + 1)]
                part[1, r, k * chunk_pad : (k + 1) * chunk_pad, :] = piece
                pstage[1, r, k * chunk_pad : (k + 1) * chunk_pad, :] = piece.astype(bf)
    send_pairs(1)

    pltpu.make_async_copy(r2, r2, w_sem.at[1]).wait()
    got = lax.dot_general(
        c9[:, :mp, :].reshape(tmn * mp, 9 * C), r2[...], NT, preferred_element_type=f32
    )
    for d in range(tmn):
        conv[partner(d)] = got[d * mp : (d + 1) * mp]
    for t in range(tmn):
        grad = conv[t, :cells, 2 * C :]
        for a in range(2):
            s = t + 2 - a
            if s < tmn:
                grad = grad + conv[s, :cells, C * a : C * (a + 1)]
        grad = (grad * gate[t]).astype(bf)
        ghb[t, :cells, :] = grad
        ghf[t * cells : (t + 1) * cells, :] = grad.astype(f32)

    own3[...] = ghf[pl.ds(pl.multiple_of(tm * cells, 8), 3 * cells), :]
    for h in range(2):
        gedge[h] = own3[pl.ds(h * (cols - 1), 3 * rows, stride=cols), :].astype(bf)
    for v in range(2):
        grim[v] = jnp.concatenate(
            [
                own3[j * cells + v * (cells - cols) : j * cells + v * (cells - cols) + cols, :]
                for j in range(3)
            ],
            axis=0,
        ).astype(bf)
    grims = near(grim, gedge, grim_in, gedge_in, gcorner_in, gnear_sem)
    start_all(grims)

    scatter(1)

    choose_x(range(tmn))

    total = None
    for d in range(tmn):
        s = partner(d)
        right_side = jnp.concatenate([ghb[s + 2 - a, :mp] for a in range(3)], axis=1)
        got = jnp.dot(xt[d, :, :mp], right_side, preferred_element_type=f32)
        total = got if total is None else total + got
    for q in range(9):
        for r in range(rn):
            for a in range(3):
                k = 9 * a + q
                piece = total[q * cwp + r * chunk_pad : q * cwp + (r + 1) * chunk_pad, C * a : C * (a + 1)]
                part[0, r, k * chunk_pad : (k + 1) * chunk_pad, :] = piece
                pstage[0, r, k * chunk_pad : (k + 1) * chunk_pad, :] = piece.astype(bf)
    send_pairs(0)

    scatter(0)

    await_all(grims)
    assemble(gf, 3, grim_in, gedge_in, gcorner_in)
    for j in range(3):
        spread(
            sh.at[j],
            own3[j * cells : (j + 1) * cells, :],
            gf[j, :cols, :],
            gf[j, cols : 2 * cols, :],
            [gf[j, base + 1 : base + 1 + rows, :] for base in (left, right)],
            [[gf[j, base + put : base + put + 1, :] for base in (left, right)] for put in (0, rows + 1)],
        )
        for q in range(9):
            b, e = q // 3, q % 3
            lane = C * (3 * q + 2 - j)
            imc[:, lane : lane + C] = sh[j, 2 - e, cols * (2 - b) : cols * (2 - b) + mp, :].astype(bf)

    total = None
    for q in range(9):
        got = lax.dot_general(
            imc[:, 3 * C * q : 3 * C * (q + 1)], r1[C * q : C * (q + 1), :], NT, preferred_element_type=f32
        )
        total = got if total is None else total + got
    back_ref[...] = flat[1] + total[:cells]

    for tensor, out in ((1, two_ref), (0, one_ref)):
        landed[tensor, col] = stage[tensor, col]
        if zn > 1:
            arrived(landed.at[tensor, : zn - 1], rs_recv.at[tensor])
        got = landed[tensor, 0].astype(f32)
        for z in range(1, zn):
            got = got + landed[tensor, z].astype(f32)
        whole = jnp.concatenate(
            [got[:, ochunk * q : ochunk * (q + 1)] for q in range(zn)], axis=0
        ).reshape(slots, chunk_pad, ochunk)
        out[...] = whole[:27, :chunk, :]

    for which in range(2):
        if tmn > 1:
            sent(gat.at[which, 1:], blk_send.at[which])
        if rn > 1:
            sent(pstage.at[which, : rn - 1], pair_send.at[which])
        if zn > 1:
            sent(stage.at[which, : zn - 1], rs_send.at[which])
    for h in range(2):

        @pl.when(side[h])
        def _():
            sent(edge_in.at[:, h], near_send.at[2 + h])

    for v in range(2):

        @pl.when(vert[v])
        def _():
            sent(rim_in.at[:, v], near_send.at[v])

    for v in range(2):
        for h in range(2):

            @pl.when(jnp.logical_and(vert[v], side[h]))
            def _():
                sent(tip_in.at[:, v, h], near_send.at[4 + 2 * v + h])

    drain_all(grims)


def finish(back_ref, one_ref, two_ref, back_out, one_out, two_out, sem):
    pairs = ((back_ref, back_out), (one_ref, one_out), (two_ref, two_out))
    copies = [pltpu.make_async_copy(src, dst, sem.at[i]) for i, (src, dst) in enumerate(pairs)]
    for copy in copies:
        copy.start()
    for copy in copies:
        copy.wait()


def body(sizes, inputs, cotangent, weight_one, weight_two):
    tmn, rn, zn = sizes
    _, rows, cols, channels = inputs.shape
    cells = rows * cols
    chunk = channels // (tmn * rn)
    chunk_pad = max(16, chunk)
    slots = 28
    lift = (rows + 2) * cols
    mp = -(-cells // 16) * 16
    kp = -(-cells // 128) * 128
    hs = -(-(2 * cols + 2 * (-(-(rows + 2) // 8) * 8)) // 16) * 16
    cwp = rn * chunk_pad
    taps = 27 * chunk_pad
    dims = (tmn, rn, zn, rows, cols, chunk, chunk_pad, slots)
    vmem = pl.BlockSpec(memory_space=pltpu.VMEM)
    bf, f32 = jnp.bfloat16, jnp.float32
    group = slots * chunk_pad // zn
    dma = pltpu.SemaphoreType.DMA
    lifted = lift + mp - cells
    sums = (27, chunk, channels // zn)
    outs = pl.pallas_call(
        functools.partial(kernel, dims),
        out_shape=(
            pltpu.VMEM((cells, channels), f32),
            pltpu.VMEM(sums, f32),
            pltpu.VMEM(sums, f32),
        ),
        in_specs=[pl.BlockSpec(memory_space=pl.ANY)] * 4,
        out_specs=(vmem,) * 3,
        scratch_shapes=[
            pltpu.VMEM((2, tmn, cells, channels), bf),
            pltpu.VMEM((2, cells, channels), f32),
            pltpu.VMEM((tmn, 3, lifted, channels), f32),
            pltpu.VMEM((tmn, 3, lifted, channels), f32),
            pltpu.VMEM((tmn, mp, 9 * channels), bf),
            pltpu.VMEM((tmn, kp, 9 * channels), bf),
            pltpu.VMEM((9 * channels, 3 * channels), bf),
            pltpu.VMEM((3 * channels, 9 * channels), bf),
            pltpu.VMEM((tmn, mp, 3 * channels), f32),
            pltpu.VMEM((tmn, cells, channels), f32),
            pltpu.VMEM(((tmn + 2) * cwp, kp), bf),
            pltpu.VMEM((tmn, 9 * cwp, kp), bf),
            pltpu.VMEM((tmn + 2, kp, channels), bf),
            pltpu.VMEM(((tmn + 2) * cells, channels), f32),
            pltpu.VMEM((3 * cells, channels), f32),
            pltpu.VMEM((3, hs, channels), f32),
            pltpu.VMEM((3, 3, lifted, channels), f32),
            pltpu.VMEM((mp, 27 * channels), bf),
            pltpu.VMEM((2, rn, taps, channels), f32),
            pltpu.VMEM((2, rn, taps, channels), bf),
            pltpu.VMEM((2, rn, taps, channels), bf),
            pltpu.VMEM((slots * chunk_pad, channels), f32),
            pltpu.VMEM((2, zn, group, channels), bf),
            pltpu.VMEM((2, zn, group, channels), bf),
            pltpu.VMEM((2, 2, cols, channels), bf),
            pltpu.VMEM((2, 2, rows, channels), bf),
            pltpu.VMEM((2, 2, 2, 2, channels), bf),
            pltpu.VMEM((2, 2, tmn, cols, channels), bf),
            pltpu.VMEM((2, 2, tmn, rows, channels), bf),
            pltpu.VMEM((2, 2, 2, tmn, 2, channels), bf),
            pltpu.VMEM((2, 3 * cols, channels), bf),
            pltpu.VMEM((2, 3 * rows, channels), bf),
            pltpu.VMEM((2, 3 * cols, channels), bf),
            pltpu.VMEM((2, 3 * rows, channels), bf),
            pltpu.VMEM((2, 2, 3 * rows, channels), bf),
            dma((2,)),
            dma((2,)),
            dma((2,)),
            dma((2, -(-tmn // 2))),
            dma((8,)),
            dma((2, 8)),
            dma((2, 8)),
            dma((2,)),
            dma((2,)),
            dma((2,)),
            dma((2,)),
        ],
        compiler_params=pltpu.CompilerParams(
            collective_id=0, has_side_effects=True, vmem_limit_bytes=60 * 1024 * 1024
        ),
    )(
        inputs.reshape(cells, channels),
        cotangent.reshape(cells, channels),
        weight_one.reshape(27 * channels, channels),
        weight_two.reshape(27 * channels, channels),
    )
    back, one, two = pl.pallas_call(
        finish,
        out_shape=(
            jax.ShapeDtypeStruct((cells, channels), f32),
            jax.ShapeDtypeStruct(sums, f32),
            jax.ShapeDtypeStruct(sums, f32),
        ),
        in_specs=[vmem] * 3,
        out_specs=(pl.BlockSpec(memory_space=pl.ANY),) * 3,
        scratch_shapes=[dma((3,))],
    )(*[pltpu.with_memory_space_constraint(out, pltpu.VMEM) for out in outs])
    return back.reshape(1, rows, cols, channels), one, two


def solution(mesh):
    sizes = (mesh.shape["tm"], mesh.shape["rows"], mesh.shape["cols"])
    placed = (P("tm", "rows", "cols", None), P("tm", "rows", "cols", None), P(), P())
    return jax.shard_map(
        functools.partial(body, sizes),
        mesh=mesh,
        in_specs=placed,
        out_specs=(
            P("tm", "rows", "cols", None),
            P(None, ("tm", "rows"), "cols"),
            P(None, ("tm", "rows"), "cols"),
        ),
        check_vma=False,
    )
```
